256 devices in a mesh: row: 4 (over y), col: 16 (over z, core), layer: 4 (over x).
Axes of the slice: x: 4, y: 4, z: 8, core: 2. Of those that a mesh axis runs over, the one named last changes fastest.
Arguments:
- blocks: bfloat16 [5632, 128, 128], P(('col', 'layer')), may hold values from -6 to 6
- block_aux: int32 [5632], P(('col', 'layer')), may hold values from 0 to 23
- block_row: int32 [5632], P(('col', 'layer')), may hold values from 0 to 15, as said below
- block_col: int32 [5632], P(('col', 'layer')), may hold values from 0 to 159, as said below
- extents: int32 [5632], P(('col', 'layer')), may hold values from 32 to 128
- occ_green: bfloat16 [20480, 2048], P('layer', 'row'), may hold values from -0.00390625 to 0.00390625
- virt_green: bfloat16 [20480, 2048], P('layer', 'row'), may hold values from -0.00390625 to 0.00390625
Outputs:
- chi: float32 [24, 24], replicated
The draws below stay inside these ranges and needn't reach their ends.
Inputs may be any that keep to these rules, and one draw needn't show every extreme that they name: block_row[n] numbers the block of 128 window functions that tile n covers. The owner of tile n is the pair (block_row[n], block_col[n] // 40). Within each device's share of 88 consecutive entries no owner appears more than 2 times, and one owner, the same for every share, appears exactly 2 times in every share.
All inputs are finite; a program needn't handle non-finite values.
Results may differ from the reference program's by a relative error of at most 0.0003.
Values may be sent and summed in bfloat16 or wider, within the bound.
No kernel may reach another device: no remote copies, remote signals or barrier semaphores. Data moves between devices by JAX's collectives and lax.ppermute only.
A program may use at most 192 MiB of HBM per device.

```python
import jax
import jax.numpy as jnp
from jax import lax

NP = 24
BS = 128
NB = 20480
BLK_DEV = 88
W = 2048
KQ = 40
DESTS = 64
CAP = 2
NBLK = 5632
N_LAYER = 4


def pick_owners(key):
    base_key = jax.random.fold_in(key, 11)
    star_key, order_key, column_key = jax.random.split(base_key, 3)
    busiest = jax.random.randint(star_key, (), 0, DESTS).astype(jnp.int32)
    pool_size = (DESTS - 1) * CAP

    def one_share(share_key):
        pick_key, shuffle_key = jax.random.split(share_key)
        picks = jax.random.permutation(pick_key, pool_size)[:BLK_DEV - CAP].astype(jnp.int32)
        others = picks // CAP
        others = others + (others >= busiest).astype(jnp.int32)
        owners = jnp.concatenate([jnp.full((CAP,), busiest, jnp.int32), others])
        return owners[jax.random.permutation(shuffle_key, BLK_DEV)]
    owners = jax.vmap(one_share)(jax.random.split(order_key, DESTS)).reshape(-1)
    window_block = owners // N_LAYER
    basis_block = owners % N_LAYER * KQ + jax.random.randint(column_key, (NBLK,), 0, KQ).astype(jnp.int32)
    return (window_block.astype(jnp.int32), basis_block.astype(jnp.int32))


def draw_block_row(key, part):
    return pick_owners(key)[0]


def draw_block_col(key, part):
    return pick_owners(key)[1]


def set_ends(entries, rng, low, largest):
    dims = entries.shape
    place = [jax.random.randint(jax.random.fold_in(rng, axis), (), 0, dims[axis]) for axis in range(len(dims))]
    entries = entries.at[tuple(place)].set(low)
    longest = dims.index(max(dims))
    place[longest] = (place[longest] + 1) % dims[longest]
    return entries.at[tuple(place)].set(largest)


def block_levels(rng, extent, pieces, smallest, top_value):
    gain, own = 1.0, jax.random.fold_in(rng, 6)
    for dim, blocks in pieces:
        steps = jnp.exp(jax.random.uniform(jax.random.fold_in(own, dim), (blocks,), jnp.float32, smallest / len(pieces), top_value / len(pieces)))
        gain = gain * jnp.repeat(steps, extent[dim] // blocks).reshape([-1 if axis == dim else 1 for axis in range(len(extent))])
    return gain


def bell_draw(key, shape, deviation, limit, shards=(), kind=jnp.bfloat16):
    level = block_levels(key, shape, shards, -0.22, 0.18) if shards else 1.0
    values = jax.random.normal(key, shape, jnp.float32) * deviation * level
    return jnp.minimum(jnp.maximum(values, -limit), limit).astype(kind)


def setup_inputs(seed: int = 0) -> dict:
    arg_keys = jax.random.split(jax.random.key(seed), 8)
    return {
        "blocks": bell_draw(arg_keys[0], (NBLK, BS, BS), 1.0, 6.0, ((0, 64),)),
        "block_aux": set_ends(jax.random.randint(arg_keys[1], (NBLK,), 0, NP), jax.random.fold_in(arg_keys[1], 1), 0, NP - 1).astype(jnp.int32),
        "block_row": draw_block_row(jax.random.fold_in(arg_keys[7], 71), 0),
        "block_col": draw_block_col(jax.random.fold_in(arg_keys[7], 71), 0),
        "extents": set_ends(jax.random.randint(arg_keys[4], (NBLK,), BS // 4, BS + 1), jax.random.fold_in(arg_keys[4], 1), BS // 4, BS).astype(jnp.int32),
        "occ_green": bell_draw(arg_keys[5], (NB, W), (5 * BS * BS * NBLK // (8 * NP)) ** -0.5, 0.00390625, ((0, 4), (1, 4))),
        "virt_green": bell_draw(arg_keys[6], (NB, W), (5 * BS * BS * NBLK // (8 * NP)) ** -0.5, 0.00390625, ((0, 4), (1, 4))),
    }


def reference(blocks, block_aux, block_row, block_col, extents, occ_green, virt_green):
    columns = jnp.arange(BS, dtype=jnp.int32)
    masked_tiles = jnp.where(columns[None, None, :] < extents[:, None, None], blocks, jnp.zeros((), blocks.dtype))
    anchor = jnp.zeros((), jnp.int32)

    def add_block(totals, record):
        occ_part, virt_part = totals
        one_tile, aux_index, row_block, col_block = record
        basis_start = (col_block * BS).astype(jnp.int32)
        window_start = (row_block * BS).astype(jnp.int32)
        occ_rows = lax.dynamic_slice_in_dim(occ_green, basis_start, BS, 0)
        virt_rows = lax.dynamic_slice_in_dim(virt_green, basis_start, BS, 0)
        occ_term = jnp.dot(one_tile, occ_rows, preferred_element_type=jnp.float32)
        virt_term = jnp.dot(one_tile, virt_rows, preferred_element_type=jnp.float32)
        where_to = (aux_index.astype(jnp.int32), window_start, anchor)
        occ_prior = lax.dynamic_slice(occ_part, where_to, (1, BS, W))
        virt_prior = lax.dynamic_slice(virt_part, where_to, (1, BS, W))
        occ_part = lax.dynamic_update_slice(occ_part, occ_prior + occ_term[None], where_to)
        virt_part = lax.dynamic_update_slice(virt_part, virt_prior + virt_term[None], where_to)
        return (occ_part, virt_part), None

    empty = jnp.zeros((NP, W, W), jnp.float32)
    (occ_part, virt_part), _ = lax.scan(add_block, (empty, empty), (masked_tiles, block_aux, block_row, block_col))
    return jnp.einsum("plv,qvl->pq", occ_part, virt_part, precision=lax.Precision.HIGHEST)
```

```python
import functools

import jax
import jax.numpy as jnp
from jax import lax
from jax.experimental import pallas as pl
from jax.experimental.pallas import tpu as pltpu
from jax.sharding import PartitionSpec as P

NP = 24
ROWS = 4
COLS = 16
LAYERS = 4
CAP = 2
OWNERS = COLS * LAYERS
BS = 128
QUARTER = BS // ROWS
WIDE = 512
HALF = NP // 2
TOP = 32700.0
STEPS = 64.0
ALL = ("row", "col", "layer")
F32 = jnp.float32
BF16 = jnp.bfloat16
S16 = jnp.int16


def params(mib):
    return pltpu.CompilerParams(vmem_limit_bytes=mib * 2**20)


def encode(block):
    peak = jnp.max(jnp.abs(block), axis=0, keepdims=True)
    level = jnp.ceil(jnp.log2(jnp.maximum(peak, 1e-30)) * STEPS)
    scaled = block * (jnp.exp2(level * (-1.0 / STEPS)) * TOP)
    return jnp.round(scaled).astype(jnp.int32).astype(S16), level


def decode(codes, level):
    return codes.astype(jnp.int32).astype(F32) * (jnp.exp2(level * (1.0 / STEPS)) * (1.0 / TOP))


def send_body(aux_ref, row_ref, col_ref, ext_ref, place_ref, blocks_ref, out_ref, count_ref, *, layer_blocks):
    del place_ref
    out_ref[...] = jnp.zeros(out_ref.shape, BF16)

    @pl.loop(0, OWNERS)
    def _(i):
        count_ref[i] = 0

    lane = lax.broadcasted_iota(jnp.int32, (QUARTER, BS), 1)
    meta_lane = lax.broadcasted_iota(jnp.int32, (8, BS), 1)

    @pl.loop(0, blocks_ref.shape[0])
    def _(i):
        col = col_ref[i]
        layer_of = col // layer_blocks
        kept = col - layer_of * layer_blocks
        owner = row_ref[i] * LAYERS + layer_of
        used = count_ref[owner]
        count_ref[owner] = used + 1
        tile = jnp.where(lane < ext_ref[i], blocks_ref[i].astype(F32), 0.0)
        out_ref[owner, pl.ds(pl.multiple_of(used * QUARTER, QUARTER), QUARTER), :] = tile.astype(BF16)
        old = out_ref[owner, 2 * QUARTER :, :].astype(F32)
        new = jnp.where(meta_lane == used * 2, aux_ref[i].astype(F32), old)
        new = jnp.where(meta_lane == used * 2 + 1, kept.astype(F32), new)
        out_ref[owner, 2 * QUARTER :, :] = new.astype(BF16)


def build_send(blocks, block_aux, block_row, block_col, extents, row_place, layer_blocks):
    held = blocks.shape[0]
    return pl.pallas_call(
        functools.partial(send_body, layer_blocks=layer_blocks),
        grid_spec=pltpu.PrefetchScalarGridSpec(
            num_scalar_prefetch=5,
            grid=(1,),
            in_specs=[pl.BlockSpec((held, QUARTER, BS), lambda i, a, r, c, e, p: (0, p[0], 0))],
            out_specs=pl.BlockSpec((OWNERS, 2 * QUARTER + 8, BS), lambda i, a, r, c, e, p: (0, 0, 0)),
            scratch_shapes=[pltpu.SMEM((OWNERS,), jnp.int32)],
        ),
        out_shape=jax.ShapeDtypeStruct((OWNERS, 2 * QUARTER + 8, BS), BF16),
        compiler_params=params(16),
        name="build_send",
    )(block_aux, block_row, block_col, extents, row_place, blocks)


def contract_body(meta_ref, place_ref, own_ref, prev_ref, next_ref, far_a_ref, far_b_ref, green_ref, *rest, transposed):
    if transposed:
        keep_ref, send0_ref, send1_ref, acc_ref, tile_ref = rest
    else:
        keep_ref, send0_ref, send1_ref, acc_ref, tile_ref = rest
    row_place = place_ref[0]
    acc_ref[...] = jnp.zeros(acc_ref.shape, F32)
    at = [pl.multiple_of(((row_place + d) % ROWS) * QUARTER, QUARTER) for d in (0, ROWS - 1, 1, 2)]
    half = OWNERS // 2

    def one_source(source, far_ref, far_source):
        for slot in range(CAP):
            span = slice(slot * QUARTER, (slot + 1) * QUARTER)
            tile_ref[slot, pl.ds(at[0], QUARTER), :] = own_ref[source, span, :]
            tile_ref[slot, pl.ds(at[1], QUARTER), :] = prev_ref[source, span, :]
            tile_ref[slot, pl.ds(at[2], QUARTER), :] = next_ref[source, span, :]
            tile_ref[slot, pl.ds(at[3], QUARTER), :] = far_ref[far_source, span, :]
        for slot in range(CAP):
            tile = tile_ref[slot]
            aux = meta_ref[source, 2 * slot]
            kept = meta_ref[source, 2 * slot + 1]
            green = green_ref[kept]
            if transposed:
                term = lax.dot_general(green, tile, (((1,), (1,)), ((), ())), preferred_element_type=F32)
                for low in range(4):
                    lanes = slice(low * BS, (low + 1) * BS)
                    acc_ref[aux, :, lanes] += term[low * BS : (low + 1) * BS, :]
            else:
                acc_ref[aux] += jnp.dot(tile, green, preferred_element_type=F32)

    @pl.loop(0, half)
    def _(source):
        one_source(source, far_a_ref, source)

    @pl.loop(0, half)
    def _(source):
        one_source(source + half, far_b_ref, source)

    bit_a = place_ref[1]
    bit_b = place_ref[2]

    def piece(a, b):
        return pl.multiple_of(jnp.where(b == 0, a, 3 - a) * QUARTER, QUARTER)

    for h, send_ref in ((0, send0_ref), (1, send1_ref)):
        kept_rows = []
        sent_rows = []
        for other in range(2):
            if h == 0:
                kept_rows.append(piece(bit_a, other))
                sent_rows.append(piece(1 - bit_a, other))
            else:
                kept_rows.append(piece(other, bit_b))
                sent_rows.append(piece(other, 1 - bit_b))

        @pl.loop(0, HALF)
        def _(p):
            levels = []
            for other in range(2):
                keep_ref[h, other, p] = acc_ref[p + h * HALF, pl.ds(kept_rows[other], QUARTER), :]
                codes, level = encode(acc_ref[p + h * HALF, pl.ds(sent_rows[other], QUARTER), :])
                send_ref[other, p] = codes
                levels.append(level)
            put_levels(send_ref, 0, p, levels[0])
            put_levels(send_ref, 1, p, levels[1])


def put_levels(ref, which, p, level):
    count = ref.shape[1] - 1
    at_row = lax.broadcasted_iota(jnp.int32, (QUARTER, ref.shape[-1]), 0) == p
    old = ref[which, count].astype(jnp.int32)
    ref[which, count] = jnp.where(at_row, level.astype(jnp.int32), old).astype(S16)


def get_levels(ref, which, p):
    count = ref.shape[1] - 1
    at_row = lax.broadcasted_iota(jnp.int32, (QUARTER, ref.shape[-1]), 0) == p
    rows = ref[which, count].astype(jnp.int32)
    return jnp.sum(jnp.where(at_row, rows, 0), axis=0, keepdims=True).astype(F32)


def contract(meta, place, quarters, green, transposed):
    own, prev, nxt, far_a, far_b = quarters
    vmem = pl.BlockSpec(memory_space=pltpu.VMEM)
    smem = pl.BlockSpec(memory_space=pltpu.SMEM)
    code = jax.ShapeDtypeStruct((2, HALF + 1, QUARTER, WIDE), S16)
    return pl.pallas_call(
        functools.partial(contract_body, transposed=transposed),
        in_specs=[smem, smem] + [vmem] * 6,
        out_specs=[vmem] * 3,
        out_shape=[jax.ShapeDtypeStruct((2, 2, HALF, QUARTER, WIDE), F32), code, code],
        scratch_shapes=[pltpu.VMEM((NP, BS, WIDE), F32), pltpu.VMEM((CAP, BS, BS), BF16)],
        compiler_params=params(48),
        name="contract_virt" if transposed else "contract_occ",
    )(meta, place, own, prev, nxt, far_a, far_b, green)


def halve_body(place_ref, keep_ref, got0_ref, got1_ref, left_ref, send0_ref, send1_ref):
    for h, got_ref, send_ref in ((0, got0_ref, send0_ref), (1, got1_ref, send1_ref)):
        mine = place_ref[2 - h]

        @pl.loop(0, HALF)
        def _(p):
            left_ref[h, p] = keep_ref[h, mine, p] + decode(got_ref[mine, p], get_levels(got_ref, mine, p))
            away = 1 - mine
            total = keep_ref[h, away, p] + decode(got_ref[away, p], get_levels(got_ref, away, p))
            codes, level = encode(total)
            send_ref[0, p] = codes
            put_levels(send_ref, 0, p, level)


def halve(place, keep, got0, got1, name):
    vmem = pl.BlockSpec(memory_space=pltpu.VMEM)
    smem = pl.BlockSpec(memory_space=pltpu.SMEM)
    code = jax.ShapeDtypeStruct((1, HALF + 1, QUARTER, WIDE), S16)
    return pl.pallas_call(
        halve_body,
        in_specs=[smem] + [vmem] * 3,
        out_specs=[vmem] * 3,
        out_shape=[jax.ShapeDtypeStruct((2, HALF, QUARTER, WIDE), F32), code, code],
        compiler_params=params(40),
        name=name,
    )(place, keep, got0, got1)


def finish_body(left_ref, got0_ref, got1_ref, out_ref, *, split):
    for h, got_ref in ((0, got0_ref), (1, got1_ref)):

        @pl.loop(0, HALF)
        def _(p):
            total = left_ref[h, p] + decode(got_ref[0, p], get_levels(got_ref, 0, p))
            codes, level = encode(total)
            if split:
                for low in range(4):
                    lanes = slice(low * BS, (low + 1) * BS)
                    out_ref[low, p + h * HALF] = codes[:, lanes]
                    put_levels(out_ref, low, p + h * HALF, level[:, lanes])
            else:
                out_ref[0, p + h * HALF] = codes
                put_levels(out_ref, 0, p + h * HALF, level)


def finish(left, got0, got1, split, name):
    vmem = pl.BlockSpec(memory_space=pltpu.VMEM)
    shape = (4, NP + 1, QUARTER, BS) if split else (1, NP + 1, QUARTER, WIDE)
    return pl.pallas_call(
        functools.partial(finish_body, split=split),
        in_specs=[vmem] * 3,
        out_specs=vmem,
        out_shape=jax.ShapeDtypeStruct(shape, S16),
        compiler_params=params(32),
        name=name,
    )(left, got0, got1)


def pair_body(low_ref, own_ref, one_ref, two_ref, three_ref, virt_ref, out_ref, occ_ref, vir_ref):
    here = low_ref[0]

    @pl.loop(0, NP)
    def _(p):
        values = decode(virt_ref[0, p], get_levels(virt_ref, 0, p))
        for low in range(4):
            vir_ref[p, low * QUARTER : (low + 1) * QUARTER, :] = values[:, low * BS : (low + 1) * BS]
        own = decode(own_ref[here, p], get_levels(own_ref, here, p))
        occ_ref[p, pl.ds(pl.multiple_of(here * QUARTER, QUARTER), QUARTER), :] = own
        for d, ref in ((1, one_ref), (2, two_ref), (3, three_ref)):
            source = (here + 4 - d) % 4
            part = decode(ref[0, p], get_levels(ref, 0, p))
            occ_ref[p, pl.ds(pl.multiple_of(source * QUARTER, QUARTER), QUARTER), :] = part

    @pl.loop(0, NP)
    def _(p):
        occ = occ_ref[p]
        for q in range(NP):
            out_ref[p, q : q + 1, :] = jnp.sum(occ * vir_ref[q], axis=0, keepdims=True)


def pair(low, own, others, virt):
    vmem = pl.BlockSpec(memory_space=pltpu.VMEM)
    smem = pl.BlockSpec(memory_space=pltpu.SMEM)
    return pl.pallas_call(
        pair_body,
        in_specs=[smem] + [vmem] * 5,
        out_specs=vmem,
        out_shape=jax.ShapeDtypeStruct((NP, NP, BS), F32),
        scratch_shapes=[pltpu.VMEM((NP, BS, BS), F32), pltpu.VMEM((NP, BS, BS), F32)],
        compiler_params=params(32),
        name="pair",
    )(low, own, *others, virt)


def rotate(size, step):
    return [(i, (i + step) % size) for i in range(size)]


def rotate_low(step):
    return [(c, c - c % 4 + (c + step) % 4) for c in range(COLS)]


def rotate_high(step):
    return [(c, (c + 4 * step) % COLS) for c in range(COLS)]


PAIRS_A = [(0, 1), (1, 0), (2, 3), (3, 2)]
PAIRS_B = [(0, 3), (3, 0), (1, 2), (2, 1)]


def index_of(row, col, layer):
    return (row * COLS + col) * LAYERS + layer


SWAP = [
    (index_of(r, c, l), index_of(c // 4, 4 * r + c % 4, l))
    for r in range(ROWS)
    for c in range(COLS)
    for l in range(LAYERS)
]


def tree_sum(values):
    rounds = (
        ("layer", [rotate(LAYERS, d) for d in (1, 2, 3)]),
        ("col", [rotate_low(d) for d in (1, 2, 3)]),
        ("row", [rotate(ROWS, d) for d in (1, 2, 3)]),
        ("col", [rotate_high(d) for d in (1, 2, 3)]),
    )
    for axis, perms in rounds:
        one, two, three = [lax.ppermute(values, axis, perm) for perm in perms]
        values = (values + two) + (one + three)
    return values


def on_device(blocks, block_aux, block_row, block_col, extents, occ_green, virt_green):
    layer_blocks = occ_green.shape[0] // BS
    row_place = lax.axis_index("row").astype(jnp.int32)
    col_place = lax.axis_index("col").astype(jnp.int32)
    layer_place = lax.axis_index("layer").astype(jnp.int32)
    bit_a = ((layer_place == 1) | (layer_place == 2)).astype(jnp.int32)
    bit_b = layer_place // 2
    place = jnp.stack([row_place, bit_a, bit_b])

    send = build_send(blocks, block_aux, block_row, block_col, extents, row_place[None], layer_blocks)
    own = lax.all_to_all(send, ("col", "layer"), 0, 0, tiled=True)
    meta = own[:, 2 * QUARTER, :4].astype(jnp.int32)
    prev = lax.ppermute(own, "row", rotate(ROWS, 1))
    nxt = lax.ppermute(own, "row", rotate(ROWS, -1))
    half = OWNERS // 2
    far_a = lax.ppermute(prev[:half], "row", rotate(ROWS, 1))
    far_b = lax.ppermute(nxt[half:], "row", rotate(ROWS, -1))
    quarters = (own, prev, nxt, far_a, far_b)

    virt_blocks = virt_green.reshape(layer_blocks, BS, WIDE).transpose(0, 2, 1)
    occ_blocks = occ_green.reshape(layer_blocks, BS, WIDE)

    v_keep, v_send0, v_send1 = contract(meta, place, quarters, virt_blocks, True)
    v_got0 = lax.ppermute(v_send0, "layer", PAIRS_A)
    v_got1 = lax.ppermute(v_send1, "layer", PAIRS_B)
    o_keep, o_send0, o_send1 = contract(meta, place, quarters, occ_blocks, False)
    o_got0 = lax.ppermute(o_send0, "layer", PAIRS_A)
    o_got1 = lax.ppermute(o_send1, "layer", PAIRS_B)
    v_left, v_send0, v_send1 = halve(place, v_keep, v_got0, v_got1, "halve_virt")
    v_got0 = lax.ppermute(v_send0, "layer", PAIRS_B)
    v_got1 = lax.ppermute(v_send1, "layer", PAIRS_A)
    o_left, o_send0, o_send1 = halve(place, o_keep, o_got0, o_got1, "halve_occ")
    o_got0 = lax.ppermute(o_send0, "layer", PAIRS_B)
    o_got1 = lax.ppermute(o_send1, "layer", PAIRS_A)
    virt = finish(v_left, v_got0, v_got1, False, "finish_virt")
    virt = lax.ppermute(virt, ALL, SWAP)
    occ = finish(o_left, o_got0, o_got1, True, "finish_occ")

    low = (col_place % 4)[None]
    others = []
    for d in (1, 2, 3):
        part = lax.dynamic_slice_in_dim(occ, (low[0] + d) % 4, 1, 0)
        others.append(lax.ppermute(part, "col", rotate_low(d)))
    partial = pair(low, occ, others, virt)
    return tree_sum(jnp.sum(partial, axis=-1))


def solution(mesh):
    in_specs = (
        P(("col", "layer"), None, None),
        P(("col", "layer")),
        P(("col", "layer")),
        P(("col", "layer")),
        P(("col", "layer")),
        P("layer", "row"),
        P("layer", "row"),
    )
    return jax.shard_map(on_device, mesh=mesh, in_specs=in_specs, out_specs=P(), check_vma=False)
```

```python
import functools

import jax
import jax.numpy as jnp
from jax import lax
from jax.experimental import pallas as pl
from jax.experimental.pallas import tpu as pltpu
from jax.sharding import PartitionSpec as P

NP = 24
ROWS = 4
COLS = 16
LAYERS = 4
CAP = 2
OWNERS = COLS * LAYERS
BS = 128
QUARTER = BS // ROWS
WIDE = 512
HALF = NP // 2
TOP = 32700.0
STEPS = 64.0
ALL = ("row", "col", "layer")
F32 = jnp.float32
BF16 = jnp.bfloat16
S16 = jnp.int16


def params(mib):
    return pltpu.CompilerParams(vmem_limit_bytes=mib * 2**20)


def encode(block):
    peak = jnp.max(jnp.abs(block), axis=0, keepdims=True)
    level = jnp.ceil(jnp.log2(jnp.maximum(peak, 1e-30)) * STEPS)
    scaled = block * (jnp.exp2(level * (-1.0 / STEPS)) * TOP)
    return jnp.round(scaled).astype(jnp.int32).astype(S16), level


def decode(codes, level):
    return codes.astype(jnp.int32).astype(F32) * (jnp.exp2(level * (1.0 / STEPS)) * (1.0 / TOP))


class Plan:
    def __init__(self, quarters):
        self.quarters = quarters
        self.group = 4 // quarters
        self.rows = 8 * quarters * self.group
        self.blocks = HALF // self.group

    def coded(self, count):
        return count * self.rows + (count + 15) // 16 * 16


def at_block(plan, index):
    return pl.ds(pl.multiple_of(index * plan.rows, 16), plan.rows)


def level_rows(plan, count):
    return slice(count * plan.rows, plan.coded(count))


def put(ref, lead, plan, count, index, block):
    codes, level = encode(block)
    put_coded(ref, lead, plan, count, index, codes, level)


def put_coded(ref, lead, plan, count, index, codes, level):
    ref[(*lead, at_block(plan, index), slice(None))] = codes
    where = (*lead, level_rows(plan, count), slice(None))
    old = ref[where].astype(jnp.int32)
    here = lax.broadcasted_iota(jnp.int32, old.shape, 0) == index
    ref[where] = jnp.where(here, level.astype(jnp.int32), old).astype(S16)


def get(ref, lead, plan, count, index):
    codes = ref[(*lead, at_block(plan, index), slice(None))]
    rows = ref[(*lead, level_rows(plan, count), slice(None))].astype(jnp.int32)
    here = lax.broadcasted_iota(jnp.int32, rows.shape, 0) == index
    level = jnp.sum(jnp.where(here, rows, 0), axis=0, keepdims=True)
    return decode(codes, level.astype(F32))


def send_body(aux_ref, row_ref, col_ref, ext_ref, place_ref, blocks_ref, *rest, layer_blocks):
    del place_ref
    out_refs, count_ref = rest[:CAP], rest[CAP]
    for ref in out_refs:
        ref[...] = jnp.zeros(ref.shape, BF16)

    @pl.loop(0, OWNERS)
    def _(i):
        count_ref[i] = 0

    lane = lax.broadcasted_iota(jnp.int32, (QUARTER, BS), 1)
    meta_lane = lax.broadcasted_iota(jnp.int32, (8, BS), 1)

    @pl.loop(0, blocks_ref.shape[0])
    def _(i):
        col = col_ref[i]
        layer_of = col // layer_blocks
        kept = col - layer_of * layer_blocks
        owner = (row_ref[i] % 4 * 4 + row_ref[i] // 4) * LAYERS + layer_of
        used = count_ref[owner]
        count_ref[owner] = used + 1
        tile = jnp.where(lane < ext_ref[i], blocks_ref[i].astype(F32), 0.0).astype(BF16)
        meta = jnp.where(meta_lane == 0, aux_ref[i], jnp.where(meta_lane == 1, kept, 0)).astype(F32).astype(BF16)
        for slot, ref in enumerate(out_refs):

            @pl.when(used == slot)
            def _():
                ref[owner, :QUARTER, :] = tile
                ref[owner, QUARTER:, :] = meta


def build_send(blocks, block_aux, block_row, block_col, extents, row_place, layer_blocks):
    held = blocks.shape[0]
    shape = (OWNERS, QUARTER + 8, BS)
    return pl.pallas_call(
        functools.partial(send_body, layer_blocks=layer_blocks),
        grid_spec=pltpu.PrefetchScalarGridSpec(
            num_scalar_prefetch=5,
            grid=(1,),
            in_specs=[pl.BlockSpec((held, QUARTER, BS), lambda i, a, r, c, e, p: (0, p[0], 0))],
            out_specs=[pl.BlockSpec(shape, lambda i, a, r, c, e, p: (0, 0, 0))] * CAP,
            scratch_shapes=[pltpu.SMEM((OWNERS,), jnp.int32)],
        ),
        out_shape=[jax.ShapeDtypeStruct(shape, BF16)] * CAP,
        compiler_params=params(16),
        name="build_send",
    )(block_aux, block_row, block_col, extents, row_place, blocks)


def split_pieces(place_ref, plan, rows_of, keep_ref, send_refs):
    bit_a = place_ref[1]
    bit_b = place_ref[2]

    def piece(a, b):
        return jnp.where(b == 0, a, 3 - a)

    for h, send_ref in enumerate(send_refs):
        kept = [piece(bit_a, o) if h == 0 else piece(o, bit_b) for o in range(2)]
        sent = [piece(1 - bit_a, o) if h == 0 else piece(o, 1 - bit_b) for o in range(2)]

        @pl.loop(0, plan.blocks)
        def _(block):
            first = h * HALF + block * plan.group
            for other in range(2):
                keep_ref[h, other, block] = rows_of(first, kept[other])
                put(send_ref, (), plan, 2 * plan.blocks, other * plan.blocks + block, rows_of(first, sent[other]))


def virt_body(meta0_ref, meta1_ref, place_ref, *rest, plan, names):
    per_slot = len(names)
    tile_refs = [rest[:per_slot], rest[per_slot : 2 * per_slot]]
    green_ref, keep_ref, send0_ref, send1_ref, acc_ref = rest[2 * per_slot :]
    acc_ref[...] = jnp.zeros(acc_ref.shape, F32)
    half = OWNERS // 2

    for part in range(2):

        @pl.loop(0, half)
        def _(local):
            source = local + part * half
            for slot, meta_ref in enumerate((meta0_ref, meta1_ref)):
                refs = tile_refs[slot]
                parts = [ref[source, :QUARTER, :] for ref in refs[:3]] + [refs[3 + part][local, :QUARTER, :]]
                tile = jnp.concatenate(parts, axis=0)
                aux = meta_ref[source, 0]
                kept = meta_ref[source, 1]
                acc_ref[aux] += jnp.dot(tile, green_ref[kept], preferred_element_type=F32)

    def rows_of(first, piece):
        parts = []
        for j in range(plan.group):
            for quarter in range(plan.quarters):
                at = pl.multiple_of(quarter * QUARTER + piece * 8, 8)
                parts.append(acc_ref[first + j, pl.ds(at, 8), :])
        return jnp.concatenate(parts, axis=0)

    split_pieces(place_ref, plan, rows_of, keep_ref, (send0_ref, send1_ref))


def step_shapes(plan):
    return [
        jax.ShapeDtypeStruct((2, 2, plan.blocks, plan.rows, WIDE), F32),
        jax.ShapeDtypeStruct((plan.coded(2 * plan.blocks), WIDE), S16),
        jax.ShapeDtypeStruct((plan.coded(2 * plan.blocks), WIDE), S16),
    ]


VMEM = pl.BlockSpec(memory_space=pltpu.VMEM)
SMEM = pl.BlockSpec(memory_space=pltpu.SMEM)


def contract_virt(metas, place, slots, names, green, plan, name):
    tiles = [slot[n] for slot in slots for n in names]
    return pl.pallas_call(
        functools.partial(virt_body, plan=plan, names=names),
        in_specs=[SMEM] * 3 + [VMEM] * (len(tiles) + 1),
        out_specs=[VMEM] * 3,
        out_shape=step_shapes(plan),
        scratch_shapes=[pltpu.VMEM((NP, plan.quarters * QUARTER, WIDE), F32)],
        compiler_params=params(48),
        name=name,
    )(*metas, place, *tiles, green)


def occ_slot(meta_ref, place_ref, tile_refs, green_ref, acc_ref, tile_ref):
    own_ref, prev_ref, next_ref, far_a_ref, far_b_ref = tile_refs
    row_place = place_ref[0]
    at = [pl.multiple_of(((row_place + d) % ROWS) * QUARTER, QUARTER) for d in (0, ROWS - 1, 1, 2)]
    half = OWNERS // 2
    for part, far_ref in enumerate((far_a_ref, far_b_ref)):

        @pl.loop(0, half // 2)
        def _(step):
            for k in range(2):
                local = step * 2 + k
                source = local + part * half
                tile_ref[k, pl.ds(at[0], QUARTER), :] = own_ref[source, :QUARTER, :]
                tile_ref[k, pl.ds(at[1], QUARTER), :] = prev_ref[source, :QUARTER, :]
                tile_ref[k, pl.ds(at[2], QUARTER), :] = next_ref[source, :QUARTER, :]
                tile_ref[k, pl.ds(at[3], QUARTER), :] = far_ref[local, :QUARTER, :]
            for k in range(2):
                source = step * 2 + k + part * half
                aux = meta_ref[source, 0]
                kept = meta_ref[source, 1]
                term = lax.dot_general(
                    green_ref[kept], tile_ref[k], (((1,), (1,)), ((), ())), preferred_element_type=F32
                )
                for low in range(4):
                    lanes = slice(low * BS, (low + 1) * BS)
                    acc_ref[aux, :, lanes] += term[low * BS : (low + 1) * BS, :]


def occ_first_body(meta_ref, place_ref, *rest):
    tile_refs, (green_ref, out_ref, tile_ref) = rest[:5], rest[5:]
    out_ref[...] = jnp.zeros(out_ref.shape, F32)
    occ_slot(meta_ref, place_ref, tile_refs, green_ref, out_ref, tile_ref)


def occ_last_body(meta_ref, place_ref, *rest, plan):
    tile_refs, (green_ref, before_ref, keep_ref, send0_ref, send1_ref, acc_ref, tile_ref, sem) = rest[:5], rest[5:]
    load = pltpu.make_async_copy(before_ref, acc_ref, sem)
    load.start()
    load.wait()
    occ_slot(meta_ref, place_ref, tile_refs, green_ref, acc_ref, tile_ref)

    def rows_of(first, piece):
        parts = []
        for quarter in range(4):
            at = pl.multiple_of(quarter * QUARTER + piece * 8, 8)
            parts.append(acc_ref[first, pl.ds(at, 8), :])
        return jnp.concatenate(parts, axis=0)

    split_pieces(place_ref, plan, rows_of, keep_ref, (send0_ref, send1_ref))


ALL_QUARTERS = ("own", "prev", "next", "far_a", "far_b")
ACC = (NP, BS, WIDE)


def contract_occ_first(meta, place, slot, green):
    return pl.pallas_call(
        occ_first_body,
        in_specs=[SMEM] * 2 + [VMEM] * 6,
        out_specs=VMEM,
        out_shape=jax.ShapeDtypeStruct(ACC, F32),
        scratch_shapes=[pltpu.VMEM((2, BS, BS), BF16)],
        compiler_params=params(40),
        name="occ_first",
    )(meta, place, *[slot[n] for n in ALL_QUARTERS], green)


def contract_occ_last(meta, place, slot, green, before, plan):
    return pl.pallas_call(
        functools.partial(occ_last_body, plan=plan),
        in_specs=[SMEM] * 2 + [VMEM] * 6 + [pl.BlockSpec(memory_space=pl.ANY)],
        out_specs=[VMEM] * 3,
        out_shape=step_shapes(plan),
        scratch_shapes=[pltpu.VMEM(ACC, F32), pltpu.VMEM((2, BS, BS), BF16), pltpu.SemaphoreType.DMA(())],
        compiler_params=params(48),
        name="occ_last",
    )(meta, place, *[slot[n] for n in ALL_QUARTERS], green, before)


def halve_body(place_ref, keep_ref, got0_ref, got1_ref, left_ref, send0_ref, send1_ref, *, plan):
    for h, got_ref, send_ref in ((0, got0_ref, send0_ref), (1, got1_ref, send1_ref)):
        mine = place_ref[2 - h]
        away = 1 - mine

        @pl.loop(0, plan.blocks)
        def _(b):
            left_ref[h, b] = keep_ref[h, mine, b] + get(got_ref, (), plan, 2 * plan.blocks, mine * plan.blocks + b)
            total = keep_ref[h, away, b] + get(got_ref, (), plan, 2 * plan.blocks, away * plan.blocks + b)
            put(send_ref, (), plan, plan.blocks, b, total)


def halve(place, keep, got0, got1, plan, name):
    code = jax.ShapeDtypeStruct((plan.coded(plan.blocks), WIDE), S16)
    return pl.pallas_call(
        functools.partial(halve_body, plan=plan),
        in_specs=[SMEM] + [VMEM] * 3,
        out_specs=[VMEM] * 3,
        out_shape=[jax.ShapeDtypeStruct((2, plan.blocks, plan.rows, WIDE), F32), code, code],
        compiler_params=params(40),
        name=name,
    )(place, keep, got0, got1)


def finish_body(left_ref, got0_ref, got1_ref, out_ref, *, plan, split):
    count = 2 * plan.blocks
    for h, got_ref in ((0, got0_ref), (1, got1_ref)):

        @pl.loop(0, plan.blocks)
        def _(b):
            total = left_ref[h, b] + get(got_ref, (), plan, plan.blocks, b)
            index = h * plan.blocks + b
            if split:
                codes, level = encode(total)
                for low in range(4):
                    lanes = slice(low * BS, (low + 1) * BS)
                    put_coded(out_ref, (low,), plan, count, index, codes[:, lanes], level[:, lanes])
            else:
                put(out_ref, (), plan, count, index, total)


def finish(left, got0, got1, plan, split, name):
    rows = plan.coded(2 * plan.blocks)
    shape = (4, rows, BS) if split else (rows, WIDE)
    return pl.pallas_call(
        functools.partial(finish_body, plan=plan, split=split),
        in_specs=[VMEM] * 3,
        out_specs=VMEM,
        out_shape=jax.ShapeDtypeStruct(shape, S16),
        compiler_params=params(32),
        name=name,
    )(left, got0, got1)


def pair_body(place_ref, own_ref, one_ref, two_ref, three_ref, *rest, plans, shifts, occ_plan):
    virt_refs, (out_ref, occ_ref, vir_ref) = rest[: len(plans)], rest[len(plans) :]
    here = place_ref[0]
    high = place_ref[1]

    for ref, plan, shift in zip(virt_refs, plans, shifts):
        at = [((high + s) % 4) * 8 for s in shift]

        @pl.loop(0, 2 * plan.blocks)
        def _(b):
            values = get(ref, (), plan, 2 * plan.blocks, b)
            for j in range(plan.group):
                for k in range(plan.quarters):
                    rows = slice((j * plan.quarters + k) * 8, (j * plan.quarters + k + 1) * 8)
                    for low in range(4):
                        to = pl.ds(pl.multiple_of(low * QUARTER + at[k], 8), 8)
                        vir_ref[b * plan.group + j, to, :] = values[rows, low * BS : (low + 1) * BS]

    @pl.loop(0, NP)
    def _(p):
        own = get(own_ref, (here,), occ_plan, NP, p)
        occ_ref[p, pl.ds(pl.multiple_of(here * QUARTER, QUARTER), QUARTER), :] = own
        for d, ref in ((1, one_ref), (2, two_ref), (3, three_ref)):
            source = (here + 4 - d) % 4
            part = get(ref, (0,), occ_plan, NP, p)
            occ_ref[p, pl.ds(pl.multiple_of(source * QUARTER, QUARTER), QUARTER), :] = part

    @pl.loop(0, NP)
    def _(p):
        occ = occ_ref[p]
        for q in range(NP):
            out_ref[p, q : q + 1, :] = jnp.sum(occ * vir_ref[q], axis=0, keepdims=True)


def pair(place, own, others, virts, plans, shifts, occ_plan):
    return pl.pallas_call(
        functools.partial(pair_body, plans=plans, shifts=shifts, occ_plan=occ_plan),
        in_specs=[SMEM] + [VMEM] * (4 + len(virts)),
        out_specs=VMEM,
        out_shape=jax.ShapeDtypeStruct((NP, NP, BS), F32),
        scratch_shapes=[pltpu.VMEM((NP, BS, BS), F32), pltpu.VMEM((NP, BS, BS), F32)],
        compiler_params=params(32),
        name="pair",
    )(place, own, *others, *virts)


def rotate(size, step):
    return [(i, (i + step) % size) for i in range(size)]


def rotate_low(step):
    return [(c, c - c % 4 + (c + step) % 4) for c in range(COLS)]


def rotate_high(step):
    return [(c, (c + 4 * step) % COLS) for c in range(COLS)]


PAIRS_A = [(0, 1), (1, 0), (2, 3), (3, 2)]
PAIRS_B = [(0, 3), (3, 0), (1, 2), (2, 1)]


def index_of(row, col, layer):
    return (row * COLS + col) * LAYERS + layer


SWAP = [
    (index_of(r, c, l), index_of(c % 4, c // 4 * 4 + r, l))
    for r in range(ROWS)
    for c in range(COLS)
    for l in range(LAYERS)
]


def tree_sum(values):
    rounds = (
        ("layer", [rotate(LAYERS, d) for d in (1, 2, 3)]),
        ("col", [rotate_low(d) for d in (1, 2, 3)]),
        ("row", [rotate(ROWS, d) for d in (1, 2, 3)]),
        ("col", [rotate_high(d) for d in (1, 2, 3)]),
    )
    for axis, perms in rounds:
        one, two, three = [lax.ppermute(values, axis, perm) for perm in perms]
        values = (values + two) + (one + three)
    return values


def gather_rows(own):
    prev = lax.ppermute(own, "row", rotate(ROWS, 1))
    nxt = lax.ppermute(own, "row", rotate(ROWS, -1))
    half = OWNERS // 2
    far_a = lax.ppermute(prev[:half], "row", rotate(ROWS, 1))
    far_b = lax.ppermute(nxt[half:], "row", rotate(ROWS, -1))
    return {"own": own, "prev": prev, "next": nxt, "far_a": far_a, "far_b": far_b}


def layer_swap(send0, send1, perms):
    return lax.ppermute(send0, "layer", perms[0]), lax.ppermute(send1, "layer", perms[1])


FIRST = (PAIRS_A, PAIRS_B)
SECOND = (PAIRS_B, PAIRS_A)


def after(*values):
    return lax.optimization_barrier(values)


def on_device(blocks, block_aux, block_row, block_col, extents, occ_green, virt_green):
    layer_blocks = occ_green.shape[0] // BS
    row_place = lax.axis_index("row").astype(jnp.int32)
    col_place = lax.axis_index("col").astype(jnp.int32)
    layer_place = lax.axis_index("layer").astype(jnp.int32)
    bit_a = ((layer_place == 1) | (layer_place == 2)).astype(jnp.int32)
    bit_b = layer_place // 2
    place = jnp.stack([row_place, bit_a, bit_b])

    full = Plan(4)
    send0, send1 = build_send(blocks, block_aux, block_row, block_col, extents, row_place[None], layer_blocks)
    own0 = lax.all_to_all(send0, ("col", "layer"), 0, 0, tiled=True)
    own0, send1 = after(own0, send1)
    own1 = lax.all_to_all(send1, ("col", "layer"), 0, 0, tiled=True)
    virt_blocks = virt_green.reshape(layer_blocks, BS, WIDE)
    occ_blocks = occ_green.reshape(layer_blocks, BS, WIDE).transpose(0, 2, 1)
    slot0 = gather_rows(own0)
    own1, occ_blocks, slot0["far_a"], slot0["far_b"] = after(own1, occ_blocks, slot0["far_a"], slot0["far_b"])
    slot1 = gather_rows(own1)
    meta0, meta1 = [own[:, QUARTER, :2].astype(jnp.int32) for own in (own0, own1)]
    metas, slots = (meta0, meta1), (slot0, slot1)

    o_acc = contract_occ_first(meta0, place, slot0, occ_blocks)
    o_acc, virt_blocks = after(o_acc, virt_blocks)
    v_keep, v0, v1 = contract_virt(metas, place, slots, ALL_QUARTERS, virt_blocks, full, "contract_virt")
    v_got = layer_swap(v0, v1, FIRST)
    o_acc, v_keep = after(o_acc, v_keep)
    o_keep, o0, o1 = contract_occ_last(meta1, place, slot1, occ_blocks, o_acc, full)
    v_keep, o_keep = after(v_keep, o_keep)
    v_left, v0, v1 = halve(place, v_keep, *v_got, full, "halve_virt")
    v_got = layer_swap(v0, v1, SECOND)
    o0, o1, *v_got = after(o0, o1, *v_got)
    o_got = layer_swap(o0, o1, FIRST)
    virt = finish(v_left, *v_got, full, False, "finish_virt")
    virt, o_keep = after(virt, o_keep)
    virt = lax.ppermute(virt, ALL, SWAP)
    o_left, o0, o1 = halve(place, o_keep, *o_got, full, "halve_occ")
    o_got = layer_swap(o0, o1, SECOND)
    occ = finish(o_left, *o_got, full, True, "finish_occ")

    low = col_place // 4
    others = []
    for d in (1, 2, 3):
        part = lax.dynamic_slice_in_dim(occ, (low + d) % 4, 1, 0)
        others.append(lax.ppermute(part, "col", rotate_high(d)))
    here = jnp.stack([low, col_place % 4])
    partial = pair(here, occ, others, [virt], (full,), ((0, 3, 1, 2),), full)
    return tree_sum(jnp.sum(partial, axis=-1))


def solution(mesh):
    in_specs = (
        P(("col", "layer"), None, None),
        P(("col", "layer")),
        P(("col", "layer")),
        P(("col", "layer")),
        P(("col", "layer")),
        P("layer", "row"),
        P("layer", "row"),
    )
    return jax.shard_map(on_device, mesh=mesh, in_specs=in_specs, out_specs=P(), check_vma=False)
```

```python
import functools

import jax
import jax.numpy as jnp
from jax import lax
from jax.experimental import pallas as pl
from jax.experimental.pallas import tpu as pltpu
from jax.sharding import PartitionSpec as P

NP = 24
ROWS = 4
COLS = 16
LAYERS = 4
CAP = 2
OWNERS = COLS * LAYERS
BS = 128
QUARTER = BS // ROWS
WIDE = 512
HALF = NP // 2
TOP = 32700.0
STEPS = 64.0
ALL = ("row", "col", "layer")
F32 = jnp.float32
BF16 = jnp.bfloat16
S16 = jnp.int16


def params(mib):
    return pltpu.CompilerParams(vmem_limit_bytes=mib * 2**20)


def encode(block):
    peak = jnp.max(jnp.abs(block), axis=0, keepdims=True)
    level = jnp.ceil(jnp.log2(jnp.maximum(peak, 1e-30)) * STEPS)
    scaled = block * (jnp.exp2(level * (-1.0 / STEPS)) * TOP)
    return jnp.round(scaled).astype(jnp.int32).astype(S16), level


def decode(codes, level):
    return codes.astype(jnp.int32).astype(F32) * (jnp.exp2(level * (1.0 / STEPS)) * (1.0 / TOP))


class Plan:
    def __init__(self, quarters):
        self.quarters = quarters
        self.group = 4 // quarters
        self.rows = 8 * quarters * self.group
        self.blocks = HALF // self.group

    def levels(self, count):
        return (count + 15) // 16 * 16

    def coded(self, count):
        return count * self.rows + self.levels(count)


def at_block(plan, index):
    return pl.ds(pl.multiple_of(index * plan.rows, 16), plan.rows)


def level_rows(plan, count):
    return slice(count * plan.rows, plan.coded(count))


def read_scales(ref, lead, plan, count, scale_ref):
    level = ref[(*lead, level_rows(plan, count), slice(None))].astype(jnp.int32).astype(F32)
    scale_ref[: plan.levels(count), :] = jnp.exp2(level * (1.0 / STEPS)) * (1.0 / TOP)


def get(ref, lead, plan, index, scale_ref):
    codes = ref[(*lead, at_block(plan, index), slice(None))]
    return codes.astype(jnp.int32).astype(F32) * scale_ref[pl.ds(index, 1), :]


def put(ref, plan, index, block, level_ref):
    codes, level = encode(block)
    ref[at_block(plan, index), :] = codes
    level_ref[pl.ds(index, 1), :] = level


def put_levels(ref, plan, count, level_ref):
    level = level_ref[: plan.levels(count), :]
    ref[level_rows(plan, count), :] = level.astype(jnp.int32).astype(S16)


def send_body(aux_ref, row_ref, col_ref, ext_ref, tiles_ref, out_ref, count_ref, *, layer_blocks):
    out_ref[...] = jnp.zeros(out_ref.shape, BF16)

    @pl.loop(0, OWNERS)
    def _(i):
        count_ref[i] = 0

    lane = lax.broadcasted_iota(jnp.int32, (QUARTER, BS), 1)
    meta_lane = lax.broadcasted_iota(jnp.int32, (8, BS), 1)

    @pl.loop(0, tiles_ref.shape[0])
    def _(i):
        col = col_ref[i]
        layer_of = col // layer_blocks
        kept = col - layer_of * layer_blocks
        owner = (row_ref[i] % 4 * 4 + row_ref[i] // 4) * LAYERS + layer_of
        used = count_ref[owner]
        count_ref[owner] = used + 1
        tile = jnp.where(lane < ext_ref[i], tiles_ref[i].astype(F32), 0.0)
        out_ref[owner, pl.ds(pl.multiple_of(used * QUARTER, QUARTER), QUARTER), :] = tile.astype(BF16)
        old = out_ref[owner, CAP * QUARTER :, :].astype(F32)
        new = jnp.where(meta_lane == used * 2, aux_ref[i].astype(F32), old)
        new = jnp.where(meta_lane == used * 2 + 1, kept.astype(F32), new)
        out_ref[owner, CAP * QUARTER :, :] = new.astype(BF16)


def build_send(tiles, block_aux, block_row, block_col, extents, layer_blocks):
    return pl.pallas_call(
        functools.partial(send_body, layer_blocks=layer_blocks),
        in_specs=[SMEM] * 4 + [VMEM],
        out_specs=VMEM,
        out_shape=jax.ShapeDtypeStruct((OWNERS, CAP * QUARTER + 8, BS), BF16),
        scratch_shapes=[pltpu.SMEM((OWNERS,), jnp.int32)],
        compiler_params=params(8),
        name="build_send",
    )(block_aux, block_row, block_col, extents, tiles)


def split_pieces(place_ref, plan, rows_of, keep_ref, send_refs, level_ref):
    bit_a = place_ref[1]
    bit_b = place_ref[2]

    def piece(a, b):
        return jnp.where(b == 0, a, 3 - a)

    for h, send_ref in enumerate(send_refs):
        kept = [piece(bit_a, o) if h == 0 else piece(o, bit_b) for o in range(2)]
        sent = [piece(1 - bit_a, o) if h == 0 else piece(o, 1 - bit_b) for o in range(2)]

        @pl.loop(0, plan.blocks)
        def _(block):
            first = h * HALF + block * plan.group
            for other in range(2):
                keep_ref[h, other, block] = rows_of(first, kept[other])
                put(send_ref, plan, other * plan.blocks + block, rows_of(first, sent[other]), level_ref)

        put_levels(send_ref, plan, 2 * plan.blocks, level_ref)


def virt_near_body(meta_ref, own_ref, prev_ref, next_ref, green_ref, acc_ref):
    acc_ref[...] = jnp.zeros(acc_ref.shape, F32)

    @pl.loop(0, OWNERS // 2)
    def _(step):
        for source in (step * 2, step * 2 + 1):
            for slot in range(CAP):
                span = slice(slot * QUARTER, (slot + 1) * QUARTER)
                tile = jnp.concatenate([ref[source, span, :] for ref in (own_ref, prev_ref, next_ref)], axis=0)
                aux = meta_ref[source, 2 * slot]
                kept = meta_ref[source, 2 * slot + 1]
                acc_ref[aux] += jnp.dot(tile, green_ref[kept], preferred_element_type=F32)


def virt_far_body(
    meta_ref, place_ref, far_a_ref, far_b_ref, green_ref, near_ref, keep_ref, send0_ref, send1_ref, acc_ref, level_ref, *, plan
):
    acc_ref[...] = jnp.zeros(acc_ref.shape, F32)
    half = OWNERS // 2
    for part, far_ref in enumerate((far_a_ref, far_b_ref)):

        @pl.loop(0, half // 2)
        def _(step):
            for local in (step * 2, step * 2 + 1):
                source = part * half + local
                for slot in range(CAP):
                    tile = far_ref[local, slot * QUARTER : (slot + 1) * QUARTER, :]
                    aux = meta_ref[source, 2 * slot]
                    kept = meta_ref[source, 2 * slot + 1]
                    acc_ref[aux] += jnp.dot(tile, green_ref[kept], preferred_element_type=F32)

    def rows_of(first, piece):
        at = [pl.multiple_of(quarter * QUARTER + piece * 8, 8) for quarter in range(3)]
        parts = [near_ref[first, pl.ds(row, 8), :] for row in at]
        return jnp.concatenate(parts + [acc_ref[first, pl.ds(at[0], 8), :]], axis=0)

    split_pieces(place_ref, plan, rows_of, keep_ref, (send0_ref, send1_ref), level_ref)


def occ_body(
    meta_ref, place_ref, own_ref, prev_ref, next_ref, far_a_ref, far_b_ref, green_ref, *rest, plan
):
    keep_ref, send0_ref, send1_ref, acc_ref, tile_ref, level_ref = rest
    acc_ref[...] = jnp.zeros(acc_ref.shape, F32)
    row_place = place_ref[0]
    rows = [pl.multiple_of(((row_place + d) % ROWS) * QUARTER, QUARTER) for d in (0, ROWS - 1, 1, 2)]
    half = OWNERS // 2
    for part, far_ref in enumerate((far_a_ref, far_b_ref)):

        @pl.loop(0, half // 2)
        def _(step):
            visits = [(j, slot) for j in range(2) for slot in range(CAP)]
            for j, slot in visits:
                local = step * 2 + j
                source = part * half + local
                span = slice(slot * QUARTER, (slot + 1) * QUARTER)
                for ref, row in zip((own_ref, prev_ref, next_ref), rows):
                    tile_ref[CAP * j + slot, pl.ds(row, QUARTER), :] = ref[source, span, :]
                tile_ref[CAP * j + slot, pl.ds(rows[3], QUARTER), :] = far_ref[local, span, :]
            for j, slot in visits:
                source = part * half + step * 2 + j
                aux = meta_ref[source, 2 * slot]
                kept = meta_ref[source, 2 * slot + 1]
                term = lax.dot_general(
                    green_ref[kept], tile_ref[CAP * j + slot], (((1,), (1,)), ((), ())), preferred_element_type=F32
                )
                for low in range(4):
                    lanes = slice(low * BS, (low + 1) * BS)
                    acc_ref[aux, :, lanes] += term[low * BS : (low + 1) * BS, :]

    def rows_of(first, piece):
        at = [pl.multiple_of(quarter * QUARTER + piece * 8, 8) for quarter in range(4)]
        return jnp.concatenate([acc_ref[first, pl.ds(row, 8), :] for row in at], axis=0)

    split_pieces(place_ref, plan, rows_of, keep_ref, (send0_ref, send1_ref), level_ref)


VMEM = pl.BlockSpec(memory_space=pltpu.VMEM)
SMEM = pl.BlockSpec(memory_space=pltpu.SMEM)
NEAR = (NP, 3 * QUARTER, WIDE)


def step_shapes(plan):
    code = jax.ShapeDtypeStruct((plan.coded(2 * plan.blocks), WIDE), S16)
    return [jax.ShapeDtypeStruct((2, 2, plan.blocks, plan.rows, WIDE), F32), code, code]


def level_scratch(plan):
    return pltpu.VMEM((plan.levels(2 * plan.blocks), WIDE), F32)


def contract_virt_near(meta, quarters, green):
    return pl.pallas_call(
        virt_near_body,
        in_specs=[SMEM] + [VMEM] * 4,
        out_specs=VMEM,
        out_shape=jax.ShapeDtypeStruct(NEAR, F32),
        compiler_params=params(20),
        name="virt_near",
    )(meta, *quarters, green)


def contract_virt_far(meta, place, fars, green, near, plan):
    return pl.pallas_call(
        functools.partial(virt_far_body, plan=plan),
        in_specs=[SMEM] * 2 + [VMEM] * 4,
        out_specs=[VMEM] * 3,
        out_shape=step_shapes(plan),
        scratch_shapes=[pltpu.VMEM((NP, QUARTER, WIDE), F32), level_scratch(plan)],
        compiler_params=params(24),
        name="virt_far",
    )(meta, place, *fars, green, near)


def contract_occ(meta, place, quarters, green, plan):
    return pl.pallas_call(
        functools.partial(occ_body, plan=plan),
        in_specs=[SMEM] * 2 + [VMEM] * 6,
        out_specs=[VMEM] * 3,
        out_shape=step_shapes(plan),
        scratch_shapes=[pltpu.VMEM((NP, BS, WIDE), F32), pltpu.VMEM((2 * CAP, BS, BS), BF16), level_scratch(plan)],
        compiler_params=params(28),
        name="contract_occ",
    )(meta, place, *quarters, green)


def halve_body(place_ref, keep_ref, got0_ref, got1_ref, left_ref, send0_ref, send1_ref, level_ref, scale_ref, *, plan):
    for h, got_ref, send_ref in ((0, got0_ref, send0_ref), (1, got1_ref, send1_ref)):
        mine = place_ref[2 - h]
        away = 1 - mine
        read_scales(got_ref, (), plan, 2 * plan.blocks, scale_ref)

        @pl.loop(0, plan.blocks)
        def _(b):
            left_ref[h, b] = keep_ref[h, mine, b] + get(got_ref, (), plan, mine * plan.blocks + b, scale_ref)
            total = keep_ref[h, away, b] + get(got_ref, (), plan, away * plan.blocks + b, scale_ref)
            put(send_ref, plan, b, total, level_ref)

        put_levels(send_ref, plan, plan.blocks, level_ref)


def halve(place, keep, got0, got1, plan, name):
    code = jax.ShapeDtypeStruct((plan.coded(plan.blocks), WIDE), S16)
    return pl.pallas_call(
        functools.partial(halve_body, plan=plan),
        in_specs=[SMEM] + [VMEM] * 3,
        out_specs=[VMEM] * 3,
        out_shape=[jax.ShapeDtypeStruct((2, plan.blocks, plan.rows, WIDE), F32), code, code],
        scratch_shapes=[level_scratch(plan), level_scratch(plan)],
        compiler_params=params(16),
        name=name,
    )(place, keep, got0, got1)


def finish_body(left_ref, got0_ref, got1_ref, out_ref, level_ref, scale_ref, *, plan, split):
    count = 2 * plan.blocks
    for h, got_ref in ((0, got0_ref), (1, got1_ref)):
        read_scales(got_ref, (), plan, plan.blocks, scale_ref)

        @pl.loop(0, plan.blocks)
        def _(b):
            total = left_ref[h, b] + get(got_ref, (), plan, b, scale_ref)
            index = h * plan.blocks + b
            if split:
                codes, level = encode(total)
                for low in range(4):
                    out_ref[low, at_block(plan, index), :] = codes[:, low * BS : (low + 1) * BS]
                level_ref[pl.ds(index, 1), :] = level
            else:
                put(out_ref, plan, index, total, level_ref)

    if split:
        levels = level_ref[...].astype(jnp.int32).astype(S16)
        for low in range(4):
            out_ref[low, level_rows(plan, count), :] = levels[:, low * BS : (low + 1) * BS]
    else:
        put_levels(out_ref, plan, count, level_ref)


def finish(left, got0, got1, plan, split, name):
    rows = plan.coded(2 * plan.blocks)
    shape = (4, rows, BS) if split else (rows, WIDE)
    return pl.pallas_call(
        functools.partial(finish_body, plan=plan, split=split),
        in_specs=[VMEM] * 3,
        out_specs=VMEM,
        out_shape=jax.ShapeDtypeStruct(shape, S16),
        scratch_shapes=[level_scratch(plan), level_scratch(plan)],
        compiler_params=params(12),
        name=name,
    )(left, got0, got1)


def pair_body(place_ref, own_ref, one_ref, two_ref, three_ref, virt_ref, out_ref, occ_ref, vir_ref, wide_ref, thin_ref, *, plan):
    here = place_ref[0]
    high = place_ref[1]
    count = 2 * plan.blocks

    at = [((high + shift) % 4) * 8 for shift in (0, ROWS - 1, 1, 2)]
    read_scales(virt_ref, (), plan, count, wide_ref)

    @pl.loop(0, NP)
    def _(q):
        values = get(virt_ref, (), plan, q, wide_ref)
        for quarter in range(4):
            for low in range(4):
                to = pl.ds(pl.multiple_of(low * QUARTER + at[quarter], 8), 8)
                vir_ref[q, to, :] = values[quarter * 8 : (quarter + 1) * 8, low * BS : (low + 1) * BS]

    for d, ref in enumerate((own_ref, one_ref, two_ref, three_ref)):
        source = (here + 4 - d) % 4
        lead = (here,) if d == 0 else (0,)
        read_scales(ref, lead, plan, count, thin_ref)
        rows = pl.ds(pl.multiple_of(source * QUARTER, QUARTER), QUARTER)

        @pl.loop(0, NP)
        def _(p):
            occ_ref[p, rows, :] = get(ref, lead, plan, p, thin_ref)

    @pl.loop(0, NP)
    def _(p):
        occ = occ_ref[p]
        for q in range(NP):
            out_ref[p, q : q + 1, :] = jnp.sum(occ * vir_ref[q], axis=0, keepdims=True)


def pair(place, own, others, virt, plan):
    levels = plan.levels(2 * plan.blocks)
    return pl.pallas_call(
        functools.partial(pair_body, plan=plan),
        in_specs=[SMEM] + [VMEM] * 5,
        out_specs=VMEM,
        out_shape=jax.ShapeDtypeStruct((NP, NP, BS), F32),
        scratch_shapes=[
            pltpu.VMEM((NP, BS, BS), F32),
            pltpu.VMEM((NP, BS, BS), F32),
            pltpu.VMEM((levels, WIDE), F32),
            pltpu.VMEM((levels, BS), F32),
        ],
        compiler_params=params(16),
        name="pair",
    )(place, own, *others, virt)


def rotate(size, step):
    return [(i, (i + step) % size) for i in range(size)]


def rotate_low(step):
    return [(c, c - c % 4 + (c + step) % 4) for c in range(COLS)]


def rotate_high(step):
    return [(c, (c + 4 * step) % COLS) for c in range(COLS)]


PAIRS_A = [(0, 1), (1, 0), (2, 3), (3, 2)]
PAIRS_B = [(0, 3), (3, 0), (1, 2), (2, 1)]


def index_of(row, col, layer):
    return (row * COLS + col) * LAYERS + layer


SWAP = [
    (index_of(r, c, l), index_of(c % 4, c // 4 * 4 + r, l))
    for r in range(ROWS)
    for c in range(COLS)
    for l in range(LAYERS)
]


def tree_sum(values):
    rounds = (
        ("layer", [rotate(LAYERS, d) for d in (1, 2, 3)]),
        ("col", [rotate_low(d) for d in (1, 2, 3)]),
        ("row", [rotate(ROWS, d) for d in (1, 2, 3)]),
        ("col", [rotate_high(d) for d in (1, 2, 3)]),
    )
    for axis, perms in rounds:
        one, two, three = [lax.ppermute(values, axis, perm) for perm in perms]
        values = (values + two) + (one + three)
    return values


def layer_swap(send0, send1, perms):
    return lax.ppermute(send0, "layer", perms[0]), lax.ppermute(send1, "layer", perms[1])


FIRST = (PAIRS_A, PAIRS_B)
SECOND = (PAIRS_B, PAIRS_A)


def after(*values):
    return lax.optimization_barrier(values)


def on_device(blocks, block_aux, block_row, block_col, extents, occ_green, virt_green):
    layer_blocks = occ_green.shape[0] // BS
    row_place = lax.axis_index("row").astype(jnp.int32)
    col_place = lax.axis_index("col").astype(jnp.int32)
    layer_place = lax.axis_index("layer").astype(jnp.int32)
    bit_a = ((layer_place == 1) | (layer_place == 2)).astype(jnp.int32)
    bit_b = layer_place // 2
    place = jnp.stack([row_place, bit_a, bit_b])
    plan = Plan(4)

    tiles = lax.dynamic_slice_in_dim(blocks, row_place * QUARTER, QUARTER, 1)
    send = build_send(tiles, block_aux, block_row, block_col, extents, layer_blocks)
    own = lax.all_to_all(send, ("col", "layer"), 0, 0, tiled=True)
    meta = own[:, CAP * QUARTER, : 2 * CAP].astype(jnp.int32)
    virt_blocks = virt_green.reshape(layer_blocks, BS, WIDE)
    occ_blocks = occ_green.reshape(layer_blocks, BS, WIDE).transpose(0, 2, 1)

    half = OWNERS // 2
    prev = lax.ppermute(own, "row", rotate(ROWS, 1))
    nxt = lax.ppermute(own, "row", rotate(ROWS, -1))
    far_a = lax.ppermute(prev[:half], "row", rotate(ROWS, 1))
    far_b = lax.ppermute(nxt[half:], "row", rotate(ROWS, -1))

    prev, nxt, occ_blocks = after(prev, nxt, occ_blocks)
    v_near = contract_virt_near(meta, (own, prev, nxt), virt_blocks)
    v_keep, v0, v1 = contract_virt_far(meta, place, (far_a, far_b), virt_blocks, v_near, plan)
    v_got = layer_swap(v0, v1, FIRST)
    occ_blocks, v_keep = after(occ_blocks, v_keep)
    o_keep, o0, o1 = contract_occ(meta, place, (own, prev, nxt, far_a, far_b), occ_blocks, plan)
    o_got = layer_swap(o0, o1, FIRST)
    v_keep, o_keep = after(v_keep, o_keep)
    v_left, v0, v1 = halve(place, v_keep, *v_got, plan, "halve_virt")
    v_got = layer_swap(v0, v1, SECOND)
    virt = finish(v_left, *v_got, plan, False, "finish_virt")
    virt, o_keep = after(virt, o_keep)
    virt = lax.ppermute(virt, ALL, SWAP)
    o_left, o0, o1 = halve(place, o_keep, *o_got, plan, "halve_occ")
    o_got = layer_swap(o0, o1, SECOND)
    occ = finish(o_left, *o_got, plan, True, "finish_occ")

    low = col_place // 4
    others = []
    for d in (1, 2, 3):
        part = lax.dynamic_slice_in_dim(occ, (low + d) % 4, 1, 0)
        others.append(lax.ppermute(part, "col", rotate_high(d)))
    here = jnp.stack([low, col_place % 4])
    partial = pair(here, occ, others, virt, plan)
    return tree_sum(jnp.sum(partial, axis=-1))


def solution(mesh):
    in_specs = (
        P(("col", "layer"), None, None),
        P(("col", "layer")),
        P(("col", "layer")),
        P(("col", "layer")),
        P(("col", "layer")),
        P("layer", "row"),
        P("layer", "row"),
    )
    return jax.shard_map(on_device, mesh=mesh, in_specs=in_specs, out_specs=P(), check_vma=False)
```

```python
import functools

import jax
import jax.numpy as jnp
from jax import lax
from jax.experimental import pallas as pl
from jax.experimental.pallas import tpu as pltpu
from jax.sharding import PartitionSpec as P

NP = 24
ROWS = 4
COLS = 16
LAYERS = 4
CAP = 2
OWNERS = COLS * LAYERS
BS = 128
QUARTER = BS // ROWS
WIDE = 512
HALF = NP // 2
TOP = 32700.0
STEPS = 64.0
ALL = ("row", "col", "layer")
F32 = jnp.float32
BF16 = jnp.bfloat16
S16 = jnp.int16


def params(mib):
    return pltpu.CompilerParams(vmem_limit_bytes=mib * 2**20)


def encode(block):
    peak = jnp.max(jnp.abs(block), axis=0, keepdims=True)
    level = jnp.ceil(jnp.log2(jnp.maximum(peak, 1e-30)) * STEPS)
    scaled = block * (jnp.exp2(level * (-1.0 / STEPS)) * TOP)
    return jnp.round(scaled).astype(jnp.int32).astype(S16), level


def decode(codes, level):
    return codes.astype(jnp.int32).astype(F32) * (jnp.exp2(level * (1.0 / STEPS)) * (1.0 / TOP))


class Plan:
    def __init__(self, quarters):
        self.quarters = quarters
        self.group = 4 // quarters
        self.rows = 8 * quarters * self.group
        self.blocks = HALF // self.group

    def levels(self, count):
        return (count + 15) // 16 * 16

    def coded(self, count):
        return count * self.rows + self.levels(count)


def at_block(plan, index):
    return pl.ds(pl.multiple_of(index * plan.rows, 16), plan.rows)


def level_rows(plan, count):
    return slice(count * plan.rows, plan.coded(count))


def read_scales(ref, lead, plan, count, scale_ref):
    level = ref[(*lead, level_rows(plan, count), slice(None))].astype(jnp.int32).astype(F32)
    scale_ref[: plan.levels(count), :] = jnp.exp2(level * (1.0 / STEPS)) * (1.0 / TOP)


def get(ref, lead, plan, index, scale_ref):
    codes = ref[(*lead, at_block(plan, index), slice(None))]
    return codes.astype(jnp.int32).astype(F32) * scale_ref[pl.ds(index, 1), :]


def put(ref, plan, index, block, level_ref):
    codes, level = encode(block)
    ref[at_block(plan, index), :] = codes
    level_ref[pl.ds(index, 1), :] = level


def put_levels(ref, plan, count, level_ref):
    level = level_ref[: plan.levels(count), :]
    ref[level_rows(plan, count), :] = level.astype(jnp.int32).astype(S16)


def send_body(aux_ref, row_ref, col_ref, ext_ref, tiles_ref, out_ref, count_ref, *, layer_blocks):
    out_ref[...] = jnp.zeros(out_ref.shape, BF16)

    @pl.loop(0, OWNERS)
    def _(i):
        count_ref[i] = 0

    lane = lax.broadcasted_iota(jnp.int32, (QUARTER, BS), 1)
    meta_lane = lax.broadcasted_iota(jnp.int32, (8, BS), 1)

    @pl.loop(0, tiles_ref.shape[0])
    def _(i):
        col = col_ref[i]
        layer_of = col // layer_blocks
        kept = col - layer_of * layer_blocks
        owner = (row_ref[i] % 4 * 4 + row_ref[i] // 4) * LAYERS + layer_of
        used = count_ref[owner]
        count_ref[owner] = used + 1
        tile = jnp.where(lane < ext_ref[i], tiles_ref[i].astype(F32), 0.0)
        out_ref[owner, pl.ds(pl.multiple_of(used * QUARTER, QUARTER), QUARTER), :] = tile.astype(BF16)
        old = out_ref[owner, CAP * QUARTER :, :].astype(F32)
        new = jnp.where(meta_lane == used * 2, aux_ref[i].astype(F32), old)
        new = jnp.where(meta_lane == used * 2 + 1, kept.astype(F32), new)
        out_ref[owner, CAP * QUARTER :, :] = new.astype(BF16)


def build_send(tiles, block_aux, block_row, block_col, extents, layer_blocks):
    return pl.pallas_call(
        functools.partial(send_body, layer_blocks=layer_blocks),
        in_specs=[SMEM] * 4 + [VMEM],
        out_specs=VMEM,
        out_shape=jax.ShapeDtypeStruct((OWNERS, CAP * QUARTER + 8, BS), BF16),
        scratch_shapes=[pltpu.SMEM((OWNERS,), jnp.int32)],
        compiler_params=params(8),
        name="build_send",
    )(block_aux, block_row, block_col, extents, tiles)


def split_pieces(place_ref, plan, rows_of, keep_ref, send_refs, level_ref):
    bit_a = place_ref[1]
    bit_b = place_ref[2]

    def piece(a, b):
        return jnp.where(b == 0, a, 3 - a)

    for h, send_ref in enumerate(send_refs):
        kept = [piece(bit_a, o) if h == 0 else piece(o, bit_b) for o in range(2)]
        sent = [piece(1 - bit_a, o) if h == 0 else piece(o, 1 - bit_b) for o in range(2)]

        @pl.loop(0, plan.blocks)
        def _(block):
            first = h * HALF + block * plan.group
            for other in range(2):
                keep_ref[h, other, block] = rows_of(first, kept[other])
                put(send_ref, plan, other * plan.blocks + block, rows_of(first, sent[other]), level_ref)

        put_levels(send_ref, plan, 2 * plan.blocks, level_ref)


def virt_body(meta_ref, place_ref, *rest, plan):
    sources, (keep_ref, send0_ref, send1_ref) = rest[:6], rest[6:9]
    refs, (acc_ref, level_ref, sems) = rest[9:15], rest[15:]
    loads = [pltpu.make_async_copy(src, dst, sems.at[i]) for i, (src, dst) in enumerate(zip(sources, refs))]
    for load in loads:
        load.start()
    acc_ref[...] = jnp.zeros(acc_ref.shape, F32)
    for load in loads:
        load.wait()
    green_ref = refs[5]
    half = OWNERS // 2
    for part in range(2):

        @pl.loop(0, half // 2)
        def _(step):
            for local in (step * 2, step * 2 + 1):
                source = part * half + local
                for slot in range(CAP):
                    span = slice(slot * QUARTER, (slot + 1) * QUARTER)
                    parts = [ref[source, span, :] for ref in refs[:3]] + [refs[3 + part][local, span, :]]
                    aux = meta_ref[source, 2 * slot]
                    kept = meta_ref[source, 2 * slot + 1]
                    tile = jnp.concatenate(parts, axis=0)
                    acc_ref[aux] += jnp.dot(tile, green_ref[kept], preferred_element_type=F32)

    split_pieces(place_ref, plan, piece_rows(acc_ref), keep_ref, (send0_ref, send1_ref), level_ref)


def piece_rows(acc_ref):
    def rows_of(first, piece):
        at = [pl.multiple_of(quarter * QUARTER + piece * 8, 8) for quarter in range(4)]
        return jnp.concatenate([acc_ref[first, pl.ds(row, 8), :] for row in at], axis=0)

    return rows_of


def occ_body(
    meta_ref, place_ref, own_ref, prev_ref, next_ref, far_a_ref, far_b_ref, green_ref, *rest, plan
):
    keep_ref, send0_ref, send1_ref, acc_ref, tile_ref, level_ref = rest
    acc_ref[...] = jnp.zeros(acc_ref.shape, F32)
    row_place = place_ref[0]
    rows = [pl.multiple_of(((row_place + d) % ROWS) * QUARTER, QUARTER) for d in (0, ROWS - 1, 1, 2)]
    half = OWNERS // 2
    for part, far_ref in enumerate((far_a_ref, far_b_ref)):

        @pl.loop(0, half // 2)
        def _(step):
            visits = [(j, slot) for j in range(2) for slot in range(CAP)]
            for j, slot in visits:
                local = step * 2 + j
                source = part * half + local
                span = slice(slot * QUARTER, (slot + 1) * QUARTER)
                for ref, row in zip((own_ref, prev_ref, next_ref), rows):
                    tile_ref[CAP * j + slot, pl.ds(row, QUARTER), :] = ref[source, span, :]
                tile_ref[CAP * j + slot, pl.ds(rows[3], QUARTER), :] = far_ref[local, span, :]
            for j, slot in visits:
                source = part * half + step * 2 + j
                aux = meta_ref[source, 2 * slot]
                kept = meta_ref[source, 2 * slot + 1]
                term = lax.dot_general(
                    green_ref[kept], tile_ref[CAP * j + slot], (((1,), (1,)), ((), ())), preferred_element_type=F32
                )
                for low in range(4):
                    lanes = slice(low * BS, (low + 1) * BS)
                    acc_ref[aux, :, lanes] += term[low * BS : (low + 1) * BS, :]

    split_pieces(place_ref, plan, piece_rows(acc_ref), keep_ref, (send0_ref, send1_ref), level_ref)


VMEM = pl.BlockSpec(memory_space=pltpu.VMEM)
SMEM = pl.BlockSpec(memory_space=pltpu.SMEM)
ANY = pl.BlockSpec(memory_space=pl.ANY)


def step_shapes(plan):
    code = jax.ShapeDtypeStruct((plan.coded(2 * plan.blocks), WIDE), S16)
    return [jax.ShapeDtypeStruct((2, 2, plan.blocks, plan.rows, WIDE), F32), code, code]


def level_scratch(plan):
    return pltpu.VMEM((plan.levels(2 * plan.blocks), WIDE), F32)


def contract_virt(meta, place, quarters, green, plan):
    operands = [*quarters, green]
    return pl.pallas_call(
        functools.partial(virt_body, plan=plan),
        in_specs=[SMEM] * 2 + [ANY] * 6,
        out_specs=[VMEM] * 3,
        out_shape=step_shapes(plan),
        scratch_shapes=[pltpu.VMEM(x.shape, x.dtype) for x in operands]
        + [pltpu.VMEM((NP, BS, WIDE), F32), level_scratch(plan), pltpu.SemaphoreType.DMA((6,))],
        compiler_params=params(55),
        name="contract_virt",
    )(meta, place, *operands)


def contract_occ(meta, place, quarters, green, plan):
    return pl.pallas_call(
        functools.partial(occ_body, plan=plan),
        in_specs=[SMEM] * 2 + [VMEM] * 6,
        out_specs=[VMEM] * 3,
        out_shape=step_shapes(plan),
        scratch_shapes=[pltpu.VMEM((NP, BS, WIDE), F32), pltpu.VMEM((2 * CAP, BS, BS), BF16), level_scratch(plan)],
        compiler_params=params(28),
        name="contract_occ",
    )(meta, place, *quarters, green)


def halve_body(place_ref, keep_ref, got0_ref, got1_ref, left_ref, send0_ref, send1_ref, level_ref, scale_ref, *, plan):
    for h, got_ref, send_ref in ((0, got0_ref, send0_ref), (1, got1_ref, send1_ref)):
        mine = place_ref[2 - h]
        away = 1 - mine
        read_scales(got_ref, (), plan, 2 * plan.blocks, scale_ref)

        @pl.loop(0, plan.blocks)
        def _(b):
            left_ref[h, b] = keep_ref[h, mine, b] + get(got_ref, (), plan, mine * plan.blocks + b, scale_ref)
            total = keep_ref[h, away, b] + get(got_ref, (), plan, away * plan.blocks + b, scale_ref)
            put(send_ref, plan, b, total, level_ref)

        put_levels(send_ref, plan, plan.blocks, level_ref)


def halve(place, keep, got0, got1, plan, name):
    code = jax.ShapeDtypeStruct((plan.coded(plan.blocks), WIDE), S16)
    return pl.pallas_call(
        functools.partial(halve_body, plan=plan),
        in_specs=[SMEM] + [VMEM] * 3,
        out_specs=[VMEM] * 3,
        out_shape=[jax.ShapeDtypeStruct((2, plan.blocks, plan.rows, WIDE), F32), code, code],
        scratch_shapes=[level_scratch(plan), level_scratch(plan)],
        compiler_params=params(16),
        name=name,
    )(place, keep, got0, got1)


def finish_body(left_ref, got0_ref, got1_ref, out_ref, level_ref, scale_ref, *, plan, split):
    count = 2 * plan.blocks
    for h, got_ref in ((0, got0_ref), (1, got1_ref)):
        read_scales(got_ref, (), plan, plan.blocks, scale_ref)

        @pl.loop(0, plan.blocks)
        def _(b):
            total = left_ref[h, b] + get(got_ref, (), plan, b, scale_ref)
            index = h * plan.blocks + b
            if split:
                codes, level = encode(total)
                for low in range(4):
                    out_ref[low, at_block(plan, index), :] = codes[:, low * BS : (low + 1) * BS]
                level_ref[pl.ds(index, 1), :] = level
            else:
                put(out_ref, plan, index, total, level_ref)

    if split:
        levels = level_ref[...].astype(jnp.int32).astype(S16)
        for low in range(4):
            out_ref[low, level_rows(plan, count), :] = levels[:, low * BS : (low + 1) * BS]
    else:
        put_levels(out_ref, plan, count, level_ref)


def finish(left, got0, got1, plan, split, name):
    rows = plan.coded(2 * plan.blocks)
    shape = (4, rows, BS) if split else (rows, WIDE)
    return pl.pallas_call(
        functools.partial(finish_body, plan=plan, split=split),
        in_specs=[VMEM] * 3,
        out_specs=VMEM,
        out_shape=jax.ShapeDtypeStruct(shape, S16),
        scratch_shapes=[level_scratch(plan), level_scratch(plan)],
        compiler_params=params(12),
        name=name,
    )(left, got0, got1)


def pair_body(place_ref, own_ref, one_ref, two_ref, three_ref, virt_ref, out_ref, occ_ref, vir_ref, wide_ref, thin_ref, *, plan):
    here = place_ref[0]
    high = place_ref[1]
    count = 2 * plan.blocks

    at = [((high + shift) % 4) * 8 for shift in (0, ROWS - 1, 1, 2)]
    read_scales(virt_ref, (), plan, count, wide_ref)

    @pl.loop(0, NP)
    def _(q):
        values = get(virt_ref, (), plan, q, wide_ref)
        for quarter in range(4):
            for low in range(4):
                to = pl.ds(pl.multiple_of(low * QUARTER + at[quarter], 8), 8)
                vir_ref[q, to, :] = values[quarter * 8 : (quarter + 1) * 8, low * BS : (low + 1) * BS]

    for d, ref in enumerate((own_ref, one_ref, two_ref, three_ref)):
        source = (here + 4 - d) % 4
        lead = (here,) if d == 0 else (0,)
        read_scales(ref, lead, plan, count, thin_ref)
        rows = pl.ds(pl.multiple_of(source * QUARTER, QUARTER), QUARTER)

        @pl.loop(0, NP)
        def _(p):
            occ_ref[p, rows, :] = get(ref, lead, plan, p, thin_ref)

    @pl.loop(0, NP)
    def _(p):
        occ = occ_ref[p]
        for q in range(NP):
            out_ref[p, q : q + 1, :] = jnp.sum(occ * vir_ref[q], axis=0, keepdims=True)


def pair(place, own, others, virt, plan):
    levels = plan.levels(2 * plan.blocks)
    return pl.pallas_call(
        functools.partial(pair_body, plan=plan),
        in_specs=[SMEM] + [VMEM] * 5,
        out_specs=VMEM,
        out_shape=jax.ShapeDtypeStruct((NP, NP, BS), F32),
        scratch_shapes=[
            pltpu.VMEM((NP, BS, BS), F32),
            pltpu.VMEM((NP, BS, BS), F32),
            pltpu.VMEM((levels, WIDE), F32),
            pltpu.VMEM((levels, BS), F32),
        ],
        compiler_params=params(16),
        name="pair",
    )(place, own, *others, virt)


def rotate(size, step):
    return [(i, (i + step) % size) for i in range(size)]


def rotate_low(step):
    return [(c, c - c % 4 + (c + step) % 4) for c in range(COLS)]


def rotate_high(step):
    return [(c, (c + 4 * step) % COLS) for c in range(COLS)]


PAIRS_A = [(0, 1), (1, 0), (2, 3), (3, 2)]
PAIRS_B = [(0, 3), (3, 0), (1, 2), (2, 1)]


def index_of(row, col, layer):
    return (row * COLS + col) * LAYERS + layer


SWAP = [
    (index_of(r, c, l), index_of(c % 4, c // 4 * 4 + r, l))
    for r in range(ROWS)
    for c in range(COLS)
    for l in range(LAYERS)
]


def tree_sum(values):
    rounds = (
        ("layer", [rotate(LAYERS, d) for d in (1, 2, 3)]),
        ("col", [rotate_low(d) for d in (1, 2, 3)]),
        ("row", [rotate(ROWS, d) for d in (1, 2, 3)]),
        ("col", [rotate_high(d) for d in (1, 2, 3)]),
    )
    for axis, perms in rounds:
        one, two, three = [lax.ppermute(values, axis, perm) for perm in perms]
        values = (values + two) + (one + three)
    return values


def layer_swap(send0, send1, perms):
    return lax.ppermute(send0, "layer", perms[0]), lax.ppermute(send1, "layer", perms[1])


FIRST = (PAIRS_A, PAIRS_B)
SECOND = (PAIRS_B, PAIRS_A)


def after(*values):
    return lax.optimization_barrier(values)


def on_device(blocks, block_aux, block_row, block_col, extents, occ_green, virt_green):
    layer_blocks = occ_green.shape[0] // BS
    row_place = lax.axis_index("row").astype(jnp.int32)
    col_place = lax.axis_index("col").astype(jnp.int32)
    layer_place = lax.axis_index("layer").astype(jnp.int32)
    bit_a = ((layer_place == 1) | (layer_place == 2)).astype(jnp.int32)
    bit_b = layer_place // 2
    place = jnp.stack([row_place, bit_a, bit_b])
    plan = Plan(4)

    tiles = lax.dynamic_slice_in_dim(blocks, row_place * QUARTER, QUARTER, 1)
    send = build_send(tiles, block_aux, block_row, block_col, extents, layer_blocks)
    own = lax.all_to_all(send, ("col", "layer"), 0, 0, tiled=True)
    meta = own[:, CAP * QUARTER, : 2 * CAP].astype(jnp.int32)
    virt_blocks = virt_green.reshape(layer_blocks, BS, WIDE)
    occ_blocks = occ_green.reshape(layer_blocks, BS, WIDE).transpose(0, 2, 1)

    half = OWNERS // 2
    prev = lax.ppermute(own, "row", rotate(ROWS, 1))
    nxt = lax.ppermute(own, "row", rotate(ROWS, -1))
    prev, nxt, occ_blocks = after(prev, nxt, occ_blocks)
    far_a = lax.ppermute(prev[:half], "row", rotate(ROWS, 1))
    far_b = lax.ppermute(nxt[half:], "row", rotate(ROWS, -1))
    quarters = (own, prev, nxt, far_a, far_b)

    v_keep, v0, v1 = contract_virt(meta, place, quarters, virt_blocks, plan)
    v_got = layer_swap(v0, v1, FIRST)
    occ_blocks, v_keep = after(occ_blocks, v_keep)
    o_keep, o0, o1 = contract_occ(meta, place, quarters, occ_blocks, plan)
    o_got = layer_swap(o0, o1, FIRST)
    v_keep, o_keep = after(v_keep, o_keep)
    v_left, v0, v1 = halve(place, v_keep, *v_got, plan, "halve_virt")
    v0, v1, *o_got = after(v0, v1, *o_got)
    v_got = layer_swap(v0, v1, SECOND)
    o_left, o0, o1 = halve(place, o_keep, *o_got, plan, "halve_occ")
    o_left, *v_got = after(o_left, *v_got)
    virt = finish(v_left, *v_got, plan, False, "finish_virt")
    virt = lax.ppermute(virt, ALL, SWAP)
    o_got = layer_swap(o0, o1, SECOND)
    occ = finish(o_left, *o_got, plan, True, "finish_occ")

    low = col_place // 4
    others = []
    for d in (1, 2, 3):
        part = lax.dynamic_slice_in_dim(occ, (low + d) % 4, 1, 0)
        others.append(lax.ppermute(part, "col", rotate_high(d)))
    here = jnp.stack([low, col_place % 4])
    partial = pair(here, occ, others, virt, plan)
    return tree_sum(jnp.sum(partial, axis=-1))


def solution(mesh):
    in_specs = (
        P(("col", "layer"), None, None),
        P(("col", "layer")),
        P(("col", "layer")),
        P(("col", "layer")),
        P(("col", "layer")),
        P("layer", "row"),
        P("layer", "row"),
    )
    return jax.shard_map(on_device, mesh=mesh, in_specs=in_specs, out_specs=P(), check_vma=False)
```

```python
import functools

import jax
import jax.numpy as jnp
from jax import lax
from jax.experimental import pallas as pl
from jax.experimental.pallas import tpu as pltpu
from jax.sharding import PartitionSpec as P

NP = 24
ROWS = 4
COLS = 16
LAYERS = 4
CAP = 2
OWNERS = COLS * LAYERS
BS = 128
QUARTER = BS // ROWS
WIDE = 512
HALF = NP // 2
TOP = 32700.0
STEPS = 64.0
ALL = ("row", "col", "layer")
F32 = jnp.float32
BF16 = jnp.bfloat16
S16 = jnp.int16


def params(mib):
    return pltpu.CompilerParams(vmem_limit_bytes=mib * 2**20)


def encode(block):
    peak = jnp.max(jnp.abs(block), axis=0, keepdims=True)
    level = jnp.ceil(jnp.log2(jnp.maximum(peak, 1e-30)) * STEPS)
    scaled = block * (jnp.exp2(level * (-1.0 / STEPS)) * TOP)
    return jnp.round(scaled).astype(jnp.int32).astype(S16), level


def decode(codes, level):
    return codes.astype(jnp.int32).astype(F32) * (jnp.exp2(level * (1.0 / STEPS)) * (1.0 / TOP))


class Plan:
    def __init__(self, quarters):
        self.quarters = quarters
        self.group = 4 // quarters
        self.rows = 8 * quarters * self.group
        self.blocks = HALF // self.group

    def levels(self, count):
        return (count + 15) // 16 * 16

    def coded(self, count):
        return count * self.rows + self.levels(count)


def at_block(plan, index):
    return pl.ds(pl.multiple_of(index * plan.rows, 16), plan.rows)


def level_rows(plan, count):
    return slice(count * plan.rows, plan.coded(count))


def read_scales(ref, lead, plan, count, scale_ref):
    level = ref[(*lead, level_rows(plan, count), slice(None))].astype(jnp.int32).astype(F32)
    scale_ref[: plan.levels(count), :] = jnp.exp2(level * (1.0 / STEPS)) * (1.0 / TOP)


def get(ref, lead, plan, index, scale_ref):
    codes = ref[(*lead, at_block(plan, index), slice(None))]
    return codes.astype(jnp.int32).astype(F32) * scale_ref[pl.ds(index, 1), :]


def put(ref, plan, index, block, level_ref):
    codes, level = encode(block)
    ref[at_block(plan, index), :] = codes
    level_ref[pl.ds(index, 1), :] = level


def put_levels(ref, plan, count, level_ref):
    level = level_ref[: plan.levels(count), :]
    ref[level_rows(plan, count), :] = level.astype(jnp.int32).astype(S16)


def send_body(aux_ref, row_ref, col_ref, ext_ref, tiles_ref, out_ref, count_ref, *, layer_blocks):
    out_ref[...] = jnp.zeros(out_ref.shape, BF16)

    @pl.loop(0, OWNERS)
    def _(i):
        count_ref[i] = 0

    lane = lax.broadcasted_iota(jnp.int32, (QUARTER, BS), 1)
    meta_lane = lax.broadcasted_iota(jnp.int32, (8, BS), 1)

    @pl.loop(0, tiles_ref.shape[0])
    def _(i):
        col = col_ref[i]
        layer_of = col // layer_blocks
        kept = col - layer_of * layer_blocks
        owner = (row_ref[i] % 4 * 4 + row_ref[i] // 4) * LAYERS + layer_of
        used = count_ref[owner]
        count_ref[owner] = used + 1
        tile = jnp.where(lane < ext_ref[i], tiles_ref[i].astype(F32), 0.0)
        out_ref[owner, pl.ds(pl.multiple_of(used * QUARTER, QUARTER), QUARTER), :] = tile.astype(BF16)
        old = out_ref[owner, CAP * QUARTER :, :].astype(F32)
        new = jnp.where(meta_lane == used * 2, aux_ref[i].astype(F32), old)
        new = jnp.where(meta_lane == used * 2 + 1, kept.astype(F32), new)
        out_ref[owner, CAP * QUARTER :, :] = new.astype(BF16)


def build_send(tiles, block_aux, block_row, block_col, extents, layer_blocks):
    return pl.pallas_call(
        functools.partial(send_body, layer_blocks=layer_blocks),
        in_specs=[SMEM] * 4 + [VMEM],
        out_specs=VMEM,
        out_shape=jax.ShapeDtypeStruct((OWNERS, CAP * QUARTER + 8, BS), BF16),
        scratch_shapes=[pltpu.SMEM((OWNERS,), jnp.int32)],
        compiler_params=params(8),
        name="build_send",
    )(block_aux, block_row, block_col, extents, tiles)


def split_pieces(place_ref, plan, rows_of, keep_ref, send_refs, level_ref):
    bit_a = place_ref[1]
    bit_b = place_ref[2]

    def piece(a, b):
        return jnp.where(b == 0, a, 3 - a)

    for h, send_ref in enumerate(send_refs):
        kept = [piece(bit_a, o) if h == 0 else piece(o, bit_b) for o in range(2)]
        sent = [piece(1 - bit_a, o) if h == 0 else piece(o, 1 - bit_b) for o in range(2)]

        @pl.loop(0, plan.blocks)
        def _(block):
            first = h * HALF + block * plan.group
            for other in range(2):
                keep_ref[h, other, block] = rows_of(first, kept[other])
                put(send_ref, plan, other * plan.blocks + block, rows_of(first, sent[other]), level_ref)

        put_levels(send_ref, plan, 2 * plan.blocks, level_ref)


def virt_body(meta_ref, place_ref, *rest, plan):
    sources, (keep_ref, send0_ref, send1_ref) = rest[:8], rest[8:11]
    refs, (acc_ref, level_ref, sems) = rest[11:19], rest[19:]
    loads = [pltpu.make_async_copy(src, dst, sems.at[i]) for i, (src, dst) in enumerate(zip(sources, refs))]
    for load in loads:
        load.start()
    acc_ref[...] = jnp.zeros(acc_ref.shape, F32)
    for load in loads:
        load.wait()
    own_ref, green_ref = refs[0], refs[7]
    half = OWNERS // 2
    for part in range(2):

        @pl.loop(0, half // 2)
        def _(step):
            for local in (step * 2, step * 2 + 1):
                source = part * half + local
                for slot in range(CAP):
                    span = slice(slot * QUARTER, (slot + 1) * QUARTER)
                    parts = [own_ref[source, span, :]] + [ref[local, span, :] for ref in refs[1 + part : 7 : 2]]
                    aux = meta_ref[source, 2 * slot]
                    kept = meta_ref[source, 2 * slot + 1]
                    tile = jnp.concatenate(parts, axis=0)
                    acc_ref[aux] += jnp.dot(tile, green_ref[kept], preferred_element_type=F32)

    split_pieces(place_ref, plan, piece_rows(acc_ref), keep_ref, (send0_ref, send1_ref), level_ref)


def piece_rows(acc_ref):
    def rows_of(first, piece):
        at = [pl.multiple_of(quarter * QUARTER + piece * 8, 8) for quarter in range(4)]
        return jnp.concatenate([acc_ref[first, pl.ds(row, 8), :] for row in at], axis=0)

    return rows_of


def occ_body(
    meta_ref, place_ref, own_ref, *rest, plan
):
    halves, green_ref, rest = rest[:6], rest[6], rest[7:]
    keep_ref, send0_ref, send1_ref, acc_ref, tile_ref, level_ref = rest
    acc_ref[...] = jnp.zeros(acc_ref.shape, F32)
    row_place = place_ref[0]
    rows = [pl.multiple_of(((row_place + d) % ROWS) * QUARTER, QUARTER) for d in (0, ROWS - 1, 1, 2)]
    half = OWNERS // 2
    for part in range(2):

        @pl.loop(0, half // 2)
        def _(step):
            visits = [(j, slot) for j in range(2) for slot in range(CAP)]
            for j, slot in visits:
                local = step * 2 + j
                source = part * half + local
                span = slice(slot * QUARTER, (slot + 1) * QUARTER)
                tile_ref[CAP * j + slot, pl.ds(rows[0], QUARTER), :] = own_ref[source, span, :]
                for ref, row in zip(halves[part::2], rows[1:]):
                    tile_ref[CAP * j + slot, pl.ds(row, QUARTER), :] = ref[local, span, :]
            for j, slot in visits:
                source = part * half + step * 2 + j
                aux = meta_ref[source, 2 * slot]
                kept = meta_ref[source, 2 * slot + 1]
                term = lax.dot_general(
                    green_ref[kept], tile_ref[CAP * j + slot], (((1,), (1,)), ((), ())), preferred_element_type=F32
                )
                for low in range(4):
                    lanes = slice(low * BS, (low + 1) * BS)
                    acc_ref[aux, :, lanes] += term[low * BS : (low + 1) * BS, :]

    split_pieces(place_ref, plan, piece_rows(acc_ref), keep_ref, (send0_ref, send1_ref), level_ref)


VMEM = pl.BlockSpec(memory_space=pltpu.VMEM)
SMEM = pl.BlockSpec(memory_space=pltpu.SMEM)
ANY = pl.BlockSpec(memory_space=pl.ANY)


def step_shapes(plan):
    code = jax.ShapeDtypeStruct((plan.coded(2 * plan.blocks), WIDE), S16)
    return [jax.ShapeDtypeStruct((2, 2, plan.blocks, plan.rows, WIDE), F32), code, code]


def level_scratch(plan):
    return pltpu.VMEM((plan.levels(2 * plan.blocks), WIDE), F32)


def contract_virt(meta, place, quarters, green, plan):
    operands = [*quarters, green]
    return pl.pallas_call(
        functools.partial(virt_body, plan=plan),
        in_specs=[SMEM] * 2 + [ANY] * 8,
        out_specs=[VMEM] * 3,
        out_shape=step_shapes(plan),
        scratch_shapes=[pltpu.VMEM(x.shape, x.dtype) for x in operands]
        + [pltpu.VMEM((NP, BS, WIDE), F32), level_scratch(plan), pltpu.SemaphoreType.DMA((8,))],
        compiler_params=params(55),
        name="contract_virt",
    )(meta, place, *operands)


def contract_occ(meta, place, quarters, green, plan):
    return pl.pallas_call(
        functools.partial(occ_body, plan=plan),
        in_specs=[SMEM] * 2 + [VMEM] * 8,
        out_specs=[VMEM] * 3,
        out_shape=step_shapes(plan),
        scratch_shapes=[pltpu.VMEM((NP, BS, WIDE), F32), pltpu.VMEM((2 * CAP, BS, BS), BF16), level_scratch(plan)],
        compiler_params=params(28),
        name="contract_occ",
    )(meta, place, *quarters, green)


def halve_body(place_ref, keep_ref, got0_ref, got1_ref, left_ref, send0_ref, send1_ref, level_ref, scale_ref, *, plan):
    for h, got_ref, send_ref in ((0, got0_ref, send0_ref), (1, got1_ref, send1_ref)):
        mine = place_ref[2 - h]
        away = 1 - mine
        read_scales(got_ref, (), plan, 2 * plan.blocks, scale_ref)

        @pl.loop(0, plan.blocks)
        def _(b):
            left_ref[h, b] = keep_ref[h, mine, b] + get(got_ref, (), plan, mine * plan.blocks + b, scale_ref)
            total = keep_ref[h, away, b] + get(got_ref, (), plan, away * plan.blocks + b, scale_ref)
            put(send_ref, plan, b, total, level_ref)

        put_levels(send_ref, plan, plan.blocks, level_ref)


def halve(place, keep, got0, got1, plan, name):
    code = jax.ShapeDtypeStruct((plan.coded(plan.blocks), WIDE), S16)
    return pl.pallas_call(
        functools.partial(halve_body, plan=plan),
        in_specs=[SMEM] + [VMEM] * 3,
        out_specs=[VMEM] * 3,
        out_shape=[jax.ShapeDtypeStruct((2, plan.blocks, plan.rows, WIDE), F32), code, code],
        scratch_shapes=[level_scratch(plan), level_scratch(plan)],
        compiler_params=params(16),
        name=name,
    )(place, keep, got0, got1)


def finish_body(left_ref, got0_ref, got1_ref, out_ref, level_ref, scale_ref, *, plan, split):
    count = 2 * plan.blocks
    for h, got_ref in ((0, got0_ref), (1, got1_ref)):
        read_scales(got_ref, (), plan, plan.blocks, scale_ref)

        @pl.loop(0, plan.blocks)
        def _(b):
            total = left_ref[h, b] + get(got_ref, (), plan, b, scale_ref)
            index = h * plan.blocks + b
            if split:
                codes, level = encode(total)
                for low in range(4):
                    out_ref[low, at_block(plan, index), :] = codes[:, low * BS : (low + 1) * BS]
                level_ref[pl.ds(index, 1), :] = level
            else:
                put(out_ref, plan, index, total, level_ref)

    if split:
        levels = level_ref[...].astype(jnp.int32).astype(S16)
        for low in range(4):
            out_ref[low, level_rows(plan, count), :] = levels[:, low * BS : (low + 1) * BS]
    else:
        put_levels(out_ref, plan, count, level_ref)


def finish(left, got0, got1, plan, split, name):
    rows = plan.coded(2 * plan.blocks)
    shape = (4, rows, BS) if split else (rows, WIDE)
    return pl.pallas_call(
        functools.partial(finish_body, plan=plan, split=split),
        in_specs=[VMEM] * 3,
        out_specs=VMEM,
        out_shape=jax.ShapeDtypeStruct(shape, S16),
        scratch_shapes=[level_scratch(plan), level_scratch(plan)],
        compiler_params=params(12),
        name=name,
    )(left, got0, got1)


def pair_body(place_ref, own_ref, one_ref, two_ref, three_ref, virt_ref, out_ref, occ_ref, vir_ref, wide_ref, thin_ref, *, plan):
    here = place_ref[0]
    high = place_ref[1]
    count = 2 * plan.blocks

    at = [((high + shift) % 4) * 8 for shift in (0, ROWS - 1, 1, 2)]
    read_scales(virt_ref, (), plan, count, wide_ref)

    @pl.loop(0, NP)
    def _(q):
        values = get(virt_ref, (), plan, q, wide_ref)
        for quarter in range(4):
            for low in range(4):
                to = pl.ds(pl.multiple_of(low * QUARTER + at[quarter], 8), 8)
                vir_ref[q, to, :] = values[quarter * 8 : (quarter + 1) * 8, low * BS : (low + 1) * BS]

    for d, ref in enumerate((own_ref, one_ref, two_ref, three_ref)):
        source = (here + 4 - d) % 4
        lead = (here,) if d == 0 else (0,)
        read_scales(ref, lead, plan, count, thin_ref)
        rows = pl.ds(pl.multiple_of(source * QUARTER, QUARTER), QUARTER)

        @pl.loop(0, NP)
        def _(p):
            occ_ref[p, rows, :] = get(ref, lead, plan, p, thin_ref)

    @pl.loop(0, NP)
    def _(p):
        occ = occ_ref[p]
        for q in range(NP):
            out_ref[p, q : q + 1, :] = jnp.sum(occ * vir_ref[q], axis=0, keepdims=True)


def pair(place, own, others, virt, plan):
    levels = plan.levels(2 * plan.blocks)
    return pl.pallas_call(
        functools.partial(pair_body, plan=plan),
        in_specs=[SMEM] + [VMEM] * 5,
        out_specs=VMEM,
        out_shape=jax.ShapeDtypeStruct((NP, NP, BS), F32),
        scratch_shapes=[
            pltpu.VMEM((NP, BS, BS), F32),
            pltpu.VMEM((NP, BS, BS), F32),
            pltpu.VMEM((levels, WIDE), F32),
            pltpu.VMEM((levels, BS), F32),
        ],
        compiler_params=params(16),
        name="pair",
    )(place, own, *others, virt)


def rotate(size, step):
    return [(i, (i + step) % size) for i in range(size)]


def rotate_low(step):
    return [(c, c - c % 4 + (c + step) % 4) for c in range(COLS)]


def rotate_high(step):
    return [(c, (c + 4 * step) % COLS) for c in range(COLS)]


PAIRS_A = [(0, 1), (1, 0), (2, 3), (3, 2)]
PAIRS_B = [(0, 3), (3, 0), (1, 2), (2, 1)]


def index_of(row, col, layer):
    return (row * COLS + col) * LAYERS + layer


SWAP = [
    (index_of(r, c, l), index_of(c % 4, c // 4 * 4 + r, l))
    for r in range(ROWS)
    for c in range(COLS)
    for l in range(LAYERS)
]


def tree_sum(values):
    rounds = (
        ("layer", [rotate(LAYERS, d) for d in (1, 2, 3)]),
        ("col", [rotate_low(d) for d in (1, 2, 3)]),
        ("row", [rotate(ROWS, d) for d in (1, 2, 3)]),
        ("col", [rotate_high(d) for d in (1, 2, 3)]),
    )
    for axis, perms in rounds:
        one, two, three = [lax.ppermute(values, axis, perm) for perm in perms]
        values = (values + two) + (one + three)
    return values


def layer_swap(send0, send1, perms):
    return lax.ppermute(send0, "layer", perms[0]), lax.ppermute(send1, "layer", perms[1])


FIRST = (PAIRS_A, PAIRS_B)
SECOND = (PAIRS_B, PAIRS_A)


def after(*values):
    return lax.optimization_barrier(values)


def on_device(blocks, block_aux, block_row, block_col, extents, occ_green, virt_green):
    layer_blocks = occ_green.shape[0] // BS
    row_place = lax.axis_index("row").astype(jnp.int32)
    col_place = lax.axis_index("col").astype(jnp.int32)
    layer_place = lax.axis_index("layer").astype(jnp.int32)
    bit_a = ((layer_place == 1) | (layer_place == 2)).astype(jnp.int32)
    bit_b = layer_place // 2
    place = jnp.stack([row_place, bit_a, bit_b])
    plan = Plan(4)

    tiles = lax.dynamic_slice_in_dim(blocks, row_place * QUARTER, QUARTER, 1)
    send = build_send(tiles, block_aux, block_row, block_col, extents, layer_blocks)
    own = lax.all_to_all(send, ("col", "layer"), 0, 0, tiled=True)
    meta = own[:, CAP * QUARTER, : 2 * CAP].astype(jnp.int32)
    virt_blocks = virt_green.reshape(layer_blocks, BS, WIDE)
    occ_blocks = occ_green.reshape(layer_blocks, BS, WIDE).transpose(0, 2, 1)

    half = OWNERS // 2
    own_a, own_b = own[:half], own[half:]
    up, down = rotate(ROWS, 1), rotate(ROWS, -1)
    prev_a = lax.ppermute(own_a, "row", up)
    next_b = lax.ppermute(own_b, "row", down)
    prev_a, next_b, own_a, own_b, occ_blocks = after(prev_a, next_b, own_a, own_b, occ_blocks)
    far_a = lax.ppermute(prev_a, "row", up)
    far_b = lax.ppermute(next_b, "row", down)
    prev_b = lax.ppermute(own_b, "row", up)
    next_a = lax.ppermute(own_a, "row", down)
    quarters = (own, prev_a, prev_b, next_a, next_b, far_a, far_b)

    v_keep, v0, v1 = contract_virt(meta, place, quarters, virt_blocks, plan)
    v_got = layer_swap(v0, v1, FIRST)
    occ_blocks, v_keep = after(occ_blocks, v_keep)
    o_keep, o0, o1 = contract_occ(meta, place, quarters, occ_blocks, plan)
    o_got = layer_swap(o0, o1, FIRST)
    v_keep, o_keep = after(v_keep, o_keep)
    v_left, v0, v1 = halve(place, v_keep, *v_got, plan, "halve_virt")
    v0, v1, *o_got = after(v0, v1, *o_got)
    v_got = layer_swap(v0, v1, SECOND)
    o_left, o0, o1 = halve(place, o_keep, *o_got, plan, "halve_occ")
    o0, o1, *v_got = after(o0, o1, *v_got)
    o_got = layer_swap(o0, o1, SECOND)
    v_left, *o_got = after(v_left, *o_got)
    virt = finish(v_left, *v_got, plan, False, "finish_virt")
    o_left, virt = after(o_left, virt)
    virt = lax.ppermute(virt, ALL, SWAP)
    occ = finish(o_left, *o_got, plan, True, "finish_occ")

    low = col_place // 4
    others = []
    for d in (1, 2, 3):
        part = lax.dynamic_slice_in_dim(occ, (low + d) % 4, 1, 0)
        others.append(lax.ppermute(part, "col", rotate_high(d)))
    here = jnp.stack([low, col_place % 4])
    partial = pair(here, occ, others, virt, plan)
    return tree_sum(jnp.sum(partial, axis=-1))


def solution(mesh):
    in_specs = (
        P(("col", "layer"), None, None),
        P(("col", "layer")),
        P(("col", "layer")),
        P(("col", "layer")),
        P(("col", "layer")),
        P("layer", "row"),
        P("layer", "row"),
    )
    return jax.shard_map(on_device, mesh=mesh, in_specs=in_specs, out_specs=P(), check_vma=False)
```

```python
import functools

import jax
import jax.numpy as jnp
from jax import lax
from jax.experimental import pallas as pl
from jax.experimental.pallas import tpu as pltpu
from jax.sharding import PartitionSpec as P

NP = 24
ROWS = 4
COLS = 16
LAYERS = 4
CAP = 2
OWNERS = COLS * LAYERS
BS = 128
QUARTER = BS // ROWS
WIDE = 512
HALF = NP // 2
TOP = 32700.0
STEPS = 64.0
ALL = ("row", "col", "layer")
F32 = jnp.float32
BF16 = jnp.bfloat16
S16 = jnp.int16


def params(mib):
    return pltpu.CompilerParams(vmem_limit_bytes=mib * 2**20)


def encode(block):
    peak = jnp.max(jnp.abs(block), axis=0, keepdims=True)
    level = jnp.ceil(jnp.log2(jnp.maximum(peak, 1e-30)) * STEPS)
    scaled = block * (jnp.exp2(level * (-1.0 / STEPS)) * TOP)
    return jnp.round(scaled).astype(jnp.int32).astype(S16), level


def decode(codes, level):
    return codes.astype(jnp.int32).astype(F32) * (jnp.exp2(level * (1.0 / STEPS)) * (1.0 / TOP))


class Plan:
    def __init__(self, quarters):
        self.quarters = quarters
        self.group = 4 // quarters
        self.rows = 8 * quarters * self.group
        self.blocks = HALF // self.group

    def levels(self, count):
        return (count + 15) // 16 * 16

    def coded(self, count):
        return count * self.rows + self.levels(count)


def at_block(plan, index):
    return pl.ds(pl.multiple_of(index * plan.rows, 16), plan.rows)


def level_rows(plan, count):
    return slice(count * plan.rows, plan.coded(count))


def read_scales(ref, lead, plan, count, scale_ref):
    level = ref[(*lead, level_rows(plan, count), slice(None))].astype(jnp.int32).astype(F32)
    scale_ref[: plan.levels(count), :] = jnp.exp2(level * (1.0 / STEPS)) * (1.0 / TOP)


def get(ref, lead, plan, index, scale_ref):
    codes = ref[(*lead, at_block(plan, index), slice(None))]
    return codes.astype(jnp.int32).astype(F32) * scale_ref[pl.ds(index, 1), :]


def put(ref, plan, index, block, level_ref):
    codes, level = encode(block)
    ref[at_block(plan, index), :] = codes
    level_ref[pl.ds(index, 1), :] = level


def put_levels(ref, plan, count, level_ref):
    level = level_ref[: plan.levels(count), :]
    ref[level_rows(plan, count), :] = level.astype(jnp.int32).astype(S16)


def send_body(aux_ref, row_ref, col_ref, ext_ref, tiles_ref, out_ref, count_ref, *, layer_blocks):
    out_ref[...] = jnp.zeros(out_ref.shape, BF16)

    @pl.loop(0, OWNERS)
    def _(i):
        count_ref[i] = 0

    lane = lax.broadcasted_iota(jnp.int32, (QUARTER, BS), 1)
    meta_lane = lax.broadcasted_iota(jnp.int32, (8, BS), 1)

    @pl.loop(0, tiles_ref.shape[0])
    def _(i):
        col = col_ref[i]
        layer_of = col // layer_blocks
        kept = col - layer_of * layer_blocks
        owner = (row_ref[i] % 4 * 4 + row_ref[i] // 4) * LAYERS + layer_of
        used = count_ref[owner]
        count_ref[owner] = used + 1
        tile = jnp.where(lane < ext_ref[i], tiles_ref[i].astype(F32), 0.0)
        out_ref[owner, pl.ds(pl.multiple_of(used * QUARTER, QUARTER), QUARTER), :] = tile.astype(BF16)
        old = out_ref[owner, CAP * QUARTER :, :].astype(F32)
        new = jnp.where(meta_lane == used * 2, aux_ref[i].astype(F32), old)
        new = jnp.where(meta_lane == used * 2 + 1, kept.astype(F32), new)
        out_ref[owner, CAP * QUARTER :, :] = new.astype(BF16)


def build_send(tiles, block_aux, block_row, block_col, extents, layer_blocks):
    return pl.pallas_call(
        functools.partial(send_body, layer_blocks=layer_blocks),
        in_specs=[SMEM] * 4 + [VMEM],
        out_specs=VMEM,
        out_shape=jax.ShapeDtypeStruct((OWNERS, CAP * QUARTER + 8, BS), BF16),
        scratch_shapes=[pltpu.SMEM((OWNERS,), jnp.int32)],
        compiler_params=params(8),
        name="build_send",
    )(block_aux, block_row, block_col, extents, tiles)


def split_pieces(place_ref, plan, rows_of, keep_ref, send_refs, level_ref):
    bit_a = place_ref[1]
    bit_b = place_ref[2]

    def piece(a, b):
        return jnp.where(b == 0, a, 3 - a)

    for h, send_ref in enumerate(send_refs):
        kept = [piece(bit_a, o) if h == 0 else piece(o, bit_b) for o in range(2)]
        sent = [piece(1 - bit_a, o) if h == 0 else piece(o, 1 - bit_b) for o in range(2)]

        @pl.loop(0, plan.blocks)
        def _(block):
            first = h * HALF + block * plan.group
            for other in range(2):
                keep_ref[h, other, block] = rows_of(first, kept[other])
                put(send_ref, plan, other * plan.blocks + block, rows_of(first, sent[other]), level_ref)

        put_levels(send_ref, plan, 2 * plan.blocks, level_ref)


def start_all(sources, targets, sems):
    loads = [pltpu.make_async_copy(src, dst, sems.at[i]) for i, (src, dst) in enumerate(zip(sources, targets))]
    for load in loads:
        load.start()
    return loads


def add_virt(meta_ref, first, quarter_refs, green_ref, acc_ref):
    @pl.loop(0, OWNERS // 4)
    def _(step):
        for local in (step * 2, step * 2 + 1):
            for slot in range(CAP):
                span = slice(slot * QUARTER, (slot + 1) * QUARTER)
                tile = jnp.concatenate([ref[local, span, :] for ref in quarter_refs], axis=0)
                aux = meta_ref[first + local, 2 * slot]
                kept = meta_ref[first + local, 2 * slot + 1]
                acc_ref[aux] += jnp.dot(tile, green_ref[kept], preferred_element_type=F32)


def virt_first_body(meta_ref, *rest):
    sources, out_ref, refs, (acc_ref, sems) = rest[:5], rest[5], rest[6:11], rest[11:]
    loads = start_all(sources, refs, sems)
    acc_ref[...] = jnp.zeros(acc_ref.shape, F32)
    for load in loads:
        load.wait()
    add_virt(meta_ref, 0, refs[:4], refs[4], acc_ref)
    store = pltpu.make_async_copy(acc_ref, out_ref, sems.at[0])
    store.start()
    store.wait()


def virt_last_body(meta_ref, place_ref, *rest, plan):
    sources, (keep_ref, send0_ref, send1_ref) = rest[:6], rest[6:9]
    refs, (level_ref, sems) = rest[9:15], rest[15:]
    for load in start_all(sources, refs, sems):
        load.wait()
    acc_ref = refs[5]
    add_virt(meta_ref, OWNERS // 2, refs[:4], refs[4], acc_ref)
    split_pieces(place_ref, plan, piece_rows(acc_ref), keep_ref, (send0_ref, send1_ref), level_ref)


def piece_rows(acc_ref):
    def rows_of(first, piece):
        at = [pl.multiple_of(quarter * QUARTER + piece * 8, 8) for quarter in range(4)]
        return jnp.concatenate([acc_ref[first, pl.ds(row, 8), :] for row in at], axis=0)

    return rows_of


def occ_body(meta_ref, place_ref, *rest, plan):
    parts, green_ref, (keep_ref, send0_ref, send1_ref, acc_ref, tile_ref, level_ref) = (rest[:4], rest[4:8]), rest[8], rest[9:]
    acc_ref[...] = jnp.zeros(acc_ref.shape, F32)
    row_place = place_ref[0]
    rows = [pl.multiple_of(((row_place + d) % ROWS) * QUARTER, QUARTER) for d in (0, ROWS - 1, 1, 2)]
    half = OWNERS // 2
    visits = [(j, slot) for j in range(2) for slot in range(CAP)]
    for part in range(2):

        @pl.loop(0, half // 2)
        def _(step):
            for j, slot in visits:
                span = slice(slot * QUARTER, (slot + 1) * QUARTER)
                for ref, row in zip(parts[part], rows):
                    tile_ref[CAP * j + slot, pl.ds(row, QUARTER), :] = ref[step * 2 + j, span, :]
            for j, slot in visits:
                source = part * half + step * 2 + j
                aux = meta_ref[source, 2 * slot]
                kept = meta_ref[source, 2 * slot + 1]
                term = lax.dot_general(
                    green_ref[kept], tile_ref[CAP * j + slot], (((1,), (1,)), ((), ())), preferred_element_type=F32
                )
                for low in range(4):
                    lanes = slice(low * BS, (low + 1) * BS)
                    acc_ref[aux, :, lanes] += term[low * BS : (low + 1) * BS, :]

    split_pieces(place_ref, plan, piece_rows(acc_ref), keep_ref, (send0_ref, send1_ref), level_ref)


VMEM = pl.BlockSpec(memory_space=pltpu.VMEM)
SMEM = pl.BlockSpec(memory_space=pltpu.SMEM)
ANY = pl.BlockSpec(memory_space=pl.ANY)


def step_shapes(plan):
    code = jax.ShapeDtypeStruct((plan.coded(2 * plan.blocks), WIDE), S16)
    return [jax.ShapeDtypeStruct((2, 2, plan.blocks, plan.rows, WIDE), F32), code, code]


def level_scratch(plan):
    return pltpu.VMEM((plan.levels(2 * plan.blocks), WIDE), F32)


ACC = (NP, BS, WIDE)


def scratch_like(operands):
    return [pltpu.VMEM(x.shape, x.dtype) for x in operands]


def contract_virt_first(meta, part, green):
    operands = [*part, green]
    return pl.pallas_call(
        virt_first_body,
        in_specs=[SMEM] + [ANY] * 5,
        out_specs=ANY,
        out_shape=jax.ShapeDtypeStruct(ACC, F32),
        scratch_shapes=scratch_like(operands) + [pltpu.VMEM(ACC, F32), pltpu.SemaphoreType.DMA((5,))],
        compiler_params=params(55),
        name="virt_first",
    )(meta, *operands)


def contract_virt_last(meta, place, part, green, before, plan):
    operands = [*part, green, before]
    return pl.pallas_call(
        functools.partial(virt_last_body, plan=plan),
        in_specs=[SMEM] * 2 + [ANY] * 6,
        out_specs=[VMEM] * 3,
        out_shape=step_shapes(plan),
        scratch_shapes=scratch_like(operands) + [level_scratch(plan), pltpu.SemaphoreType.DMA((6,))],
        compiler_params=params(55),
        name="virt_last",
    )(meta, place, *operands)


def contract_occ(meta, place, parts, green, plan):
    return pl.pallas_call(
        functools.partial(occ_body, plan=plan),
        in_specs=[SMEM] * 2 + [VMEM] * 9,
        out_specs=[VMEM] * 3,
        out_shape=step_shapes(plan),
        scratch_shapes=[pltpu.VMEM(ACC, F32), pltpu.VMEM((2 * CAP, BS, BS), BF16), level_scratch(plan)],
        compiler_params=params(28),
        name="contract_occ",
    )(meta, place, *parts[0], *parts[1], green)


def halve_body(place_ref, keep_ref, got0_ref, got1_ref, left_ref, send0_ref, send1_ref, level_ref, scale_ref, *, plan):
    for h, got_ref, send_ref in ((0, got0_ref, send0_ref), (1, got1_ref, send1_ref)):
        mine = place_ref[2 - h]
        away = 1 - mine
        read_scales(got_ref, (), plan, 2 * plan.blocks, scale_ref)

        @pl.loop(0, plan.blocks)
        def _(b):
            left_ref[h, b] = keep_ref[h, mine, b] + get(got_ref, (), plan, mine * plan.blocks + b, scale_ref)
            total = keep_ref[h, away, b] + get(got_ref, (), plan, away * plan.blocks + b, scale_ref)
            put(send_ref, plan, b, total, level_ref)

        put_levels(send_ref, plan, plan.blocks, level_ref)


def halve(place, keep, got0, got1, plan, name):
    code = jax.ShapeDtypeStruct((plan.coded(plan.blocks), WIDE), S16)
    return pl.pallas_call(
        functools.partial(halve_body, plan=plan),
        in_specs=[SMEM] + [VMEM] * 3,
        out_specs=[VMEM] * 3,
        out_shape=[jax.ShapeDtypeStruct((2, plan.blocks, plan.rows, WIDE), F32), code, code],
        scratch_shapes=[level_scratch(plan), level_scratch(plan)],
        compiler_params=params(16),
        name=name,
    )(place, keep, got0, got1)


def finish_body(left_ref, got0_ref, got1_ref, out_ref, level_ref, scale_ref, *, plan, split):
    count = 2 * plan.blocks
    for h, got_ref in ((0, got0_ref), (1, got1_ref)):
        read_scales(got_ref, (), plan, plan.blocks, scale_ref)

        @pl.loop(0, plan.blocks)
        def _(b):
            total = left_ref[h, b] + get(got_ref, (), plan, b, scale_ref)
            index = h * plan.blocks + b
            if split:
                codes, level = encode(total)
                for low in range(4):
                    out_ref[low, at_block(plan, index), :] = codes[:, low * BS : (low + 1) * BS]
                level_ref[pl.ds(index, 1), :] = level
            else:
                put(out_ref, plan, index, total, level_ref)

    if split:
        levels = level_ref[...].astype(jnp.int32).astype(S16)
        for low in range(4):
            out_ref[low, level_rows(plan, count), :] = levels[:, low * BS : (low + 1) * BS]
    else:
        put_levels(out_ref, plan, count, level_ref)


def finish(left, got0, got1, plan, split, name):
    rows = plan.coded(2 * plan.blocks)
    shape = (4, rows, BS) if split else (rows, WIDE)
    return pl.pallas_call(
        functools.partial(finish_body, plan=plan, split=split),
        in_specs=[VMEM] * 3,
        out_specs=VMEM,
        out_shape=jax.ShapeDtypeStruct(shape, S16),
        scratch_shapes=[level_scratch(plan), level_scratch(plan)],
        compiler_params=params(12),
        name=name,
    )(left, got0, got1)


def pair_body(place_ref, own_ref, one_ref, two_ref, three_ref, virt_ref, out_ref, occ_ref, vir_ref, wide_ref, thin_ref, *, plan):
    here = place_ref[0]
    high = place_ref[1]
    count = 2 * plan.blocks

    at = [((high + shift) % 4) * 8 for shift in (0, ROWS - 1, 1, 2)]
    read_scales(virt_ref, (), plan, count, wide_ref)

    @pl.loop(0, NP)
    def _(q):
        values = get(virt_ref, (), plan, q, wide_ref)
        for quarter in range(4):
            for low in range(4):
                to = pl.ds(pl.multiple_of(low * QUARTER + at[quarter], 8), 8)
                vir_ref[q, to, :] = values[quarter * 8 : (quarter + 1) * 8, low * BS : (low + 1) * BS]

    for d, ref in enumerate((own_ref, one_ref, two_ref, three_ref)):
        source = (here + 4 - d) % 4
        lead = (here,) if d == 0 else (0,)
        read_scales(ref, lead, plan, count, thin_ref)
        rows = pl.ds(pl.multiple_of(source * QUARTER, QUARTER), QUARTER)

        @pl.loop(0, NP)
        def _(p):
            occ_ref[p, rows, :] = get(ref, lead, plan, p, thin_ref)

    @pl.loop(0, NP)
    def _(p):
        occ = occ_ref[p]
        for q in range(NP):
            out_ref[p, q : q + 1, :] = jnp.sum(occ * vir_ref[q], axis=0, keepdims=True)


def pair(place, own, others, virt, plan):
    levels = plan.levels(2 * plan.blocks)
    return pl.pallas_call(
        functools.partial(pair_body, plan=plan),
        in_specs=[SMEM] + [VMEM] * 5,
        out_specs=VMEM,
        out_shape=jax.ShapeDtypeStruct((NP, NP, BS), F32),
        scratch_shapes=[
            pltpu.VMEM((NP, BS, BS), F32),
            pltpu.VMEM((NP, BS, BS), F32),
            pltpu.VMEM((levels, WIDE), F32),
            pltpu.VMEM((levels, BS), F32),
        ],
        compiler_params=params(16),
        name="pair",
    )(place, own, *others, virt)


def rotate(size, step):
    return [(i, (i + step) % size) for i in range(size)]


def rotate_low(step):
    return [(c, c - c % 4 + (c + step) % 4) for c in range(COLS)]


def rotate_high(step):
    return [(c, (c + 4 * step) % COLS) for c in range(COLS)]


PAIRS_A = [(0, 1), (1, 0), (2, 3), (3, 2)]
PAIRS_B = [(0, 3), (3, 0), (1, 2), (2, 1)]


def index_of(row, col, layer):
    return (row * COLS + col) * LAYERS + layer


SWAP = [
    (index_of(r, c, l), index_of(c % 4, c // 4 * 4 + r, l))
    for r in range(ROWS)
    for c in range(COLS)
    for l in range(LAYERS)
]


def tree_sum(values):
    rounds = (
        ("layer", [rotate(LAYERS, d) for d in (1, 2, 3)]),
        ("col", [rotate_low(d) for d in (1, 2, 3)]),
        ("row", [rotate(ROWS, d) for d in (1, 2, 3)]),
        ("col", [rotate_high(d) for d in (1, 2, 3)]),
    )
    for axis, perms in rounds:
        one, two, three = [lax.ppermute(values, axis, perm) for perm in perms]
        values = (values + two) + (one + three)
    return values


def layer_swap(send0, send1, perms):
    return lax.ppermute(send0, "layer", perms[0]), lax.ppermute(send1, "layer", perms[1])


FIRST = (PAIRS_A, PAIRS_B)
SECOND = (PAIRS_B, PAIRS_A)


def after(*values):
    return lax.optimization_barrier(values)


def on_device(blocks, block_aux, block_row, block_col, extents, occ_green, virt_green):
    layer_blocks = occ_green.shape[0] // BS
    row_place = lax.axis_index("row").astype(jnp.int32)
    col_place = lax.axis_index("col").astype(jnp.int32)
    layer_place = lax.axis_index("layer").astype(jnp.int32)
    bit_a = ((layer_place == 1) | (layer_place == 2)).astype(jnp.int32)
    bit_b = layer_place // 2
    place = jnp.stack([row_place, bit_a, bit_b])
    plan = Plan(4)

    tiles = lax.dynamic_slice_in_dim(blocks, row_place * QUARTER, QUARTER, 1)
    send = build_send(tiles, block_aux, block_row, block_col, extents, layer_blocks)
    own = lax.all_to_all(send, ("col", "layer"), 0, 0, tiled=True)
    meta = own[:, CAP * QUARTER, : 2 * CAP].astype(jnp.int32)
    virt_blocks = virt_green.reshape(layer_blocks, BS, WIDE)
    occ_blocks = occ_green.reshape(layer_blocks, BS, WIDE).transpose(0, 2, 1)

    half = OWNERS // 2
    own_a, own_b = own[:half, : CAP * QUARTER], own[half:, : CAP * QUARTER]
    up, down = rotate(ROWS, 1), rotate(ROWS, -1)
    prev_a = lax.ppermute(own_a, "row", up)
    next_a = lax.ppermute(own_a, "row", down)
    prev_a, next_a, own_b, occ_blocks = after(prev_a, next_a, own_b, occ_blocks)
    far_a = lax.ppermute(prev_a, "row", up)
    next_b = lax.ppermute(own_b, "row", down)
    far_a, next_b, own_b = after(far_a, next_b, own_b)
    prev_b = lax.ppermute(own_b, "row", up)
    far_b = lax.ppermute(next_b, "row", down)
    part_a, part_b = (own_a, prev_a, next_a, far_a), (own_b, prev_b, next_b, far_b)

    v_acc = contract_virt_first(meta, part_a, virt_blocks)
    v_keep, v0, v1 = contract_virt_last(meta, place, part_b, virt_blocks, v_acc, plan)
    v_got = layer_swap(v0, v1, FIRST)
    occ_blocks, v_keep = after(occ_blocks, v_keep)
    o_keep, o0, o1 = contract_occ(meta, place, (part_a, part_b), occ_blocks, plan)
    v_keep, o_keep = after(v_keep, o_keep)
    v_left, v0, v1 = halve(place, v_keep, *v_got, plan, "halve_virt")
    v_got = layer_swap(v0, v1, SECOND)
    o0, o1, *v_got = after(o0, o1, *v_got)
    o_got = layer_swap(o0, o1, FIRST)
    virt = finish(v_left, *v_got, plan, False, "finish_virt")
    virt, o_keep = after(virt, o_keep)
    virt = lax.ppermute(virt, ALL, SWAP)
    o_left, o0, o1 = halve(place, o_keep, *o_got, plan, "halve_occ")
    o_got = layer_swap(o0, o1, SECOND)
    occ = finish(o_left, *o_got, plan, True, "finish_occ")

    low = col_place // 4
    others = []
    for d in (1, 2, 3):
        part = lax.dynamic_slice_in_dim(occ, (low + d) % 4, 1, 0)
        others.append(lax.ppermute(part, "col", rotate_high(d)))
    here = jnp.stack([low, col_place % 4])
    partial = pair(here, occ, others, virt, plan)
    return tree_sum(jnp.sum(partial, axis=-1))


def solution(mesh):
    in_specs = (
        P(("col", "layer"), None, None),
        P(("col", "layer")),
        P(("col", "layer")),
        P(("col", "layer")),
        P(("col", "layer")),
        P("layer", "row"),
        P("layer", "row"),
    )
    return jax.shard_map(on_device, mesh=mesh, in_specs=in_specs, out_specs=P(), check_vma=False)
```

```python
import functools

import jax
import jax.numpy as jnp
from jax import lax
from jax.experimental import pallas as pl
from jax.experimental.pallas import tpu as pltpu
from jax.sharding import PartitionSpec as P

NP = 24
ROWS = 4
COLS = 16
LAYERS = 4
CAP = 2
OWNERS = COLS * LAYERS
BS = 128
QUARTER = BS // ROWS
WIDE = 512
HALF = NP // 2
TOP = 32700.0
STEPS = 64.0
ALL = ("row", "col", "layer")
F32 = jnp.float32
BF16 = jnp.bfloat16
S16 = jnp.int16


def params(mib):
    return pltpu.CompilerParams(vmem_limit_bytes=mib * 2**20)


def encode(block):
    peak = jnp.max(jnp.abs(block), axis=0, keepdims=True)
    level = jnp.ceil(jnp.log2(jnp.maximum(peak, 1e-30)) * STEPS)
    scaled = block * (jnp.exp2(level * (-1.0 / STEPS)) * TOP)
    return jnp.round(scaled).astype(jnp.int32).astype(S16), level


def decode(codes, level):
    return codes.astype(jnp.int32).astype(F32) * (jnp.exp2(level * (1.0 / STEPS)) * (1.0 / TOP))


class Plan:
    def __init__(self, quarters):
        self.quarters = quarters
        self.group = 4 // quarters
        self.rows = 8 * quarters * self.group
        self.blocks = HALF // self.group

    def levels(self, count):
        return (count + 15) // 16 * 16

    def coded(self, count):
        return count * self.rows + self.levels(count)


def at_block(plan, index):
    return pl.ds(pl.multiple_of(index * plan.rows, 16), plan.rows)


def level_rows(plan, count):
    return slice(count * plan.rows, plan.coded(count))


def read_scales(ref, lead, plan, count, scale_ref):
    level = ref[(*lead, level_rows(plan, count), slice(None))].astype(jnp.int32).astype(F32)
    scale_ref[: plan.levels(count), :] = jnp.exp2(level * (1.0 / STEPS)) * (1.0 / TOP)


def get(ref, lead, plan, index, scale_ref):
    codes = ref[(*lead, at_block(plan, index), slice(None))]
    return codes.astype(jnp.int32).astype(F32) * scale_ref[pl.ds(index, 1), :]


def put(ref, plan, index, block, level_ref):
    codes, level = encode(block)
    ref[at_block(plan, index), :] = codes
    level_ref[pl.ds(index, 1), :] = level


def put_levels(ref, plan, count, level_ref):
    level = level_ref[: plan.levels(count), :]
    ref[level_rows(plan, count), :] = level.astype(jnp.int32).astype(S16)


def send_body(aux_ref, row_ref, col_ref, ext_ref, tiles_ref, out_ref, count_ref, *, layer_blocks):
    out_ref[...] = jnp.zeros(out_ref.shape, BF16)

    @pl.loop(0, OWNERS)
    def _(i):
        count_ref[i] = 0

    lane = lax.broadcasted_iota(jnp.int32, (QUARTER, BS), 1)
    meta_lane = lax.broadcasted_iota(jnp.int32, (8, BS), 1)

    @pl.loop(0, tiles_ref.shape[0])
    def _(i):
        col = col_ref[i]
        layer_of = col // layer_blocks
        kept = col - layer_of * layer_blocks
        owner = (row_ref[i] % 4 * 4 + row_ref[i] // 4) * LAYERS + layer_of
        used = count_ref[owner]
        count_ref[owner] = used + 1
        tile = jnp.where(lane < ext_ref[i], tiles_ref[i].astype(F32), 0.0)
        out_ref[owner, pl.ds(pl.multiple_of(used * QUARTER, QUARTER), QUARTER), :] = tile.astype(BF16)
        old = out_ref[owner, CAP * QUARTER :, :].astype(F32)
        new = jnp.where(meta_lane == used * 2, aux_ref[i].astype(F32), old)
        new = jnp.where(meta_lane == used * 2 + 1, kept.astype(F32), new)
        out_ref[owner, CAP * QUARTER :, :] = new.astype(BF16)


def build_send(tiles, block_aux, block_row, block_col, extents, layer_blocks):
    return pl.pallas_call(
        functools.partial(send_body, layer_blocks=layer_blocks),
        in_specs=[SMEM] * 4 + [VMEM],
        out_specs=VMEM,
        out_shape=jax.ShapeDtypeStruct((OWNERS, CAP * QUARTER + 8, BS), BF16),
        scratch_shapes=[pltpu.SMEM((OWNERS,), jnp.int32)],
        compiler_params=params(8),
        name="build_send",
    )(block_aux, block_row, block_col, extents, tiles)


def split_pieces(place_ref, plan, rows_of, keep_ref, send_refs, level_ref):
    bit_a = place_ref[1]
    bit_b = place_ref[2]

    def piece(a, b):
        return jnp.where(b == 0, a, 3 - a)

    for h, send_ref in enumerate(send_refs):
        kept = [piece(bit_a, o) if h == 0 else piece(o, bit_b) for o in range(2)]
        sent = [piece(1 - bit_a, o) if h == 0 else piece(o, 1 - bit_b) for o in range(2)]

        @pl.loop(0, plan.blocks)
        def _(block):
            first = h * HALF + block * plan.group
            for other in range(2):
                keep_ref[h, other, block] = rows_of(first, kept[other])
                put(send_ref, plan, other * plan.blocks + block, rows_of(first, sent[other]), level_ref)

        put_levels(send_ref, plan, 2 * plan.blocks, level_ref)


def start_all(sources, targets, sems):
    loads = [pltpu.make_async_copy(src, dst, sems.at[i]) for i, (src, dst) in enumerate(zip(sources, targets))]
    for load in loads:
        load.start()
    return loads


def add_virt(meta_ref, first, quarter_refs, green_ref, acc_ref):
    @pl.loop(0, OWNERS // 4)
    def _(step):
        for local in (step * 2, step * 2 + 1):
            for slot in range(CAP):
                span = slice(slot * QUARTER, (slot + 1) * QUARTER)
                tile = jnp.concatenate([ref[local, span, :] for ref in quarter_refs], axis=0)
                aux = meta_ref[first + local, 2 * slot]
                kept = meta_ref[first + local, 2 * slot + 1]
                acc_ref[aux] += jnp.dot(tile, green_ref[kept], preferred_element_type=F32)


def virt_first_body(meta_ref, *rest):
    sources, out_ref, refs, (acc_ref, sems) = rest[:5], rest[5], rest[6:11], rest[11:]
    loads = start_all(sources, refs, sems)
    acc_ref[...] = jnp.zeros(acc_ref.shape, F32)
    for load in loads:
        load.wait()
    add_virt(meta_ref, 0, refs[:4], refs[4], acc_ref)
    store = pltpu.make_async_copy(acc_ref, out_ref, sems.at[0])
    store.start()
    store.wait()


def virt_last_body(meta_ref, place_ref, *rest, plan):
    sources, (keep_ref, send0_ref, send1_ref) = rest[:6], rest[6:9]
    refs, (acc_ref, level_ref, sems) = rest[9:15], rest[15:]
    *loads, before = start_all(sources, refs, sems)
    acc_ref[...] = jnp.zeros(acc_ref.shape, F32)
    for load in loads:
        load.wait()
    add_virt(meta_ref, OWNERS // 2, refs[:4], refs[4], acc_ref)
    before.wait()
    these, those = piece_rows(acc_ref), piece_rows(refs[5])

    def rows_of(first, piece):
        return these(first, piece) + those(first, piece)

    split_pieces(place_ref, plan, rows_of, keep_ref, (send0_ref, send1_ref), level_ref)


def piece_rows(acc_ref):
    def rows_of(first, piece):
        at = [pl.multiple_of(quarter * QUARTER + piece * 8, 8) for quarter in range(4)]
        return jnp.concatenate([acc_ref[first, pl.ds(row, 8), :] for row in at], axis=0)

    return rows_of


def occ_body(meta_ref, place_ref, *rest, plan):
    parts, green_ref, (keep_ref, send0_ref, send1_ref, acc_ref, tile_ref, level_ref) = (rest[:4], rest[4:8]), rest[8], rest[9:]
    acc_ref[...] = jnp.zeros(acc_ref.shape, F32)
    row_place = place_ref[0]
    rows = [pl.multiple_of(((row_place + d) % ROWS) * QUARTER, QUARTER) for d in (0, ROWS - 1, 1, 2)]
    half = OWNERS // 2
    visits = [(j, slot) for j in range(2) for slot in range(CAP)]
    for part in range(2):

        @pl.loop(0, half // 2)
        def _(step):
            for j, slot in visits:
                span = slice(slot * QUARTER, (slot + 1) * QUARTER)
                for ref, row in zip(parts[part], rows):
                    tile_ref[CAP * j + slot, pl.ds(row, QUARTER), :] = ref[step * 2 + j, span, :]
            for j, slot in visits:
                source = part * half + step * 2 + j
                aux = meta_ref[source, 2 * slot]
                kept = meta_ref[source, 2 * slot + 1]
                term = lax.dot_general(
                    green_ref[kept], tile_ref[CAP * j + slot], (((1,), (1,)), ((), ())), preferred_element_type=F32
                )
                for low in range(4):
                    lanes = slice(low * BS, (low + 1) * BS)
                    acc_ref[aux, :, lanes] += term[low * BS : (low + 1) * BS, :]

    split_pieces(place_ref, plan, piece_rows(acc_ref), keep_ref, (send0_ref, send1_ref), level_ref)


VMEM = pl.BlockSpec(memory_space=pltpu.VMEM)
SMEM = pl.BlockSpec(memory_space=pltpu.SMEM)
ANY = pl.BlockSpec(memory_space=pl.ANY)


def step_shapes(plan):
    code = jax.ShapeDtypeStruct((plan.coded(2 * plan.blocks), WIDE), S16)
    return [jax.ShapeDtypeStruct((2, 2, plan.blocks, plan.rows, WIDE), F32), code, code]


def level_scratch(plan):
    return pltpu.VMEM((plan.levels(2 * plan.blocks), WIDE), F32)


ACC = (NP, BS, WIDE)


def scratch_like(operands):
    return [pltpu.VMEM(x.shape, x.dtype) for x in operands]


def contract_virt_first(meta, part, green):
    operands = [*part, green]
    return pl.pallas_call(
        virt_first_body,
        in_specs=[SMEM] + [ANY] * 5,
        out_specs=ANY,
        out_shape=jax.ShapeDtypeStruct(ACC, F32),
        scratch_shapes=scratch_like(operands) + [pltpu.VMEM(ACC, F32), pltpu.SemaphoreType.DMA((5,))],
        compiler_params=params(55),
        name="virt_first",
    )(meta, *operands)


def contract_virt_last(meta, place, part, green, before, plan):
    operands = [*part, green, before]
    return pl.pallas_call(
        functools.partial(virt_last_body, plan=plan),
        in_specs=[SMEM] * 2 + [ANY] * 6,
        out_specs=[VMEM] * 3,
        out_shape=step_shapes(plan),
        scratch_shapes=scratch_like(operands) + [pltpu.VMEM(ACC, F32), level_scratch(plan), pltpu.SemaphoreType.DMA((6,))],
        compiler_params=params(55),
        name="virt_last",
    )(meta, place, *operands)


def contract_occ(meta, place, parts, green, plan):
    return pl.pallas_call(
        functools.partial(occ_body, plan=plan),
        in_specs=[SMEM] * 2 + [VMEM] * 9,
        out_specs=[VMEM] * 3,
        out_shape=step_shapes(plan),
        scratch_shapes=[pltpu.VMEM(ACC, F32), pltpu.VMEM((2 * CAP, BS, BS), BF16), level_scratch(plan)],
        compiler_params=params(28),
        name="contract_occ",
    )(meta, place, *parts[0], *parts[1], green)


def halve_body(place_ref, keep_ref, got0_ref, got1_ref, left_ref, send0_ref, send1_ref, level_ref, scale_ref, *, plan):
    for h, got_ref, send_ref in ((0, got0_ref, send0_ref), (1, got1_ref, send1_ref)):
        mine = place_ref[2 - h]
        away = 1 - mine
        read_scales(got_ref, (), plan, 2 * plan.blocks, scale_ref)

        @pl.loop(0, plan.blocks)
        def _(b):
            left_ref[h, b] = keep_ref[h, mine, b] + get(got_ref, (), plan, mine * plan.blocks + b, scale_ref)
            total = keep_ref[h, away, b] + get(got_ref, (), plan, away * plan.blocks + b, scale_ref)
            put(send_ref, plan, b, total, level_ref)

        put_levels(send_ref, plan, plan.blocks, level_ref)


def halve(place, keep, got0, got1, plan, name):
    code = jax.ShapeDtypeStruct((plan.coded(plan.blocks), WIDE), S16)
    return pl.pallas_call(
        functools.partial(halve_body, plan=plan),
        in_specs=[SMEM] + [VMEM] * 3,
        out_specs=[VMEM] * 3,
        out_shape=[jax.ShapeDtypeStruct((2, plan.blocks, plan.rows, WIDE), F32), code, code],
        scratch_shapes=[level_scratch(plan), level_scratch(plan)],
        compiler_params=params(16),
        name=name,
    )(place, keep, got0, got1)


def finish_blocks(left_ref, got_refs, scale_ref, plan, store):
    for h, got_ref in enumerate(got_refs):
        read_scales(got_ref, (), plan, plan.blocks, scale_ref)

        @pl.loop(0, plan.blocks)
        def _(b):
            store(h * plan.blocks + b, left_ref[h, b] + get(got_ref, (), plan, b, scale_ref))


def finish_virt_body(left_ref, got0_ref, got1_ref, out_ref, level_ref, scale_ref, *, plan):
    def store(index, total):
        put(out_ref, plan, index, total, level_ref)

    finish_blocks(left_ref, (got0_ref, got1_ref), scale_ref, plan, store)
    put_levels(out_ref, plan, 2 * plan.blocks, level_ref)


def finish_occ_body(place_ref, left_ref, got0_ref, got1_ref, *rest, plan):
    out_refs, (code_ref, level_ref, scale_ref) = rest[:4], rest[4:]
    lanes = [pl.ds(pl.multiple_of((place_ref[0] + d) % 4 * BS, BS), BS) for d in range(4)]

    def store(index, total):
        codes, level = encode(total)
        code_ref[...] = codes
        level_ref[pl.ds(index, 1), :] = level
        for out_ref, part in zip(out_refs, lanes):
            out_ref[at_block(plan, index), :] = code_ref[:, part]

    finish_blocks(left_ref, (got0_ref, got1_ref), scale_ref, plan, store)
    for out_ref, part in zip(out_refs, lanes):
        out_ref[level_rows(plan, 2 * plan.blocks), :] = level_ref[:, part].astype(jnp.int32).astype(S16)


def finish_virt(left, got0, got1, plan):
    return pl.pallas_call(
        functools.partial(finish_virt_body, plan=plan),
        in_specs=[VMEM] * 3,
        out_specs=VMEM,
        out_shape=jax.ShapeDtypeStruct((plan.coded(2 * plan.blocks), WIDE), S16),
        scratch_shapes=[level_scratch(plan), level_scratch(plan)],
        compiler_params=params(12),
        name="finish_virt",
    )(left, got0, got1)


def finish_occ(place, left, got0, got1, plan):
    part = jax.ShapeDtypeStruct((plan.coded(2 * plan.blocks), BS), S16)
    return pl.pallas_call(
        functools.partial(finish_occ_body, plan=plan),
        in_specs=[SMEM] + [VMEM] * 3,
        out_specs=[VMEM] * 4,
        out_shape=[part] * 4,
        scratch_shapes=[pltpu.VMEM((plan.rows, WIDE), S16), level_scratch(plan), level_scratch(plan)],
        compiler_params=params(12),
        name="finish_occ",
    )(place, left, got0, got1)


def pair_body(place_ref, own_ref, one_ref, two_ref, three_ref, virt_ref, out_ref, occ_ref, vir_ref, wide_ref, thin_ref, *, plan):
    here = place_ref[0]
    high = place_ref[1]
    count = 2 * plan.blocks

    at = [((high + shift) % 4) * 8 for shift in (0, ROWS - 1, 1, 2)]
    read_scales(virt_ref, (), plan, count, wide_ref)

    @pl.loop(0, NP)
    def _(q):
        values = get(virt_ref, (), plan, q, wide_ref)
        for quarter in range(4):
            for low in range(4):
                to = pl.ds(pl.multiple_of(low * QUARTER + at[quarter], 8), 8)
                vir_ref[q, to, :] = values[quarter * 8 : (quarter + 1) * 8, low * BS : (low + 1) * BS]

    for d, ref in enumerate((own_ref, one_ref, two_ref, three_ref)):
        source = (here + 4 - d) % 4
        read_scales(ref, (), plan, count, thin_ref)
        rows = pl.ds(pl.multiple_of(source * QUARTER, QUARTER), QUARTER)

        @pl.loop(0, NP)
        def _(p):
            occ_ref[p, rows, :] = get(ref, (), plan, p, thin_ref)

    @pl.loop(0, NP)
    def _(p):
        occ = occ_ref[p]
        for q in range(NP):
            out_ref[p, q : q + 1, :] = jnp.sum(occ * vir_ref[q], axis=0, keepdims=True)


def pair(place, own, others, virt, plan):
    levels = plan.levels(2 * plan.blocks)
    return pl.pallas_call(
        functools.partial(pair_body, plan=plan),
        in_specs=[SMEM] + [VMEM] * 5,
        out_specs=VMEM,
        out_shape=jax.ShapeDtypeStruct((NP, NP, BS), F32),
        scratch_shapes=[
            pltpu.VMEM((NP, BS, BS), F32),
            pltpu.VMEM((NP, BS, BS), F32),
            pltpu.VMEM((levels, WIDE), F32),
            pltpu.VMEM((levels, BS), F32),
        ],
        compiler_params=params(16),
        name="pair",
    )(place, own, *others, virt)


def rotate(size, step):
    return [(i, (i + step) % size) for i in range(size)]


def rotate_high(step):
    return [(c, (c + 4 * step) % COLS) for c in range(COLS)]


PAIRS_A = [(0, 1), (1, 0), (2, 3), (3, 2)]
PAIRS_B = [(0, 3), (3, 0), (1, 2), (2, 1)]


def index_of(row, col, layer):
    return (row * COLS + col) * LAYERS + layer


SWAP = [
    (index_of(r, c, l), index_of(c % 4, c // 4 * 4 + r, l))
    for r in range(ROWS)
    for c in range(COLS)
    for l in range(LAYERS)
]


def sum_all(values):
    for axes in ("col", ("row", "layer")):
        copies = jnp.broadcast_to(values[None], (16, *values.shape))
        values = jnp.sum(lax.all_to_all(copies, axes, 0, 0, tiled=True), axis=0)
    return values


def layer_swap(send0, send1, perms):
    return lax.ppermute(send0, "layer", perms[0]), lax.ppermute(send1, "layer", perms[1])


FIRST = (PAIRS_A, PAIRS_B)
SECOND = (PAIRS_B, PAIRS_A)


def after(*values):
    return lax.optimization_barrier(values)


def on_device(blocks, block_aux, block_row, block_col, extents, occ_green, virt_green):
    layer_blocks = occ_green.shape[0] // BS
    row_place = lax.axis_index("row").astype(jnp.int32)
    col_place = lax.axis_index("col").astype(jnp.int32)
    layer_place = lax.axis_index("layer").astype(jnp.int32)
    bit_a = ((layer_place == 1) | (layer_place == 2)).astype(jnp.int32)
    bit_b = layer_place // 2
    place = jnp.stack([row_place, bit_a, bit_b])
    plan = Plan(4)

    tiles = lax.dynamic_slice_in_dim(blocks, row_place * QUARTER, QUARTER, 1)
    send = build_send(tiles, block_aux, block_row, block_col, extents, layer_blocks)
    own = lax.all_to_all(send, ("col", "layer"), 0, 0, tiled=True)
    meta = own[:, CAP * QUARTER, : 2 * CAP].astype(jnp.int32)
    virt_blocks = virt_green.reshape(layer_blocks, BS, WIDE)
    occ_blocks = occ_green.reshape(layer_blocks, BS, WIDE).transpose(0, 2, 1)

    half = OWNERS // 2
    own_a, own_b = own[:half, : CAP * QUARTER], own[half:, : CAP * QUARTER]
    up, down = rotate(ROWS, 1), rotate(ROWS, -1)
    prev_a = lax.ppermute(own_a, "row", up)
    next_a = lax.ppermute(own_a, "row", down)
    prev_a, next_a, own_b, occ_blocks, meta = after(prev_a, next_a, own_b, occ_blocks, meta)
    far_a = lax.ppermute(prev_a, "row", up)
    next_b = lax.ppermute(own_b, "row", down)
    far_a, next_b, own_b = after(far_a, next_b, own_b)
    prev_b = lax.ppermute(own_b, "row", up)
    far_b = lax.ppermute(next_b, "row", down)
    part_a, part_b = (own_a, prev_a, next_a, far_a), (own_b, prev_b, next_b, far_b)

    v_acc = contract_virt_first(meta, part_a, virt_blocks)
    v_keep, v0, v1 = contract_virt_last(meta, place, part_b, virt_blocks, v_acc, plan)
    v_got = layer_swap(v0, v1, FIRST)
    occ_blocks, v_keep = after(occ_blocks, v_keep)
    o_keep, o0, o1 = contract_occ(meta, place, (part_a, part_b), occ_blocks, plan)
    v_keep, o_keep = after(v_keep, o_keep)
    v_left, v0, v1 = halve(place, v_keep, *v_got, plan, "halve_virt")
    v_got = layer_swap(v0, v1, SECOND)
    o0, o1, *v_got = after(o0, o1, *v_got)
    o_got = layer_swap(o0, o1, FIRST)
    virt = finish_virt(v_left, *v_got, plan)
    virt, o_keep = after(virt, o_keep)
    virt = lax.ppermute(virt, ALL, SWAP)
    o_left, o0, o1 = halve(place, o_keep, *o_got, plan, "halve_occ")
    o_got = layer_swap(o0, o1, SECOND)
    here = jnp.stack([col_place // 4, col_place % 4])
    occ, *others = finish_occ(here, o_left, *o_got, plan)
    others = [lax.ppermute(part, "col", rotate_high(d)) for d, part in zip((1, 2, 3), others)]
    partial = pair(here, occ, others, virt, plan)
    return sum_all(jnp.sum(partial, axis=-1))


def solution(mesh):
    in_specs = (
        P(("col", "layer"), None, None),
        P(("col", "layer")),
        P(("col", "layer")),
        P(("col", "layer")),
        P(("col", "layer")),
        P("layer", "row"),
        P("layer", "row"),
    )
    return jax.shard_map(on_device, mesh=mesh, in_specs=in_specs, out_specs=P(), check_vma=False)
```

```python
import functools

import jax
import jax.numpy as jnp
from jax import lax
from jax.experimental import pallas as pl
from jax.experimental.pallas import tpu as pltpu
from jax.sharding import PartitionSpec as P

NP = 24
ROWS = 4
COLS = 16
LAYERS = 4
CAP = 2
OWNERS = COLS * LAYERS
BS = 128
QUARTER = BS // ROWS
WIDE = 512
HALF = NP // 2
TOP = 32700.0
STEPS = 64.0
ALL = ("row", "col", "layer")
F32 = jnp.float32
BF16 = jnp.bfloat16
S16 = jnp.int16


def params(mib):
    return pltpu.CompilerParams(vmem_limit_bytes=mib * 2**20)


def encode(block):
    peak = jnp.max(jnp.abs(block), axis=0, keepdims=True)
    level = jnp.ceil(jnp.log2(jnp.maximum(peak, 1e-30)) * STEPS)
    scaled = block * (jnp.exp2(level * (-1.0 / STEPS)) * TOP)
    return jnp.round(scaled).astype(jnp.int32).astype(S16), level


def decode(codes, level):
    return codes.astype(jnp.int32).astype(F32) * (jnp.exp2(level * (1.0 / STEPS)) * (1.0 / TOP))


class Plan:
    def __init__(self, quarters):
        self.quarters = quarters
        self.group = 4 // quarters
        self.rows = 8 * quarters * self.group
        self.blocks = HALF // self.group

    def levels(self, count):
        return (count + 15) // 16 * 16

    def coded(self, count):
        return count * self.rows + self.levels(count)


def at_block(plan, index):
    return pl.ds(pl.multiple_of(index * plan.rows, 16), plan.rows)


def level_rows(plan, count):
    return slice(count * plan.rows, plan.coded(count))


def read_scales(ref, lead, plan, count, scale_ref):
    level = ref[(*lead, level_rows(plan, count), slice(None))].astype(jnp.int32).astype(F32)
    scale_ref[: plan.levels(count), :] = jnp.exp2(level * (1.0 / STEPS)) * (1.0 / TOP)


def get(ref, lead, plan, index, scale_ref):
    codes = ref[(*lead, at_block(plan, index), slice(None))]
    return codes.astype(jnp.int32).astype(F32) * scale_ref[pl.ds(index, 1), :]


def put(ref, plan, index, block, level_ref):
    codes, level = encode(block)
    ref[at_block(plan, index), :] = codes
    level_ref[pl.ds(index, 1), :] = level


def put_levels(ref, plan, count, level_ref):
    level = level_ref[: plan.levels(count), :]
    ref[level_rows(plan, count), :] = level.astype(jnp.int32).astype(S16)


def send_body(
    aux_ref, row_ref, col_ref, ext_ref, place_ref, blocks_ref, out_ref, count_ref, tiles_ref, sem, *, layer_blocks
):
    rows = pl.ds(pl.multiple_of(place_ref[0] * QUARTER, QUARTER), QUARTER)
    load = pltpu.make_async_copy(blocks_ref.at[:, rows, :], tiles_ref, sem)
    load.start()
    out_ref[...] = jnp.zeros(out_ref.shape, BF16)

    @pl.loop(0, OWNERS)
    def _(i):
        count_ref[i] = 0

    lane = lax.broadcasted_iota(jnp.int32, (QUARTER, BS), 1)
    meta_lane = lax.broadcasted_iota(jnp.int32, (8, BS), 1)
    load.wait()

    @pl.loop(0, tiles_ref.shape[0])
    def _(i):
        col = col_ref[i]
        layer_of = col // layer_blocks
        kept = col - layer_of * layer_blocks
        owner = (row_ref[i] % 4 * 4 + row_ref[i] // 4) * LAYERS + layer_of
        used = count_ref[owner]
        count_ref[owner] = used + 1
        tile = jnp.where(lane < ext_ref[i], tiles_ref[i].astype(F32), 0.0)
        out_ref[owner, pl.ds(pl.multiple_of(used * QUARTER, QUARTER), QUARTER), :] = tile.astype(BF16)
        old = out_ref[owner, CAP * QUARTER :, :].astype(F32)
        new = jnp.where(meta_lane == used * 2, aux_ref[i].astype(F32), old)
        new = jnp.where(meta_lane == used * 2 + 1, kept.astype(F32), new)
        out_ref[owner, CAP * QUARTER :, :] = new.astype(BF16)


def build_send(blocks, block_aux, block_row, block_col, extents, place, layer_blocks):
    return pl.pallas_call(
        functools.partial(send_body, layer_blocks=layer_blocks),
        in_specs=[SMEM] * 5 + [ANY],
        out_specs=VMEM,
        out_shape=jax.ShapeDtypeStruct((OWNERS, CAP * QUARTER + 8, BS), BF16),
        scratch_shapes=[
            pltpu.SMEM((OWNERS,), jnp.int32),
            pltpu.VMEM((blocks.shape[0], QUARTER, BS), BF16),
            pltpu.SemaphoreType.DMA(()),
        ],
        compiler_params=params(60),
        name="build_send",
    )(block_aux, block_row, block_col, extents, place, blocks)


def split_pieces(place_ref, plan, rows_of, keep_ref, send_refs, level_ref):
    bit_a = place_ref[1]
    bit_b = place_ref[2]

    def piece(a, b):
        return jnp.where(b == 0, a, 3 - a)

    for h, send_ref in enumerate(send_refs):
        kept = [piece(bit_a, o) if h == 0 else piece(o, bit_b) for o in range(2)]
        sent = [piece(1 - bit_a, o) if h == 0 else piece(o, 1 - bit_b) for o in range(2)]

        @pl.loop(0, plan.blocks, unroll=2)
        def _(block):
            first = h * HALF + block * plan.group
            for other in range(2):
                keep_ref[h, other, block] = rows_of(first, kept[other])
                put(send_ref, plan, other * plan.blocks + block, rows_of(first, sent[other]), level_ref)

        put_levels(send_ref, plan, 2 * plan.blocks, level_ref)


def start_all(sources, targets, sems):
    loads = [pltpu.make_async_copy(src, dst, sems.at[i]) for i, (src, dst) in enumerate(zip(sources, targets))]
    for load in loads:
        load.start()
    return loads


def add_virt(meta_ref, first, quarter_refs, green_ref, acc_ref):
    @pl.loop(0, OWNERS // 4)
    def _(step):
        for local in (step * 2, step * 2 + 1):
            for slot in range(CAP):
                span = slice(slot * QUARTER, (slot + 1) * QUARTER)
                tile = jnp.concatenate([ref[local, span, :] for ref in quarter_refs], axis=0)
                aux = meta_ref[first + local, 2 * slot]
                kept = meta_ref[first + local, 2 * slot + 1]
                acc_ref[aux] += jnp.dot(tile, green_ref[kept], preferred_element_type=F32)


def virt_first_body(meta_ref, *rest):
    sources, out_ref, refs, (acc_ref, sems) = rest[:5], rest[5], rest[6:11], rest[11:]
    loads = start_all(sources, refs, sems)
    acc_ref[...] = jnp.zeros(acc_ref.shape, F32)
    for load in loads:
        load.wait()
    add_virt(meta_ref, 0, refs[:4], refs[4], acc_ref)
    store = pltpu.make_async_copy(acc_ref, out_ref, sems.at[0])
    store.start()
    store.wait()


def virt_last_body(meta_ref, place_ref, *rest, plan):
    sources, (keep_ref, send0_ref, send1_ref) = rest[:6], rest[6:9]
    refs, (acc_ref, level_ref, sems) = rest[9:15], rest[15:]
    loads = start_all(sources[:5], refs, sems)
    acc_ref[...] = jnp.zeros(acc_ref.shape, F32)
    for load in loads:
        load.wait()
    before = pltpu.make_async_copy(sources[5], refs[5], sems.at[5])
    before.start()
    add_virt(meta_ref, OWNERS // 2, refs[:4], refs[4], acc_ref)
    before.wait()
    these, those = piece_rows(acc_ref), piece_rows(refs[5])

    def rows_of(first, piece):
        return these(first, piece) + those(first, piece)

    split_pieces(place_ref, plan, rows_of, keep_ref, (send0_ref, send1_ref), level_ref)


def piece_rows(acc_ref):
    def rows_of(first, piece):
        at = [pl.multiple_of(quarter * QUARTER + piece * 8, 8) for quarter in range(4)]
        return jnp.concatenate([acc_ref[first, pl.ds(row, 8), :] for row in at], axis=0)

    return rows_of


def occ_body(meta_ref, place_ref, *rest, plan):
    parts, green_ref, (keep_ref, send0_ref, send1_ref, acc_ref, tile_ref, level_ref) = (rest[:4], rest[4:8]), rest[8], rest[9:]
    acc_ref[...] = jnp.zeros(acc_ref.shape, F32)
    row_place = place_ref[0]
    rows = [pl.multiple_of(((row_place + d) % ROWS) * QUARTER, QUARTER) for d in (0, ROWS - 1, 1, 2)]
    half = OWNERS // 2
    visits = [(j, slot) for j in range(2) for slot in range(CAP)]
    for part in range(2):

        @pl.loop(0, half // 2)
        def _(step):
            for j, slot in visits:
                span = slice(slot * QUARTER, (slot + 1) * QUARTER)
                for ref, row in zip(parts[part], rows):
                    tile_ref[CAP * j + slot, pl.ds(row, QUARTER), :] = ref[step * 2 + j, span, :]
            for j, slot in visits:
                source = part * half + step * 2 + j
                aux = meta_ref[source, 2 * slot]
                kept = meta_ref[source, 2 * slot + 1]
                term = lax.dot_general(
                    green_ref[kept], tile_ref[CAP * j + slot], (((1,), (1,)), ((), ())), preferred_element_type=F32
                )
                for low in range(4):
                    lanes = slice(low * BS, (low + 1) * BS)
                    acc_ref[aux, :, lanes] += term[low * BS : (low + 1) * BS, :]

    split_pieces(place_ref, plan, piece_rows(acc_ref), keep_ref, (send0_ref, send1_ref), level_ref)


VMEM = pl.BlockSpec(memory_space=pltpu.VMEM)
SMEM = pl.BlockSpec(memory_space=pltpu.SMEM)
ANY = pl.BlockSpec(memory_space=pl.ANY)


def step_shapes(plan):
    code = jax.ShapeDtypeStruct((plan.coded(2 * plan.blocks), WIDE), S16)
    return [jax.ShapeDtypeStruct((2, 2, plan.blocks, plan.rows, WIDE), F32), code, code]


def level_scratch(plan):
    return pltpu.VMEM((plan.levels(2 * plan.blocks), WIDE), F32)


ACC = (NP, BS, WIDE)


def scratch_like(operands):
    return [pltpu.VMEM(x.shape, x.dtype) for x in operands]


def contract_virt_first(meta, part, green):
    operands = [*part, green]
    return pl.pallas_call(
        virt_first_body,
        in_specs=[SMEM] + [ANY] * 5,
        out_specs=ANY,
        out_shape=jax.ShapeDtypeStruct(ACC, F32),
        scratch_shapes=scratch_like(operands) + [pltpu.VMEM(ACC, F32), pltpu.SemaphoreType.DMA((5,))],
        compiler_params=params(55),
        name="virt_first",
    )(meta, *operands)


def contract_virt_last(meta, place, part, green, before, plan):
    operands = [*part, green, before]
    return pl.pallas_call(
        functools.partial(virt_last_body, plan=plan),
        in_specs=[SMEM] * 2 + [ANY] * 6,
        out_specs=[VMEM] * 3,
        out_shape=step_shapes(plan),
        scratch_shapes=scratch_like(operands) + [pltpu.VMEM(ACC, F32), level_scratch(plan), pltpu.SemaphoreType.DMA((6,))],
        compiler_params=params(55),
        name="virt_last",
    )(meta, place, *operands)


def contract_occ(meta, place, parts, green, plan):
    return pl.pallas_call(
        functools.partial(occ_body, plan=plan),
        in_specs=[SMEM] * 2 + [VMEM] * 9,
        out_specs=[VMEM] * 3,
        out_shape=step_shapes(plan),
        scratch_shapes=[pltpu.VMEM(ACC, F32), pltpu.VMEM((2 * CAP, BS, BS), BF16), level_scratch(plan)],
        compiler_params=params(28),
        name="contract_occ",
    )(meta, place, *parts[0], *parts[1], green)


def halve_body(place_ref, keep_ref, got0_ref, got1_ref, left_ref, send0_ref, send1_ref, level_ref, scale_ref, *, plan):
    for h, got_ref, send_ref in ((0, got0_ref, send0_ref), (1, got1_ref, send1_ref)):
        mine = place_ref[2 - h]
        away = 1 - mine
        read_scales(got_ref, (), plan, 2 * plan.blocks, scale_ref)

        @pl.loop(0, plan.blocks, unroll=2)
        def _(b):
            left_ref[h, b] = keep_ref[h, mine, b] + get(got_ref, (), plan, mine * plan.blocks + b, scale_ref)
            total = keep_ref[h, away, b] + get(got_ref, (), plan, away * plan.blocks + b, scale_ref)
            put(send_ref, plan, b, total, level_ref)

        put_levels(send_ref, plan, plan.blocks, level_ref)


def halve(place, keep, got0, got1, plan, name):
    code = jax.ShapeDtypeStruct((plan.coded(plan.blocks), WIDE), S16)
    return pl.pallas_call(
        functools.partial(halve_body, plan=plan),
        in_specs=[SMEM] + [VMEM] * 3,
        out_specs=[VMEM] * 3,
        out_shape=[jax.ShapeDtypeStruct((2, plan.blocks, plan.rows, WIDE), F32), code, code],
        scratch_shapes=[level_scratch(plan), level_scratch(plan)],
        compiler_params=params(16),
        name=name,
    )(place, keep, got0, got1)


def finish_blocks(left_ref, got_refs, scale_ref, plan, store):
    for h, got_ref in enumerate(got_refs):
        read_scales(got_ref, (), plan, plan.blocks, scale_ref)

        @pl.loop(0, plan.blocks, unroll=2)
        def _(b):
            store(h * plan.blocks + b, left_ref[h, b] + get(got_ref, (), plan, b, scale_ref))


def finish_virt_body(left_ref, got0_ref, got1_ref, out_ref, level_ref, scale_ref, *, plan):
    def store(index, total):
        put(out_ref, plan, index, total, level_ref)

    finish_blocks(left_ref, (got0_ref, got1_ref), scale_ref, plan, store)
    put_levels(out_ref, plan, 2 * plan.blocks, level_ref)


def finish_occ_body(place_ref, left_ref, got0_ref, got1_ref, *rest, plan):
    out_refs, (code_ref, level_ref, scale_ref) = rest[:4], rest[4:]
    lanes = [pl.ds(pl.multiple_of((place_ref[0] + d) % 4 * BS, BS), BS) for d in range(4)]

    def store(index, total):
        codes, level = encode(total)
        code_ref[...] = codes
        level_ref[pl.ds(index, 1), :] = level
        for out_ref, part in zip(out_refs, lanes):
            out_ref[at_block(plan, index), :] = code_ref[:, part]

    finish_blocks(left_ref, (got0_ref, got1_ref), scale_ref, plan, store)
    for out_ref, part in zip(out_refs, lanes):
        out_ref[level_rows(plan, 2 * plan.blocks), :] = level_ref[:, part].astype(jnp.int32).astype(S16)


def finish_virt(left, got0, got1, plan):
    return pl.pallas_call(
        functools.partial(finish_virt_body, plan=plan),
        in_specs=[VMEM] * 3,
        out_specs=VMEM,
        out_shape=jax.ShapeDtypeStruct((plan.coded(2 * plan.blocks), WIDE), S16),
        scratch_shapes=[level_scratch(plan), level_scratch(plan)],
        compiler_params=params(12),
        name="finish_virt",
    )(left, got0, got1)


def finish_occ(place, left, got0, got1, plan):
    part = jax.ShapeDtypeStruct((plan.coded(2 * plan.blocks), BS), S16)
    return pl.pallas_call(
        functools.partial(finish_occ_body, plan=plan),
        in_specs=[SMEM] + [VMEM] * 3,
        out_specs=[VMEM] * 4,
        out_shape=[part] * 4,
        scratch_shapes=[pltpu.VMEM((plan.rows, WIDE), S16), level_scratch(plan), level_scratch(plan)],
        compiler_params=params(12),
        name="finish_occ",
    )(place, left, got0, got1)


def decode_virt_body(place_ref, virt_ref, vir_ref, scale_ref, *, plan):
    at = [((place_ref[1] + shift) % 4) * 8 for shift in (0, ROWS - 1, 1, 2)]
    read_scales(virt_ref, (), plan, 2 * plan.blocks, scale_ref)

    @pl.loop(0, NP, unroll=2)
    def _(q):
        values = get(virt_ref, (), plan, q, scale_ref)
        for quarter in range(4):
            for low in range(4):
                to = pl.ds(pl.multiple_of(low * QUARTER + at[quarter], 8), 8)
                vir_ref[q, to, :] = values[quarter * 8 : (quarter + 1) * 8, low * BS : (low + 1) * BS]


def decode_virt(place, virt, plan):
    return pl.pallas_call(
        functools.partial(decode_virt_body, plan=plan),
        in_specs=[SMEM, VMEM],
        out_specs=VMEM,
        out_shape=jax.ShapeDtypeStruct((NP, BS, BS), F32),
        scratch_shapes=[level_scratch(plan)],
        compiler_params=params(8),
        name="decode_virt",
    )(place, virt)


def pair_body(place_ref, own_ref, one_ref, two_ref, three_ref, vir_ref, out_ref, occ_ref, scale_ref, *, plan):
    here = place_ref[0]

    for d, ref in enumerate((own_ref, one_ref, two_ref, three_ref)):
        source = (here + 4 - d) % 4
        read_scales(ref, (), plan, 2 * plan.blocks, scale_ref)
        rows = pl.ds(pl.multiple_of(source * QUARTER, QUARTER), QUARTER)

        @pl.loop(0, NP, unroll=4)
        def _(p):
            occ_ref[p, rows, :] = get(ref, (), plan, p, scale_ref)

    @pl.loop(0, NP)
    def _(p):
        occ = occ_ref[p]
        for q in range(NP):
            out_ref[p, q : q + 1, :] = jnp.sum(occ * vir_ref[q], axis=0, keepdims=True)


def pair(place, own, others, vir, plan):
    return pl.pallas_call(
        functools.partial(pair_body, plan=plan),
        in_specs=[SMEM] + [VMEM] * 5,
        out_specs=VMEM,
        out_shape=jax.ShapeDtypeStruct((NP, NP, BS), F32),
        scratch_shapes=[pltpu.VMEM((NP, BS, BS), F32), pltpu.VMEM((plan.levels(2 * plan.blocks), BS), F32)],
        compiler_params=params(16),
        name="pair",
    )(place, own, *others, vir)


def rotate(size, step):
    return [(i, (i + step) % size) for i in range(size)]


def rotate_high(step):
    return [(c, (c + 4 * step) % COLS) for c in range(COLS)]


PAIRS_A = [(0, 1), (1, 0), (2, 3), (3, 2)]
PAIRS_B = [(0, 3), (3, 0), (1, 2), (2, 1)]


def index_of(row, col, layer):
    return (row * COLS + col) * LAYERS + layer


SWAP = [
    (index_of(r, c, l), index_of(c % 4, c // 4 * 4 + r, l))
    for r in range(ROWS)
    for c in range(COLS)
    for l in range(LAYERS)
]


def sum_all(values):
    for axes in ("col", ("row", "layer")):
        copies = jnp.broadcast_to(values[None], (16, *values.shape))
        values = jnp.sum(lax.all_to_all(copies, axes, 0, 0, tiled=True), axis=0)
    return values


def layer_swap(send0, send1, perms):
    return lax.ppermute(send0, "layer", perms[0]), lax.ppermute(send1, "layer", perms[1])


FIRST = (PAIRS_A, PAIRS_B)
SECOND = (PAIRS_B, PAIRS_A)


def after(*values):
    return lax.optimization_barrier(values)


def on_device(blocks, block_aux, block_row, block_col, extents, occ_green, virt_green):
    layer_blocks = occ_green.shape[0] // BS
    row_place = lax.axis_index("row").astype(jnp.int32)
    col_place = lax.axis_index("col").astype(jnp.int32)
    layer_place = lax.axis_index("layer").astype(jnp.int32)
    bit_a = ((layer_place == 1) | (layer_place == 2)).astype(jnp.int32)
    bit_b = layer_place // 2
    place = jnp.stack([row_place, bit_a, bit_b])
    plan = Plan(4)

    send = build_send(blocks, block_aux, block_row, block_col, extents, row_place[None], layer_blocks)
    own = lax.all_to_all(send, ("col", "layer"), 0, 0, tiled=True)
    virt_blocks = virt_green.reshape(layer_blocks, BS, WIDE)
    occ_blocks = occ_green.reshape(layer_blocks, BS, WIDE).transpose(0, 2, 1)

    half = OWNERS // 2
    own_a = own[:half, : CAP * QUARTER]
    later, occ_blocks = after(own, occ_blocks)
    own_b = later[half:, : CAP * QUARTER]
    meta = later[:, CAP * QUARTER, : 2 * CAP].astype(jnp.int32)
    up, down = rotate(ROWS, 1), rotate(ROWS, -1)
    prev_a = lax.ppermute(own_a, "row", up)
    next_a = lax.ppermute(own_a, "row", down)
    prev_a, next_a, own_b, occ_blocks, meta = after(prev_a, next_a, own_b, occ_blocks, meta)
    far_a = lax.ppermute(prev_a, "row", up)
    next_b = lax.ppermute(own_b, "row", down)
    far_a, next_b, own_b = after(far_a, next_b, own_b)
    prev_b = lax.ppermute(own_b, "row", up)
    far_b = lax.ppermute(next_b, "row", down)
    part_a, part_b = (own_a, prev_a, next_a, far_a), (own_b, prev_b, next_b, far_b)

    v_acc = contract_virt_first(meta, part_a, virt_blocks)
    v_keep, v0, v1 = contract_virt_last(meta, place, part_b, virt_blocks, v_acc, plan)
    v_got = layer_swap(v0, v1, FIRST)
    occ_blocks, v_keep = after(occ_blocks, v_keep)
    o_keep, o0, o1 = contract_occ(meta, place, (part_a, part_b), occ_blocks, plan)
    v_keep, o_keep = after(v_keep, o_keep)
    v_left, v0, v1 = halve(place, v_keep, *v_got, plan, "halve_virt")
    v_got = layer_swap(v0, v1, SECOND)
    o0, o1, *v_got = after(o0, o1, *v_got)
    o_got = layer_swap(o0, o1, FIRST)
    virt = finish_virt(v_left, *v_got, plan)
    virt, o_keep = after(virt, o_keep)
    virt = lax.ppermute(virt, ALL, SWAP)
    o_left, o0, o1 = halve(place, o_keep, *o_got, plan, "halve_occ")
    o_got = layer_swap(o0, o1, SECOND)
    here = jnp.stack([col_place // 4, col_place % 4])
    occ, *others = finish_occ(here, o_left, *o_got, plan)
    others = [lax.ppermute(part, "col", rotate_high(d)) for d, part in zip((1, 2, 3), others)]
    partial = pair(here, occ, others, decode_virt(here, virt, plan), plan)
    return sum_all(jnp.sum(partial, axis=-1))


def solution(mesh):
    in_specs = (
        P(("col", "layer"), None, None),
        P(("col", "layer")),
        P(("col", "layer")),
        P(("col", "layer")),
        P(("col", "layer")),
        P("layer", "row"),
        P("layer", "row"),
    )
    return jax.shard_map(on_device, mesh=mesh, in_specs=in_specs, out_specs=P(), check_vma=False)
```

```python
import functools

import jax
import jax.numpy as jnp
from jax import lax
from jax.experimental import pallas as pl
from jax.experimental.pallas import tpu as pltpu
from jax.sharding import PartitionSpec as P

NP = 24
ROWS = 4
COLS = 16
LAYERS = 4
CAP = 2
OWNERS = COLS * LAYERS
BS = 128
QUARTER = BS // ROWS
WIDE = 512
HALF = NP // 2
TOP = 32700.0
STEPS = 64.0
ALL = ("row", "col", "layer")
F32 = jnp.float32
BF16 = jnp.bfloat16
S16 = jnp.int16


def params(mib):
    return pltpu.CompilerParams(vmem_limit_bytes=mib * 2**20)


def encode(block):
    peak = jnp.max(jnp.abs(block), axis=0, keepdims=True)
    level = jnp.ceil(jnp.log2(jnp.maximum(peak, 1e-30)) * STEPS)
    scaled = block * (jnp.exp2(level * (-1.0 / STEPS)) * TOP)
    return jnp.round(scaled).astype(jnp.int32).astype(S16), level


def decode(codes, level):
    return codes.astype(jnp.int32).astype(F32) * (jnp.exp2(level * (1.0 / STEPS)) * (1.0 / TOP))


class Plan:
    def __init__(self, quarters, parts=1):
        self.quarters = quarters
        self.parts = parts
        self.group = 4 // quarters
        self.rows = 8 * quarters * self.group
        self.blocks = HALF // self.group // parts

    def levels(self, count):
        return (count + 15) // 16 * 16

    def coded(self, count):
        return count * self.rows + self.levels(count)


def at_block(plan, index):
    return pl.ds(pl.multiple_of(index * plan.rows, 16), plan.rows)


def level_rows(plan, count):
    return slice(count * plan.rows, plan.coded(count))


def read_scales(ref, lead, plan, count, scale_ref):
    level = ref[(*lead, level_rows(plan, count), slice(None))].astype(jnp.int32).astype(F32)
    scale_ref[: plan.levels(count), :] = jnp.exp2(level * (1.0 / STEPS)) * (1.0 / TOP)


def get(ref, lead, plan, index, scale_ref):
    codes = ref[(*lead, at_block(plan, index), slice(None))]
    return codes.astype(jnp.int32).astype(F32) * scale_ref[pl.ds(index, 1), :]


def put(ref, plan, index, block, level_ref):
    codes, level = encode(block)
    ref[at_block(plan, index), :] = codes
    level_ref[pl.ds(index, 1), :] = level


def put_levels(ref, plan, count, level_ref):
    level = level_ref[: plan.levels(count), :]
    ref[level_rows(plan, count), :] = level.astype(jnp.int32).astype(S16)


def send_body(
    aux_ref, row_ref, col_ref, ext_ref, place_ref, blocks_ref, out_ref, count_ref, tiles_ref, sem, *, layer_blocks
):
    rows = pl.ds(pl.multiple_of(place_ref[0] * QUARTER, QUARTER), QUARTER)
    load = pltpu.make_async_copy(blocks_ref.at[:, rows, :], tiles_ref, sem)
    load.start()
    out_ref[...] = jnp.zeros(out_ref.shape, BF16)

    @pl.loop(0, OWNERS)
    def _(i):
        count_ref[i] = 0

    lane = lax.broadcasted_iota(jnp.int32, (QUARTER, BS), 1)
    meta_lane = lax.broadcasted_iota(jnp.int32, (8, BS), 1)
    load.wait()

    @pl.loop(0, tiles_ref.shape[0])
    def _(i):
        col = col_ref[i]
        layer_of = col // layer_blocks
        kept = col - layer_of * layer_blocks
        owner = (row_ref[i] % 4 * 4 + row_ref[i] // 4) * LAYERS + layer_of
        used = count_ref[owner]
        count_ref[owner] = used + 1
        tile = jnp.where(lane < ext_ref[i], tiles_ref[i].astype(F32), 0.0)
        out_ref[owner, pl.ds(pl.multiple_of(used * QUARTER, QUARTER), QUARTER), :] = tile.astype(BF16)
        old = out_ref[owner, CAP * QUARTER :, :].astype(F32)
        new = jnp.where(meta_lane == used * 2, aux_ref[i].astype(F32), old)
        new = jnp.where(meta_lane == used * 2 + 1, kept.astype(F32), new)
        out_ref[owner, CAP * QUARTER :, :] = new.astype(BF16)


def build_send(blocks, block_aux, block_row, block_col, extents, place, layer_blocks):
    return pl.pallas_call(
        functools.partial(send_body, layer_blocks=layer_blocks),
        in_specs=[SMEM] * 5 + [ANY],
        out_specs=VMEM,
        out_shape=jax.ShapeDtypeStruct((OWNERS, CAP * QUARTER + 8, BS), BF16),
        scratch_shapes=[
            pltpu.SMEM((OWNERS,), jnp.int32),
            pltpu.VMEM((blocks.shape[0], QUARTER, BS), BF16),
            pltpu.SemaphoreType.DMA(()),
        ],
        compiler_params=params(60),
        name="build_send",
    )(block_aux, block_row, block_col, extents, place, blocks)


def split_pieces(place_ref, plan, rows_of, out_refs, level_ref):
    bit_a = place_ref[1]
    bit_b = place_ref[2]

    def piece(a, b):
        return jnp.where(b == 0, a, 3 - a)

    for part in range(plan.parts):
        keep_ref, *send_refs = out_refs[3 * part : 3 * part + 3]
        for h, send_ref in enumerate(send_refs):
            kept = [piece(bit_a, o) if h == 0 else piece(o, bit_b) for o in range(2)]
            sent = [piece(1 - bit_a, o) if h == 0 else piece(o, 1 - bit_b) for o in range(2)]

            @pl.loop(0, plan.blocks, unroll=2)
            def _(block):
                first = h * HALF + (part * plan.blocks + block) * plan.group
                for other in range(2):
                    keep_ref[h, other, block] = rows_of(first, kept[other])
                    put(send_ref, plan, other * plan.blocks + block, rows_of(first, sent[other]), level_ref)

            put_levels(send_ref, plan, 2 * plan.blocks, level_ref)


def start_all(sources, targets, sems):
    loads = [pltpu.make_async_copy(src, dst, sems.at[i]) for i, (src, dst) in enumerate(zip(sources, targets))]
    for load in loads:
        load.start()
    return loads


def add_virt(meta_ref, first, quarter_refs, green_ref, acc_ref):
    @pl.loop(0, OWNERS // 4)
    def _(step):
        for local in (step * 2, step * 2 + 1):
            for slot in range(CAP):
                span = slice(slot * QUARTER, (slot + 1) * QUARTER)
                tile = jnp.concatenate([ref[local, span, :] for ref in quarter_refs], axis=0)
                aux = meta_ref[first + local, 2 * slot]
                kept = meta_ref[first + local, 2 * slot + 1]
                acc_ref[aux] += jnp.dot(tile, green_ref[kept], preferred_element_type=F32)


def virt_first_body(meta_ref, *rest):
    sources, out_ref, refs, (acc_ref, sems) = rest[:5], rest[5], rest[6:11], rest[11:]
    loads = start_all(sources, refs, sems)
    acc_ref[...] = jnp.zeros(acc_ref.shape, F32)
    for load in loads:
        load.wait()
    add_virt(meta_ref, 0, refs[:4], refs[4], acc_ref)
    store = pltpu.make_async_copy(acc_ref, out_ref, sems.at[0])
    store.start()
    store.wait()


def virt_last_body(meta_ref, place_ref, *rest, plan):
    sources, (keep_ref, send0_ref, send1_ref) = rest[:6], rest[6:9]
    refs, (acc_ref, level_ref, sems) = rest[9:15], rest[15:]
    loads = start_all(sources[:5], refs, sems)
    acc_ref[...] = jnp.zeros(acc_ref.shape, F32)
    for load in loads:
        load.wait()
    before = pltpu.make_async_copy(sources[5], refs[5], sems.at[5])
    before.start()
    add_virt(meta_ref, OWNERS // 2, refs[:4], refs[4], acc_ref)
    before.wait()
    these, those = piece_rows(acc_ref), piece_rows(refs[5])

    def rows_of(first, piece):
        return these(first, piece) + those(first, piece)

    split_pieces(place_ref, plan, rows_of, (keep_ref, send0_ref, send1_ref), level_ref)


def piece_rows(acc_ref):
    def rows_of(first, piece):
        at = [pl.multiple_of(quarter * QUARTER + piece * 8, 8) for quarter in range(4)]
        return jnp.concatenate([acc_ref[first, pl.ds(row, 8), :] for row in at], axis=0)

    return rows_of


def occ_body(meta_ref, place_ref, *rest, plan):
    parts, green_ref = (rest[:4], rest[4:8]), rest[8]
    out_refs, (acc_ref, tile_ref, level_ref) = rest[9:-3], rest[-3:]
    acc_ref[...] = jnp.zeros(acc_ref.shape, F32)
    row_place = place_ref[0]
    rows = [pl.multiple_of(((row_place + d) % ROWS) * QUARTER, QUARTER) for d in (0, ROWS - 1, 1, 2)]
    half = OWNERS // 2
    visits = [(j, slot) for j in range(2) for slot in range(CAP)]
    for part in range(2):

        @pl.loop(0, half // 2)
        def _(step):
            for j, slot in visits:
                span = slice(slot * QUARTER, (slot + 1) * QUARTER)
                for ref, row in zip(parts[part], rows):
                    tile_ref[CAP * j + slot, pl.ds(row, QUARTER), :] = ref[step * 2 + j, span, :]
            for j, slot in visits:
                source = part * half + step * 2 + j
                aux = meta_ref[source, 2 * slot]
                kept = meta_ref[source, 2 * slot + 1]
                term = lax.dot_general(
                    green_ref[kept], tile_ref[CAP * j + slot], (((1,), (1,)), ((), ())), preferred_element_type=F32
                )
                for low in range(4):
                    lanes = slice(low * BS, (low + 1) * BS)
                    acc_ref[aux, :, lanes] += term[low * BS : (low + 1) * BS, :]

    split_pieces(place_ref, plan, piece_rows(acc_ref), out_refs, level_ref)


VMEM = pl.BlockSpec(memory_space=pltpu.VMEM)
SMEM = pl.BlockSpec(memory_space=pltpu.SMEM)
ANY = pl.BlockSpec(memory_space=pl.ANY)


def step_shapes(plan):
    code = jax.ShapeDtypeStruct((plan.coded(2 * plan.blocks), WIDE), S16)
    return [jax.ShapeDtypeStruct((2, 2, plan.blocks, plan.rows, WIDE), F32), code, code]


def level_scratch(plan):
    return pltpu.VMEM((plan.levels(2 * plan.blocks), WIDE), F32)


ACC = (NP, BS, WIDE)


def scratch_like(operands):
    return [pltpu.VMEM(x.shape, x.dtype) for x in operands]


def contract_virt_first(meta, part, green):
    operands = [*part, green]
    return pl.pallas_call(
        virt_first_body,
        in_specs=[SMEM] + [ANY] * 5,
        out_specs=ANY,
        out_shape=jax.ShapeDtypeStruct(ACC, F32),
        scratch_shapes=scratch_like(operands) + [pltpu.VMEM(ACC, F32), pltpu.SemaphoreType.DMA((5,))],
        compiler_params=params(55),
        name="virt_first",
    )(meta, *operands)


def contract_virt_last(meta, place, part, green, before, plan):
    operands = [*part, green, before]
    return pl.pallas_call(
        functools.partial(virt_last_body, plan=plan),
        in_specs=[SMEM] * 2 + [ANY] * 6,
        out_specs=[VMEM] * 3,
        out_shape=step_shapes(plan),
        scratch_shapes=scratch_like(operands) + [pltpu.VMEM(ACC, F32), level_scratch(plan), pltpu.SemaphoreType.DMA((6,))],
        compiler_params=params(55),
        name="virt_last",
    )(meta, place, *operands)


def contract_occ(meta, place, parts, green, plan):
    return pl.pallas_call(
        functools.partial(occ_body, plan=plan),
        in_specs=[SMEM] * 2 + [VMEM] * 9,
        out_specs=[VMEM] * 3 * plan.parts,
        out_shape=step_shapes(plan) * plan.parts,
        scratch_shapes=[pltpu.VMEM(ACC, F32), pltpu.VMEM((2 * CAP, BS, BS), BF16), level_scratch(plan)],
        compiler_params=params(28),
        name="contract_occ",
    )(meta, place, *parts[0], *parts[1], green)


def halve_body(place_ref, keep_ref, got0_ref, got1_ref, left_ref, send0_ref, send1_ref, level_ref, scale_ref, *, plan):
    for h, got_ref, send_ref in ((0, got0_ref, send0_ref), (1, got1_ref, send1_ref)):
        mine = place_ref[2 - h]
        away = 1 - mine
        read_scales(got_ref, (), plan, 2 * plan.blocks, scale_ref)

        @pl.loop(0, plan.blocks, unroll=2)
        def _(b):
            left_ref[h, b] = keep_ref[h, mine, b] + get(got_ref, (), plan, mine * plan.blocks + b, scale_ref)
            total = keep_ref[h, away, b] + get(got_ref, (), plan, away * plan.blocks + b, scale_ref)
            put(send_ref, plan, b, total, level_ref)

        put_levels(send_ref, plan, plan.blocks, level_ref)


def halve(place, keep, got0, got1, plan, name):
    code = jax.ShapeDtypeStruct((plan.coded(plan.blocks), WIDE), S16)
    return pl.pallas_call(
        functools.partial(halve_body, plan=plan),
        in_specs=[SMEM] + [VMEM] * 3,
        out_specs=[VMEM] * 3,
        out_shape=[jax.ShapeDtypeStruct((2, plan.blocks, plan.rows, WIDE), F32), code, code],
        scratch_shapes=[level_scratch(plan), level_scratch(plan)],
        compiler_params=params(16),
        name=name,
    )(place, keep, got0, got1)


def finish_blocks(refs, scale_ref, plan, store):
    for part in range(plan.parts):
        left_ref, *got_refs = refs[3 * part : 3 * part + 3]
        for h, got_ref in enumerate(got_refs):
            read_scales(got_ref, (), plan, plan.blocks, scale_ref)

            @pl.loop(0, plan.blocks, unroll=2)
            def _(b):
                total = left_ref[h, b] + get(got_ref, (), plan, b, scale_ref)
                store((h * plan.parts + part) * plan.blocks + b, total)


def finish_virt_body(left_ref, got0_ref, got1_ref, out_ref, level_ref, scale_ref, *, plan):
    def store(index, total):
        put(out_ref, plan, index, total, level_ref)

    finish_blocks((left_ref, got0_ref, got1_ref), scale_ref, plan, store)
    put_levels(out_ref, plan, 2 * plan.blocks, level_ref)


def finish_occ_body(place_ref, *rest, plan, whole):
    refs, out_refs, (code_ref, level_ref, scale_ref) = rest[:-7], rest[-7:-3], rest[-3:]
    lanes = [pl.ds(pl.multiple_of((place_ref[0] + d) % 4 * BS, BS), BS) for d in range(4)]

    def store(index, total):
        codes, level = encode(total)
        code_ref[...] = codes
        level_ref[pl.ds(index, 1), :] = level
        for out_ref, part in zip(out_refs, lanes):
            out_ref[at_block(plan, index), :] = code_ref[:, part]

    finish_blocks(refs, scale_ref, plan, store)
    for out_ref, part in zip(out_refs, lanes):
        out_ref[level_rows(whole, 2 * whole.blocks), :] = level_ref[:, part].astype(jnp.int32).astype(S16)


def finish_virt(left, got0, got1, plan):
    return pl.pallas_call(
        functools.partial(finish_virt_body, plan=plan),
        in_specs=[VMEM] * 3,
        out_specs=VMEM,
        out_shape=jax.ShapeDtypeStruct((plan.coded(2 * plan.blocks), WIDE), S16),
        scratch_shapes=[level_scratch(plan), level_scratch(plan)],
        compiler_params=params(12),
        name="finish_virt",
    )(left, got0, got1)


def finish_occ(place, sums, plan, whole):
    part = jax.ShapeDtypeStruct((whole.coded(2 * whole.blocks), BS), S16)
    return pl.pallas_call(
        functools.partial(finish_occ_body, plan=plan, whole=whole),
        in_specs=[SMEM] + [VMEM] * len(sums),
        out_specs=[VMEM] * 4,
        out_shape=[part] * 4,
        scratch_shapes=[pltpu.VMEM((plan.rows, WIDE), S16), level_scratch(whole), level_scratch(whole)],
        compiler_params=params(12),
        name="finish_occ",
    )(place, *sums)


def decode_virt_body(place_ref, virt_ref, vir_ref, scale_ref, *, plan):
    at = [((place_ref[1] + shift) % 4) * 8 for shift in (0, ROWS - 1, 1, 2)]
    read_scales(virt_ref, (), plan, 2 * plan.blocks, scale_ref)

    @pl.loop(0, NP, unroll=2)
    def _(q):
        values = get(virt_ref, (), plan, q, scale_ref)
        for quarter in range(4):
            for low in range(4):
                to = pl.ds(pl.multiple_of(low * QUARTER + at[quarter], 8), 8)
                vir_ref[q, to, :] = values[quarter * 8 : (quarter + 1) * 8, low * BS : (low + 1) * BS]


def decode_virt(place, virt, plan):
    return pl.pallas_call(
        functools.partial(decode_virt_body, plan=plan),
        in_specs=[SMEM, VMEM],
        out_specs=VMEM,
        out_shape=jax.ShapeDtypeStruct((NP, BS, BS), F32),
        scratch_shapes=[level_scratch(plan)],
        compiler_params=params(8),
        name="decode_virt",
    )(place, virt)


def pair_body(place_ref, own_ref, one_ref, two_ref, three_ref, vir_ref, out_ref, occ_ref, scale_ref, *, plan):
    here = place_ref[0]

    for d, ref in enumerate((own_ref, one_ref, two_ref, three_ref)):
        source = (here + 4 - d) % 4
        read_scales(ref, (), plan, 2 * plan.blocks, scale_ref)
        rows = pl.ds(pl.multiple_of(source * QUARTER, QUARTER), QUARTER)

        @pl.loop(0, NP, unroll=4)
        def _(p):
            occ_ref[p, rows, :] = get(ref, (), plan, p, scale_ref)

    @pl.loop(0, NP)
    def _(p):
        occ = occ_ref[p]
        for q in range(NP):
            out_ref[p, q : q + 1, :] = jnp.sum(occ * vir_ref[q], axis=0, keepdims=True)


def pair(place, own, others, vir, plan):
    return pl.pallas_call(
        functools.partial(pair_body, plan=plan),
        in_specs=[SMEM] + [VMEM] * 5,
        out_specs=VMEM,
        out_shape=jax.ShapeDtypeStruct((NP, NP, BS), F32),
        scratch_shapes=[pltpu.VMEM((NP, BS, BS), F32), pltpu.VMEM((plan.levels(2 * plan.blocks), BS), F32)],
        compiler_params=params(16),
        name="pair",
    )(place, own, *others, vir)


def rotate(size, step):
    return [(i, (i + step) % size) for i in range(size)]


def rotate_high(step):
    return [(c, (c + 4 * step) % COLS) for c in range(COLS)]


PAIRS_A = [(0, 1), (1, 0), (2, 3), (3, 2)]
PAIRS_B = [(0, 3), (3, 0), (1, 2), (2, 1)]


def index_of(row, col, layer):
    return (row * COLS + col) * LAYERS + layer


SWAP = [
    (index_of(r, c, l), index_of(c % 4, c // 4 * 4 + r, l))
    for r in range(ROWS)
    for c in range(COLS)
    for l in range(LAYERS)
]


def sum_all(values):
    for axes in ("col", ("row", "layer")):
        copies = jnp.broadcast_to(values[None], (16, *values.shape))
        values = jnp.sum(lax.all_to_all(copies, axes, 0, 0, tiled=True), axis=0)
    return values


def layer_swap(send0, send1, perms):
    return lax.ppermute(send0, "layer", perms[0]), lax.ppermute(send1, "layer", perms[1])


FIRST = (PAIRS_A, PAIRS_B)
SECOND = (PAIRS_B, PAIRS_A)


def after(*values):
    return lax.optimization_barrier(values)


def on_device(blocks, block_aux, block_row, block_col, extents, occ_green, virt_green):
    layer_blocks = occ_green.shape[0] // BS
    row_place = lax.axis_index("row").astype(jnp.int32)
    col_place = lax.axis_index("col").astype(jnp.int32)
    layer_place = lax.axis_index("layer").astype(jnp.int32)
    bit_a = ((layer_place == 1) | (layer_place == 2)).astype(jnp.int32)
    bit_b = layer_place // 2
    place = jnp.stack([row_place, bit_a, bit_b])
    plan = Plan(4)

    send = build_send(blocks, block_aux, block_row, block_col, extents, row_place[None], layer_blocks)
    own = lax.all_to_all(send, ("col", "layer"), 0, 0, tiled=True)
    virt_blocks = virt_green.reshape(layer_blocks, BS, WIDE)
    occ_blocks = occ_green.reshape(layer_blocks, BS, WIDE).transpose(0, 2, 1)

    half = OWNERS // 2
    own_a = own[:half, : CAP * QUARTER]
    later, occ_blocks = after(own, occ_blocks)
    own_b = later[half:, : CAP * QUARTER]
    meta = later[:, CAP * QUARTER, : 2 * CAP].astype(jnp.int32)
    up, down = rotate(ROWS, 1), rotate(ROWS, -1)
    prev_a = lax.ppermute(own_a, "row", up)
    next_a = lax.ppermute(own_a, "row", down)
    prev_a, next_a, own_b, occ_blocks, meta = after(prev_a, next_a, own_b, occ_blocks, meta)
    far_a = lax.ppermute(prev_a, "row", up)
    next_b = lax.ppermute(own_b, "row", down)
    far_a, next_b, own_b = after(far_a, next_b, own_b)
    prev_b = lax.ppermute(own_b, "row", up)
    far_b = lax.ppermute(next_b, "row", down)
    part_a, part_b = (own_a, prev_a, next_a, far_a), (own_b, prev_b, next_b, far_b)

    v_acc = contract_virt_first(meta, part_a, virt_blocks)
    v_keep, v0, v1 = contract_virt_last(meta, place, part_b, virt_blocks, v_acc, plan)
    v_got = layer_swap(v0, v1, FIRST)
    occ_blocks, v_keep = after(occ_blocks, v_keep)
    halves = Plan(4, parts=2)
    a_keep, a0, a1, b_keep, b0, b1 = contract_occ(meta, place, (part_a, part_b), occ_blocks, halves)
    a_got = layer_swap(a0, a1, FIRST)
    v_keep, a_keep, b_keep = after(v_keep, a_keep, b_keep)
    v_left, v0, v1 = halve(place, v_keep, *v_got, plan, "halve_virt")
    v_got = layer_swap(v0, v1, SECOND)
    a_keep, v_left = after(a_keep, v_left)
    a_left, a0, a1 = halve(place, a_keep, *a_got, halves, "halve_occ_a")
    a_left, *v_got = after(a_left, *v_got)
    a0, a1, b0, b1, *v_got = after(a0, a1, b0, b1, *v_got)
    b_got = layer_swap(b0, b1, FIRST)
    a_got = layer_swap(a0, a1, SECOND)
    virt = finish_virt(v_left, *v_got, plan)
    virt, b_keep = after(virt, b_keep)
    virt = lax.ppermute(virt, ALL, SWAP)
    b_left, b0, b1 = halve(place, b_keep, *b_got, halves, "halve_occ_b")
    b_got = layer_swap(b0, b1, SECOND)
    here = jnp.stack([col_place // 4, col_place % 4])
    occ, *others = finish_occ(here, (a_left, *a_got, b_left, *b_got), halves, plan)
    others = [lax.ppermute(part, "col", rotate_high(d)) for d, part in zip((1, 2, 3), others)]
    partial = pair(here, occ, others, decode_virt(here, virt, plan), plan)
    return sum_all(jnp.sum(partial, axis=-1))


def solution(mesh):
    in_specs = (
        P(("col", "layer"), None, None),
        P(("col", "layer")),
        P(("col", "layer")),
        P(("col", "layer")),
        P(("col", "layer")),
        P("layer", "row"),
        P("layer", "row"),
    )
    return jax.shard_map(on_device, mesh=mesh, in_specs=in_specs, out_specs=P(), check_vma=False)
```

```python
import functools

import jax
import jax.numpy as jnp
from jax import lax
from jax.experimental import pallas as pl
from jax.experimental.pallas import tpu as pltpu
from jax.sharding import PartitionSpec as P

NP = 24
ROWS = 4
COLS = 16
LAYERS = 4
CAP = 2
OWNERS = COLS * LAYERS
BS = 128
QUARTER = BS // ROWS
WIDE = 512
HALF = NP // 2
TOP = 32700.0
STEPS = 64.0
ALL = ("row", "col", "layer")
F32 = jnp.float32
BF16 = jnp.bfloat16
S16 = jnp.int16


def params(mib):
    return pltpu.CompilerParams(vmem_limit_bytes=mib * 2**20)


def encode(block):
    peak = jnp.max(jnp.abs(block), axis=0, keepdims=True)
    level = jnp.ceil(jnp.log2(jnp.maximum(peak, 1e-30)) * STEPS)
    scaled = block * (jnp.exp2(level * (-1.0 / STEPS)) * TOP)
    return jnp.round(scaled).astype(jnp.int32).astype(S16), level


def decode(codes, level):
    return codes.astype(jnp.int32).astype(F32) * (jnp.exp2(level * (1.0 / STEPS)) * (1.0 / TOP))


class Plan:
    def __init__(self, quarters, first=0, blocks=None):
        self.quarters = quarters
        self.group = 4 // quarters
        self.rows = 8 * quarters * self.group
        self.first = first
        self.blocks = blocks or HALF // self.group

    def levels(self, count):
        return (count + 15) // 16 * 16

    def coded(self, count):
        return count * self.rows + self.levels(count)


def at_block(plan, index):
    return pl.ds(pl.multiple_of(index * plan.rows, 16), plan.rows)


def level_rows(plan, count):
    return slice(count * plan.rows, plan.coded(count))


def read_scales(ref, lead, plan, count, scale_ref):
    level = ref[(*lead, level_rows(plan, count), slice(None))].astype(jnp.int32).astype(F32)
    scale_ref[: plan.levels(count), :] = jnp.exp2(level * (1.0 / STEPS)) * (1.0 / TOP)


def get(ref, lead, plan, index, scale_ref):
    codes = ref[(*lead, at_block(plan, index), slice(None))]
    return codes.astype(jnp.int32).astype(F32) * scale_ref[pl.ds(index, 1), :]


def put(ref, plan, index, block, level_ref):
    codes, level = encode(block)
    ref[at_block(plan, index), :] = codes
    level_ref[pl.ds(index, 1), :] = level


def put_levels(ref, plan, count, level_ref):
    level = level_ref[: plan.levels(count), :]
    ref[level_rows(plan, count), :] = level.astype(jnp.int32).astype(S16)


def send_body(
    aux_ref, row_ref, col_ref, ext_ref, place_ref, blocks_ref, out_ref, count_ref, tiles_ref, sem, *, layer_blocks
):
    rows = pl.ds(pl.multiple_of(place_ref[0] * QUARTER, QUARTER), QUARTER)
    load = pltpu.make_async_copy(blocks_ref.at[:, rows, :], tiles_ref, sem)
    load.start()
    out_ref[...] = jnp.zeros(out_ref.shape, BF16)

    @pl.loop(0, OWNERS)
    def _(i):
        count_ref[i] = 0

    lane = lax.broadcasted_iota(jnp.int32, (QUARTER, BS), 1)
    meta_lane = lax.broadcasted_iota(jnp.int32, (8, BS), 1)
    load.wait()

    @pl.loop(0, tiles_ref.shape[0])
    def _(i):
        col = col_ref[i]
        layer_of = col // layer_blocks
        kept = col - layer_of * layer_blocks
        owner = (row_ref[i] % 4 * 4 + row_ref[i] // 4) * LAYERS + layer_of
        used = count_ref[owner]
        count_ref[owner] = used + 1
        tile = jnp.where(lane < ext_ref[i], tiles_ref[i].astype(F32), 0.0)
        out_ref[owner, pl.ds(pl.multiple_of(used * QUARTER, QUARTER), QUARTER), :] = tile.astype(BF16)
        old = out_ref[owner, CAP * QUARTER :, :].astype(F32)
        new = jnp.where(meta_lane == used * 2, aux_ref[i].astype(F32), old)
        new = jnp.where(meta_lane == used * 2 + 1, kept.astype(F32), new)
        out_ref[owner, CAP * QUARTER :, :] = new.astype(BF16)


def build_send(blocks, block_aux, block_row, block_col, extents, place, layer_blocks):
    return pl.pallas_call(
        functools.partial(send_body, layer_blocks=layer_blocks),
        in_specs=[SMEM] * 5 + [ANY],
        out_specs=VMEM,
        out_shape=jax.ShapeDtypeStruct((OWNERS, CAP * QUARTER + 8, BS), BF16),
        scratch_shapes=[
            pltpu.SMEM((OWNERS,), jnp.int32),
            pltpu.VMEM((blocks.shape[0], QUARTER, BS), BF16),
            pltpu.SemaphoreType.DMA(()),
        ],
        compiler_params=params(60),
        name="build_send",
    )(block_aux, block_row, block_col, extents, place, blocks)


def split_pieces(place_ref, plans, rows_of, out_refs, level_ref):
    bit_a = place_ref[1]
    bit_b = place_ref[2]

    def piece(a, b):
        return jnp.where(b == 0, a, 3 - a)

    for part, plan in enumerate(plans):
        keep_ref, *send_refs = out_refs[3 * part : 3 * part + 3]
        for h, send_ref in enumerate(send_refs):
            kept = [piece(bit_a, o) if h == 0 else piece(o, bit_b) for o in range(2)]
            sent = [piece(1 - bit_a, o) if h == 0 else piece(o, 1 - bit_b) for o in range(2)]

            @pl.loop(0, plan.blocks, unroll=2)
            def _(block):
                first = h * HALF + (plan.first + block) * plan.group
                for other in range(2):
                    keep_ref[h, other, block] = rows_of(first, kept[other])
                    put(send_ref, plan, other * plan.blocks + block, rows_of(first, sent[other]), level_ref)

            put_levels(send_ref, plan, 2 * plan.blocks, level_ref)


def start_all(sources, targets, sems):
    loads = [pltpu.make_async_copy(src, dst, sems.at[i]) for i, (src, dst) in enumerate(zip(sources, targets))]
    for load in loads:
        load.start()
    return loads


def add_virt(meta_ref, first, quarter_refs, green_ref, acc_ref):
    @pl.loop(0, OWNERS // 4)
    def _(step):
        for local in (step * 2, step * 2 + 1):
            for slot in range(CAP):
                span = slice(slot * QUARTER, (slot + 1) * QUARTER)
                tile = jnp.concatenate([ref[local, span, :] for ref in quarter_refs], axis=0)
                aux = meta_ref[first + local, 2 * slot]
                kept = meta_ref[first + local, 2 * slot + 1]
                acc_ref[aux] += jnp.dot(tile, green_ref[kept], preferred_element_type=F32)


def virt_first_body(meta_ref, *rest):
    sources, out_ref, refs, (acc_ref, sems) = rest[:5], rest[5], rest[6:11], rest[11:]
    loads = start_all(sources, refs, sems)
    acc_ref[...] = jnp.zeros(acc_ref.shape, F32)
    for load in loads:
        load.wait()
    add_virt(meta_ref, 0, refs[:4], refs[4], acc_ref)
    store = pltpu.make_async_copy(acc_ref, out_ref, sems.at[0])
    store.start()
    store.wait()


def virt_last_body(meta_ref, place_ref, *rest, plan):
    sources, (keep_ref, send0_ref, send1_ref) = rest[:6], rest[6:9]
    refs, (acc_ref, level_ref, sems) = rest[9:15], rest[15:]
    loads = start_all(sources[:5], refs, sems)
    acc_ref[...] = jnp.zeros(acc_ref.shape, F32)
    for load in loads:
        load.wait()
    before = pltpu.make_async_copy(sources[5], refs[5], sems.at[5])
    before.start()
    add_virt(meta_ref, OWNERS // 2, refs[:4], refs[4], acc_ref)
    before.wait()
    these, those = piece_rows(acc_ref), piece_rows(refs[5])

    def rows_of(first, piece):
        return these(first, piece) + those(first, piece)

    split_pieces(place_ref, (plan,), rows_of, (keep_ref, send0_ref, send1_ref), level_ref)


def piece_rows(acc_ref):
    def rows_of(first, piece):
        at = [pl.multiple_of(quarter * QUARTER + piece * 8, 8) for quarter in range(4)]
        return jnp.concatenate([acc_ref[first, pl.ds(row, 8), :] for row in at], axis=0)

    return rows_of


def occ_body(meta_ref, place_ref, *rest, plans):
    parts, green_ref = (rest[:4], rest[4:8]), rest[8]
    out_refs, (acc_ref, tile_ref, level_ref) = rest[9:-3], rest[-3:]
    acc_ref[...] = jnp.zeros(acc_ref.shape, F32)
    row_place = place_ref[0]
    rows = [pl.multiple_of(((row_place + d) % ROWS) * QUARTER, QUARTER) for d in (0, ROWS - 1, 1, 2)]
    half = OWNERS // 2
    visits = [(j, slot) for j in range(2) for slot in range(CAP)]
    for part in range(2):

        @pl.loop(0, half // 2)
        def _(step):
            for j, slot in visits:
                span = slice(slot * QUARTER, (slot + 1) * QUARTER)
                for ref, row in zip(parts[part], rows):
                    tile_ref[CAP * j + slot, pl.ds(row, QUARTER), :] = ref[step * 2 + j, span, :]
            for j, slot in visits:
                source = part * half + step * 2 + j
                aux = meta_ref[source, 2 * slot]
                kept = meta_ref[source, 2 * slot + 1]
                term = lax.dot_general(
                    green_ref[kept], tile_ref[CAP * j + slot], (((1,), (1,)), ((), ())), preferred_element_type=F32
                )
                for low in range(4):
                    lanes = slice(low * BS, (low + 1) * BS)
                    acc_ref[aux, :, lanes] += term[low * BS : (low + 1) * BS, :]

    split_pieces(place_ref, plans, piece_rows(acc_ref), out_refs, level_ref)


VMEM = pl.BlockSpec(memory_space=pltpu.VMEM)
SMEM = pl.BlockSpec(memory_space=pltpu.SMEM)
ANY = pl.BlockSpec(memory_space=pl.ANY)


def step_shapes(plan):
    code = jax.ShapeDtypeStruct((plan.coded(2 * plan.blocks), WIDE), S16)
    return [jax.ShapeDtypeStruct((2, 2, plan.blocks, plan.rows, WIDE), F32), code, code]


def level_scratch(plan):
    return pltpu.VMEM((plan.levels(2 * plan.blocks), WIDE), F32)


ACC = (NP, BS, WIDE)


def scratch_like(operands):
    return [pltpu.VMEM(x.shape, x.dtype) for x in operands]


def contract_virt_first(meta, part, green):
    operands = [*part, green]
    return pl.pallas_call(
        virt_first_body,
        in_specs=[SMEM] + [ANY] * 5,
        out_specs=ANY,
        out_shape=jax.ShapeDtypeStruct(ACC, F32),
        scratch_shapes=scratch_like(operands) + [pltpu.VMEM(ACC, F32), pltpu.SemaphoreType.DMA((5,))],
        compiler_params=params(55),
        name="virt_first",
    )(meta, *operands)


def contract_virt_last(meta, place, part, green, before, plan):
    operands = [*part, green, before]
    return pl.pallas_call(
        functools.partial(virt_last_body, plan=plan),
        in_specs=[SMEM] * 2 + [ANY] * 6,
        out_specs=[VMEM] * 3,
        out_shape=step_shapes(plan),
        scratch_shapes=scratch_like(operands) + [pltpu.VMEM(ACC, F32), level_scratch(plan), pltpu.SemaphoreType.DMA((6,))],
        compiler_params=params(55),
        name="virt_last",
    )(meta, place, *operands)


def contract_occ(meta, place, parts, green, plans):
    return pl.pallas_call(
        functools.partial(occ_body, plans=plans),
        in_specs=[SMEM] * 2 + [VMEM] * 9,
        out_specs=[VMEM] * 3 * len(plans),
        out_shape=[shape for plan in plans for shape in step_shapes(plan)],
        scratch_shapes=[pltpu.VMEM(ACC, F32), pltpu.VMEM((2 * CAP, BS, BS), BF16), level_scratch(plans[-1])],
        compiler_params=params(28),
        name="contract_occ",
    )(meta, place, *parts[0], *parts[1], green)


def halve_body(place_ref, keep_ref, got0_ref, got1_ref, left_ref, send0_ref, send1_ref, level_ref, scale_ref, *, plan):
    for h, got_ref, send_ref in ((0, got0_ref, send0_ref), (1, got1_ref, send1_ref)):
        mine = place_ref[2 - h]
        away = 1 - mine
        read_scales(got_ref, (), plan, 2 * plan.blocks, scale_ref)

        @pl.loop(0, plan.blocks, unroll=2)
        def _(b):
            left_ref[h, b] = keep_ref[h, mine, b] + get(got_ref, (), plan, mine * plan.blocks + b, scale_ref)
            total = keep_ref[h, away, b] + get(got_ref, (), plan, away * plan.blocks + b, scale_ref)
            put(send_ref, plan, b, total, level_ref)

        put_levels(send_ref, plan, plan.blocks, level_ref)


def halve(place, keep, got0, got1, plan, name):
    code = jax.ShapeDtypeStruct((plan.coded(plan.blocks), WIDE), S16)
    return pl.pallas_call(
        functools.partial(halve_body, plan=plan),
        in_specs=[SMEM] + [VMEM] * 3,
        out_specs=[VMEM] * 3,
        out_shape=[jax.ShapeDtypeStruct((2, plan.blocks, plan.rows, WIDE), F32), code, code],
        scratch_shapes=[level_scratch(plan), level_scratch(plan)],
        compiler_params=params(16),
        name=name,
    )(place, keep, got0, got1)


def finish_blocks(refs, scale_ref, plans, store):
    for part, plan in enumerate(plans):
        left_ref, *got_refs = refs[3 * part : 3 * part + 3]
        for h, got_ref in enumerate(got_refs):
            read_scales(got_ref, (), plan, plan.blocks, scale_ref)

            @pl.loop(0, plan.blocks, unroll=2)
            def _(b):
                total = left_ref[h, b] + get(got_ref, (), plan, b, scale_ref)
                store(h * HALF // plan.group + plan.first + b, total)


def finish_virt_body(left_ref, got0_ref, got1_ref, out_ref, level_ref, scale_ref, *, plan):
    def store(index, total):
        put(out_ref, plan, index, total, level_ref)

    finish_blocks((left_ref, got0_ref, got1_ref), scale_ref, (plan,), store)
    put_levels(out_ref, plan, 2 * plan.blocks, level_ref)


def finish_occ_body(place_ref, *rest, plans, whole):
    refs, out_refs, (code_ref, level_ref, scale_ref) = rest[:-7], rest[-7:-3], rest[-3:]
    lanes = [pl.ds(pl.multiple_of((place_ref[0] + d) % 4 * BS, BS), BS) for d in range(4)]

    def store(index, total):
        codes, level = encode(total)
        code_ref[...] = codes
        level_ref[pl.ds(index, 1), :] = level
        for out_ref, part in zip(out_refs, lanes):
            out_ref[at_block(whole, index), :] = code_ref[:, part]

    finish_blocks(refs, scale_ref, plans, store)
    for out_ref, part in zip(out_refs, lanes):
        out_ref[level_rows(whole, 2 * whole.blocks), :] = level_ref[:, part].astype(jnp.int32).astype(S16)


def finish_virt(left, got0, got1, plan):
    return pl.pallas_call(
        functools.partial(finish_virt_body, plan=plan),
        in_specs=[VMEM] * 3,
        out_specs=VMEM,
        out_shape=jax.ShapeDtypeStruct((plan.coded(2 * plan.blocks), WIDE), S16),
        scratch_shapes=[level_scratch(plan), level_scratch(plan)],
        compiler_params=params(12),
        name="finish_virt",
    )(left, got0, got1)


def finish_occ(place, sums, plans, whole):
    part = jax.ShapeDtypeStruct((whole.coded(2 * whole.blocks), BS), S16)
    return pl.pallas_call(
        functools.partial(finish_occ_body, plans=plans, whole=whole),
        in_specs=[SMEM] + [VMEM] * len(sums),
        out_specs=[VMEM] * 4,
        out_shape=[part] * 4,
        scratch_shapes=[pltpu.VMEM((whole.rows, WIDE), S16), level_scratch(whole), level_scratch(whole)],
        compiler_params=params(12),
        name="finish_occ",
    )(place, *sums)


def decode_virt_body(place_ref, virt_ref, vir_ref, scale_ref, *, plan):
    at = [((place_ref[1] + shift) % 4) * 8 for shift in (0, ROWS - 1, 1, 2)]
    read_scales(virt_ref, (), plan, 2 * plan.blocks, scale_ref)

    @pl.loop(0, NP, unroll=2)
    def _(q):
        values = get(virt_ref, (), plan, q, scale_ref)
        for quarter in range(4):
            for low in range(4):
                to = pl.ds(pl.multiple_of(low * QUARTER + at[quarter], 8), 8)
                vir_ref[q, to, :] = values[quarter * 8 : (quarter + 1) * 8, low * BS : (low + 1) * BS]


def decode_virt(place, virt, plan):
    return pl.pallas_call(
        functools.partial(decode_virt_body, plan=plan),
        in_specs=[SMEM, VMEM],
        out_specs=VMEM,
        out_shape=jax.ShapeDtypeStruct((NP, BS, BS), F32),
        scratch_shapes=[level_scratch(plan)],
        compiler_params=params(8),
        name="decode_virt",
    )(place, virt)


def pair_body(place_ref, own_ref, one_ref, two_ref, three_ref, vir_ref, out_ref, occ_ref, scale_ref, *, plan):
    here = place_ref[0]

    for d, ref in enumerate((own_ref, one_ref, two_ref, three_ref)):
        source = (here + 4 - d) % 4
        read_scales(ref, (), plan, 2 * plan.blocks, scale_ref)
        rows = pl.ds(pl.multiple_of(source * QUARTER, QUARTER), QUARTER)

        @pl.loop(0, NP, unroll=4)
        def _(p):
            occ_ref[p, rows, :] = get(ref, (), plan, p, scale_ref)

    @pl.loop(0, NP)
    def _(p):
        occ = occ_ref[p]
        for q in range(NP):
            out_ref[p, q : q + 1, :] = jnp.sum(occ * vir_ref[q], axis=0, keepdims=True)


def pair(place, own, others, vir, plan):
    return pl.pallas_call(
        functools.partial(pair_body, plan=plan),
        in_specs=[SMEM] + [VMEM] * 5,
        out_specs=VMEM,
        out_shape=jax.ShapeDtypeStruct((NP, NP, BS), F32),
        scratch_shapes=[pltpu.VMEM((NP, BS, BS), F32), pltpu.VMEM((plan.levels(2 * plan.blocks), BS), F32)],
        compiler_params=params(16),
        name="pair",
    )(place, own, *others, vir)


def rotate(size, step):
    return [(i, (i + step) % size) for i in range(size)]


def rotate_high(step):
    return [(c, (c + 4 * step) % COLS) for c in range(COLS)]


PAIRS_A = [(0, 1), (1, 0), (2, 3), (3, 2)]
PAIRS_B = [(0, 3), (3, 0), (1, 2), (2, 1)]


def index_of(row, col, layer):
    return (row * COLS + col) * LAYERS + layer


SWAP = [
    (index_of(r, c, l), index_of(c % 4, c // 4 * 4 + r, l))
    for r in range(ROWS)
    for c in range(COLS)
    for l in range(LAYERS)
]


def sum_all(values):
    for axes in ("col", ("row", "layer")):
        copies = jnp.broadcast_to(values[None], (16, *values.shape))
        values = jnp.sum(lax.all_to_all(copies, axes, 0, 0, tiled=True), axis=0)
    return values


def layer_swap(send0, send1, perms):
    return lax.ppermute(send0, "layer", perms[0]), lax.ppermute(send1, "layer", perms[1])


FIRST = (PAIRS_A, PAIRS_B)
SECOND = (PAIRS_B, PAIRS_A)


def after(*values):
    return lax.optimization_barrier(values)


def on_device(blocks, block_aux, block_row, block_col, extents, occ_green, virt_green):
    layer_blocks = occ_green.shape[0] // BS
    row_place = lax.axis_index("row").astype(jnp.int32)
    col_place = lax.axis_index("col").astype(jnp.int32)
    layer_place = lax.axis_index("layer").astype(jnp.int32)
    bit_a = ((layer_place == 1) | (layer_place == 2)).astype(jnp.int32)
    bit_b = layer_place // 2
    place = jnp.stack([row_place, bit_a, bit_b])
    plan = Plan(4)

    send = build_send(blocks, block_aux, block_row, block_col, extents, row_place[None], layer_blocks)
    own = lax.all_to_all(send, ("col", "layer"), 0, 0, tiled=True)
    virt_blocks = virt_green.reshape(layer_blocks, BS, WIDE)
    occ_blocks = occ_green.reshape(layer_blocks, BS, WIDE).transpose(0, 2, 1)

    half = OWNERS // 2
    own_a = own[:half, : CAP * QUARTER]
    later, occ_blocks = after(own, occ_blocks)
    own_b = later[half:, : CAP * QUARTER]
    meta = later[:, CAP * QUARTER, : 2 * CAP].astype(jnp.int32)
    up, down = rotate(ROWS, 1), rotate(ROWS, -1)
    prev_a = lax.ppermute(own_a, "row", up)
    next_a = lax.ppermute(own_a, "row", down)
    prev_a, next_a, own_b, occ_blocks, meta = after(prev_a, next_a, own_b, occ_blocks, meta)
    far_a = lax.ppermute(prev_a, "row", up)
    next_b = lax.ppermute(own_b, "row", down)
    far_a, next_b, own_b = after(far_a, next_b, own_b)
    prev_b = lax.ppermute(own_b, "row", up)
    far_b = lax.ppermute(next_b, "row", down)
    part_a, part_b = (own_a, prev_a, next_a, far_a), (own_b, prev_b, next_b, far_b)

    v_acc = contract_virt_first(meta, part_a, virt_blocks)
    v_keep, v0, v1 = contract_virt_last(meta, place, part_b, virt_blocks, v_acc, plan)
    v_got = layer_swap(v0, v1, FIRST)
    occ_blocks, v_keep = after(occ_blocks, v_keep)
    small, large = parts = Plan(4, 0, 4), Plan(4, 4, 8)
    a_keep, a0, a1, b_keep, b0, b1 = contract_occ(meta, place, (part_a, part_b), occ_blocks, parts)
    a_got = layer_swap(a0, a1, FIRST)
    v_keep, a_keep, b_keep = after(v_keep, a_keep, b_keep)
    v_left, v0, v1 = halve(place, v_keep, *v_got, plan, "halve_virt")
    v0, v1, *a_got = after(v0, v1, *a_got)
    v_got = layer_swap(v0, v1, SECOND)
    a_keep, v_left = after(a_keep, v_left)
    a_left, a0, a1 = halve(place, a_keep, *a_got, small, "halve_occ_a")
    a_left, *v_got = after(a_left, *v_got)
    a0, a1, b0, b1, *v_got = after(a0, a1, b0, b1, *v_got)
    b_got = layer_swap(b0, b1, FIRST)
    a_got = layer_swap(a0, a1, SECOND)
    virt = finish_virt(v_left, *v_got, plan)
    virt, b_keep = after(virt, b_keep)
    virt = lax.ppermute(virt, ALL, SWAP)
    b_left, b0, b1 = halve(place, b_keep, *b_got, large, "halve_occ_b")
    b_got = layer_swap(b0, b1, SECOND)
    here = jnp.stack([col_place // 4, col_place % 4])
    occ, *others = finish_occ(here, (a_left, *a_got, b_left, *b_got), parts, plan)
    far = lax.ppermute(others[1], "col", rotate_high(2))
    others = [lax.ppermute(others[0], "col", rotate_high(1)), far, lax.ppermute(others[2], "col", rotate_high(3))]
    partial = pair(here, occ, others, decode_virt(here, virt, plan), plan)
    return sum_all(jnp.sum(partial, axis=-1))


def solution(mesh):
    in_specs = (
        P(("col", "layer"), None, None),
        P(("col", "layer")),
        P(("col", "layer")),
        P(("col", "layer")),
        P(("col", "layer")),
        P("layer", "row"),
        P("layer", "row"),
    )
    return jax.shard_map(on_device, mesh=mesh, in_specs=in_specs, out_specs=P(), check_vma=False)
```

```python
import functools

import jax
import jax.numpy as jnp
from jax import lax
from jax.experimental import pallas as pl
from jax.experimental.pallas import tpu as pltpu
from jax.sharding import PartitionSpec as P

NP = 24
ROWS = 4
COLS = 16
LAYERS = 4
CAP = 2
OWNERS = COLS * LAYERS
BS = 128
QUARTER = BS // ROWS
WIDE = 512
HALF = NP // 2
TOP = 32700.0
STEPS = 64.0
ALL = ("row", "col", "layer")
F32 = jnp.float32
BF16 = jnp.bfloat16
S16 = jnp.int16


def params(mib):
    return pltpu.CompilerParams(vmem_limit_bytes=mib * 2**20)


def encode(block):
    peak = jnp.max(jnp.abs(block), axis=0, keepdims=True)
    level = jnp.ceil(jnp.log2(jnp.maximum(peak, 1e-30)) * STEPS)
    scaled = block * (jnp.exp2(level * (-1.0 / STEPS)) * TOP)
    return jnp.round(scaled).astype(jnp.int32).astype(S16), level


def decode(codes, level):
    return codes.astype(jnp.int32).astype(F32) * (jnp.exp2(level * (1.0 / STEPS)) * (1.0 / TOP))


class Plan:
    def __init__(self, quarters, first=0, blocks=None):
        self.quarters = quarters
        self.group = 4 // quarters
        self.rows = 8 * quarters * self.group
        self.first = first
        self.blocks = blocks or HALF // self.group

    def levels(self, count):
        return (count + 15) // 16 * 16

    def coded(self, count):
        return count * self.rows + self.levels(count)


def at_block(plan, index):
    return pl.ds(pl.multiple_of(index * plan.rows, 16), plan.rows)


def level_rows(plan, count):
    return slice(count * plan.rows, plan.coded(count))


def read_scales(ref, lead, plan, count, scale_ref):
    level = ref[(*lead, level_rows(plan, count), slice(None))].astype(jnp.int32).astype(F32)
    scale_ref[: plan.levels(count), :] = jnp.exp2(level * (1.0 / STEPS)) * (1.0 / TOP)


def get(ref, lead, plan, index, scale_ref):
    codes = ref[(*lead, at_block(plan, index), slice(None))]
    return codes.astype(jnp.int32).astype(F32) * scale_ref[pl.ds(index, 1), :]


def put(ref, plan, index, block, level_ref):
    codes, level = encode(block)
    ref[at_block(plan, index), :] = codes
    level_ref[pl.ds(index, 1), :] = level


def put_levels(ref, plan, count, level_ref):
    level = level_ref[: plan.levels(count), :]
    ref[level_rows(plan, count), :] = level.astype(jnp.int32).astype(S16)


def send_body(
    aux_ref, row_ref, col_ref, ext_ref, place_ref, blocks_ref, out_ref, count_ref, tiles_ref, sem, *, layer_blocks
):
    rows = pl.ds(pl.multiple_of(place_ref[0] * QUARTER, QUARTER), QUARTER)
    load = pltpu.make_async_copy(blocks_ref.at[:, rows, :], tiles_ref, sem)
    load.start()
    out_ref[...] = jnp.zeros(out_ref.shape, BF16)

    @pl.loop(0, OWNERS)
    def _(i):
        count_ref[i] = 0

    lane = lax.broadcasted_iota(jnp.int32, (QUARTER, BS), 1)
    meta_lane = lax.broadcasted_iota(jnp.int32, (8, BS), 1)
    load.wait()

    @pl.loop(0, tiles_ref.shape[0], unroll=2)
    def _(i):
        col = col_ref[i]
        layer_of = col // layer_blocks
        kept = col - layer_of * layer_blocks
        owner = (row_ref[i] % 4 * 4 + row_ref[i] // 4) * LAYERS + layer_of
        used = count_ref[owner]
        count_ref[owner] = used + 1
        tile = jnp.where(lane < ext_ref[i], tiles_ref[i].astype(F32), 0.0)
        out_ref[owner, pl.ds(pl.multiple_of(used * QUARTER, QUARTER), QUARTER), :] = tile.astype(BF16)
        old = out_ref[owner, CAP * QUARTER :, :].astype(F32)
        new = jnp.where(meta_lane == used * 2, aux_ref[i].astype(F32), old)
        new = jnp.where(meta_lane == used * 2 + 1, kept.astype(F32), new)
        out_ref[owner, CAP * QUARTER :, :] = new.astype(BF16)


def build_send(blocks, block_aux, block_row, block_col, extents, place, layer_blocks):
    return pl.pallas_call(
        functools.partial(send_body, layer_blocks=layer_blocks),
        in_specs=[SMEM] * 5 + [ANY],
        out_specs=VMEM,
        out_shape=jax.ShapeDtypeStruct((OWNERS, CAP * QUARTER + 8, BS), BF16),
        scratch_shapes=[
            pltpu.SMEM((OWNERS,), jnp.int32),
            pltpu.VMEM((blocks.shape[0], QUARTER, BS), BF16),
            pltpu.SemaphoreType.DMA(()),
        ],
        compiler_params=params(60),
        name="build_send",
    )(block_aux, block_row, block_col, extents, place, blocks)


def split_pieces(place_ref, plans, rows_of, out_refs, level_ref):
    bit_a = place_ref[1]
    bit_b = place_ref[2]

    def piece(a, b):
        return jnp.where(b == 0, a, 3 - a)

    for part, plan in enumerate(plans):
        keep_ref, *send_refs = out_refs[3 * part : 3 * part + 3]
        for h, send_ref in enumerate(send_refs):
            kept = [piece(bit_a, o) if h == 0 else piece(o, bit_b) for o in range(2)]
            sent = [piece(1 - bit_a, o) if h == 0 else piece(o, 1 - bit_b) for o in range(2)]

            @pl.loop(0, plan.blocks, unroll=2)
            def _(block):
                first = h * HALF + (plan.first + block) * plan.group
                for other in range(2):
                    keep_ref[h, other, block] = rows_of(first, kept[other])
                    put(send_ref, plan, other * plan.blocks + block, rows_of(first, sent[other]), level_ref)

            put_levels(send_ref, plan, 2 * plan.blocks, level_ref)


def start_all(sources, targets, sems):
    loads = [pltpu.make_async_copy(src, dst, sems.at[i]) for i, (src, dst) in enumerate(zip(sources, targets))]
    for load in loads:
        load.start()
    return loads


def add_virt(meta_ref, first, quarter_refs, green_ref, acc_ref):
    @pl.loop(0, OWNERS // 8)
    def _(step):
        for local in [step * 4 + k for k in range(4)]:
            for slot in range(CAP):
                span = slice(slot * QUARTER, (slot + 1) * QUARTER)
                tile = jnp.concatenate([ref[local, span, :] for ref in quarter_refs], axis=0)
                aux = meta_ref[first + local, 2 * slot]
                kept = meta_ref[first + local, 2 * slot + 1]
                acc_ref[aux] += jnp.dot(tile, green_ref[kept], preferred_element_type=F32)


def virt_first_body(meta_ref, *rest):
    sources, out_ref, refs, (acc_ref, sems) = rest[:5], rest[5], rest[6:11], rest[11:]
    loads = start_all(sources, refs, sems)
    acc_ref[...] = jnp.zeros(acc_ref.shape, F32)
    for load in loads:
        load.wait()
    add_virt(meta_ref, 0, refs[:4], refs[4], acc_ref)
    store = pltpu.make_async_copy(acc_ref, out_ref, sems.at[0])
    store.start()
    store.wait()


def virt_last_body(meta_ref, place_ref, *rest, plan):
    sources, (keep_ref, send0_ref, send1_ref) = rest[:6], rest[6:9]
    refs, (acc_ref, level_ref, sems) = rest[9:15], rest[15:]
    loads = start_all(sources[:5], refs, sems)
    acc_ref[...] = jnp.zeros(acc_ref.shape, F32)
    for load in loads:
        load.wait()
    before = pltpu.make_async_copy(sources[5], refs[5], sems.at[5])
    before.start()
    add_virt(meta_ref, OWNERS // 2, refs[:4], refs[4], acc_ref)
    before.wait()
    these, those = piece_rows(acc_ref), piece_rows(refs[5])

    def rows_of(first, piece):
        return these(first, piece) + those(first, piece)

    split_pieces(place_ref, (plan,), rows_of, (keep_ref, send0_ref, send1_ref), level_ref)


def piece_rows(acc_ref):
    def rows_of(first, piece):
        at = [pl.multiple_of(quarter * QUARTER + piece * 8, 8) for quarter in range(4)]
        return jnp.concatenate([acc_ref[first, pl.ds(row, 8), :] for row in at], axis=0)

    return rows_of


def occ_body(meta_ref, place_ref, *rest, plans):
    parts, green_ref = (rest[:4], rest[4:8]), rest[8]
    out_refs, (acc_ref, tile_ref, level_ref) = rest[9:-3], rest[-3:]
    acc_ref[...] = jnp.zeros(acc_ref.shape, F32)
    row_place = place_ref[0]
    rows = [pl.multiple_of(((row_place + d) % ROWS) * QUARTER, QUARTER) for d in (0, ROWS - 1, 1, 2)]
    half = OWNERS // 2
    visits = [(j, slot) for j in range(2) for slot in range(CAP)]
    for part in range(2):

        @pl.loop(0, half // 2)
        def _(step):
            for j, slot in visits:
                span = slice(slot * QUARTER, (slot + 1) * QUARTER)
                for ref, row in zip(parts[part], rows):
                    tile_ref[CAP * j + slot, pl.ds(row, QUARTER), :] = ref[step * 2 + j, span, :]
            for j, slot in visits:
                source = part * half + step * 2 + j
                aux = meta_ref[source, 2 * slot]
                kept = meta_ref[source, 2 * slot + 1]
                term = lax.dot_general(
                    green_ref[kept], tile_ref[CAP * j + slot], (((1,), (1,)), ((), ())), preferred_element_type=F32
                )
                for low in range(4):
                    lanes = slice(low * BS, (low + 1) * BS)
                    acc_ref[aux, :, lanes] += term[low * BS : (low + 1) * BS, :]

    split_pieces(place_ref, plans, piece_rows(acc_ref), out_refs, level_ref)


VMEM = pl.BlockSpec(memory_space=pltpu.VMEM)
SMEM = pl.BlockSpec(memory_space=pltpu.SMEM)
ANY = pl.BlockSpec(memory_space=pl.ANY)


def step_shapes(plan):
    code = jax.ShapeDtypeStruct((plan.coded(2 * plan.blocks), WIDE), S16)
    return [jax.ShapeDtypeStruct((2, 2, plan.blocks, plan.rows, WIDE), F32), code, code]


def level_scratch(plan):
    return pltpu.VMEM((plan.levels(2 * plan.blocks), WIDE), F32)


ACC = (NP, BS, WIDE)


def scratch_like(operands):
    return [pltpu.VMEM(x.shape, x.dtype) for x in operands]


def contract_virt_first(meta, part, green):
    operands = [*part, green]
    return pl.pallas_call(
        virt_first_body,
        in_specs=[SMEM] + [ANY] * 5,
        out_specs=ANY,
        out_shape=jax.ShapeDtypeStruct(ACC, F32),
        scratch_shapes=scratch_like(operands) + [pltpu.VMEM(ACC, F32), pltpu.SemaphoreType.DMA((5,))],
        compiler_params=params(55),
        name="virt_first",
    )(meta, *operands)


def contract_virt_last(meta, place, part, green, before, plan):
    operands = [*part, green, before]
    return pl.pallas_call(
        functools.partial(virt_last_body, plan=plan),
        in_specs=[SMEM] * 2 + [ANY] * 6,
        out_specs=[VMEM] * 3,
        out_shape=step_shapes(plan),
        scratch_shapes=scratch_like(operands) + [pltpu.VMEM(ACC, F32), level_scratch(plan), pltpu.SemaphoreType.DMA((6,))],
        compiler_params=params(55),
        name="virt_last",
    )(meta, place, *operands)


def contract_occ(meta, place, parts, green, plans):
    return pl.pallas_call(
        functools.partial(occ_body, plans=plans),
        in_specs=[SMEM] * 2 + [VMEM] * 9,
        out_specs=[VMEM] * 3 * len(plans),
        out_shape=[shape for plan in plans for shape in step_shapes(plan)],
        scratch_shapes=[pltpu.VMEM(ACC, F32), pltpu.VMEM((2 * CAP, BS, BS), BF16), level_scratch(plans[-1])],
        compiler_params=params(28),
        name="contract_occ",
    )(meta, place, *parts[0], *parts[1], green)


def halve_body(place_ref, keep_ref, got0_ref, got1_ref, left_ref, send0_ref, send1_ref, level_ref, scale_ref, *, plan):
    for h, got_ref, send_ref in ((0, got0_ref, send0_ref), (1, got1_ref, send1_ref)):
        mine = place_ref[2 - h]
        away = 1 - mine
        read_scales(got_ref, (), plan, 2 * plan.blocks, scale_ref)

        @pl.loop(0, plan.blocks, unroll=2)
        def _(b):
            left_ref[h, b] = keep_ref[h, mine, b] + get(got_ref, (), plan, mine * plan.blocks + b, scale_ref)
            total = keep_ref[h, away, b] + get(got_ref, (), plan, away * plan.blocks + b, scale_ref)
            put(send_ref, plan, b, total, level_ref)

        put_levels(send_ref, plan, plan.blocks, level_ref)


def halve(place, keep, got0, got1, plan, name):
    code = jax.ShapeDtypeStruct((plan.coded(plan.blocks), WIDE), S16)
    return pl.pallas_call(
        functools.partial(halve_body, plan=plan),
        in_specs=[SMEM] + [VMEM] * 3,
        out_specs=[VMEM] * 3,
        out_shape=[jax.ShapeDtypeStruct((2, plan.blocks, plan.rows, WIDE), F32), code, code],
        scratch_shapes=[level_scratch(plan), level_scratch(plan)],
        compiler_params=params(16),
        name=name,
    )(place, keep, got0, got1)


def finish_blocks(refs, scale_ref, plans, store):
    for part, plan in enumerate(plans):
        left_ref, *got_refs = refs[3 * part : 3 * part + 3]
        for h, got_ref in enumerate(got_refs):
            read_scales(got_ref, (), plan, plan.blocks, scale_ref)

            @pl.loop(0, plan.blocks, unroll=2)
            def _(b):
                total = left_ref[h, b] + get(got_ref, (), plan, b, scale_ref)
                store(h * HALF // plan.group + plan.first + b, total)


def finish_virt_body(left_ref, got0_ref, got1_ref, out_ref, level_ref, scale_ref, *, plan):
    def store(index, total):
        put(out_ref, plan, index, total, level_ref)

    finish_blocks((left_ref, got0_ref, got1_ref), scale_ref, (plan,), store)
    put_levels(out_ref, plan, 2 * plan.blocks, level_ref)


def finish_occ_body(place_ref, *rest, plans, whole):
    refs, out_refs, (code_ref, level_ref, scale_ref) = rest[:-7], rest[-7:-3], rest[-3:]
    lanes = [pl.ds(pl.multiple_of((place_ref[0] + d) % 4 * BS, BS), BS) for d in range(4)]

    def store(index, total):
        codes, level = encode(total)
        code_ref[...] = codes
        level_ref[pl.ds(index, 1), :] = level
        for out_ref, part in zip(out_refs, lanes):
            out_ref[at_block(whole, index), :] = code_ref[:, part]

    finish_blocks(refs, scale_ref, plans, store)
    for out_ref, part in zip(out_refs, lanes):
        out_ref[level_rows(whole, 2 * whole.blocks), :] = level_ref[:, part].astype(jnp.int32).astype(S16)


def finish_virt(left, got0, got1, plan):
    return pl.pallas_call(
        functools.partial(finish_virt_body, plan=plan),
        in_specs=[VMEM] * 3,
        out_specs=VMEM,
        out_shape=jax.ShapeDtypeStruct((plan.coded(2 * plan.blocks), WIDE), S16),
        scratch_shapes=[level_scratch(plan), level_scratch(plan)],
        compiler_params=params(12),
        name="finish_virt",
    )(left, got0, got1)


def finish_occ(place, sums, plans, whole):
    part = jax.ShapeDtypeStruct((whole.coded(2 * whole.blocks), BS), S16)
    return pl.pallas_call(
        functools.partial(finish_occ_body, plans=plans, whole=whole),
        in_specs=[SMEM] + [VMEM] * len(sums),
        out_specs=[VMEM] * 4,
        out_shape=[part] * 4,
        scratch_shapes=[pltpu.VMEM((whole.rows, WIDE), S16), level_scratch(whole), level_scratch(whole)],
        compiler_params=params(12),
        name="finish_occ",
    )(place, *sums)


def decode_virt_body(place_ref, virt_ref, vir_ref, scale_ref, *, plan):
    at = [((place_ref[1] + shift) % 4) * 8 for shift in (0, ROWS - 1, 1, 2)]
    read_scales(virt_ref, (), plan, 2 * plan.blocks, scale_ref)

    @pl.loop(0, NP, unroll=2)
    def _(q):
        values = get(virt_ref, (), plan, q, scale_ref)
        for quarter in range(4):
            for low in range(4):
                to = pl.ds(pl.multiple_of(low * QUARTER + at[quarter], 8), 8)
                vir_ref[q, to, :] = values[quarter * 8 : (quarter + 1) * 8, low * BS : (low + 1) * BS]


def decode_virt(place, virt, plan):
    return pl.pallas_call(
        functools.partial(decode_virt_body, plan=plan),
        in_specs=[SMEM, VMEM],
        out_specs=VMEM,
        out_shape=jax.ShapeDtypeStruct((NP, BS, BS), F32),
        scratch_shapes=[level_scratch(plan)],
        compiler_params=params(8),
        name="decode_virt",
    )(place, virt)


def pair_body(place_ref, own_ref, one_ref, two_ref, three_ref, vir_ref, out_ref, occ_ref, scale_ref, *, plan):
    here = place_ref[0]

    for d, ref in enumerate((own_ref, one_ref, two_ref, three_ref)):
        source = (here + 4 - d) % 4
        read_scales(ref, (), plan, 2 * plan.blocks, scale_ref)
        rows = pl.ds(pl.multiple_of(source * QUARTER, QUARTER), QUARTER)

        @pl.loop(0, NP, unroll=4)
        def _(p):
            occ_ref[p, rows, :] = get(ref, (), plan, p, scale_ref)

    @pl.loop(0, NP)
    def _(p):
        occ = occ_ref[p]
        for q in range(NP):
            out_ref[p, q : q + 1, :] = jnp.sum(occ * vir_ref[q], axis=0, keepdims=True)


def pair(place, own, others, vir, plan):
    return pl.pallas_call(
        functools.partial(pair_body, plan=plan),
        in_specs=[SMEM] + [VMEM] * 5,
        out_specs=VMEM,
        out_shape=jax.ShapeDtypeStruct((NP, NP, BS), F32),
        scratch_shapes=[pltpu.VMEM((NP, BS, BS), F32), pltpu.VMEM((plan.levels(2 * plan.blocks), BS), F32)],
        compiler_params=params(16),
        name="pair",
    )(place, own, *others, vir)


def rotate(size, step):
    return [(i, (i + step) % size) for i in range(size)]


def rotate_high(step):
    return [(c, (c + 4 * step) % COLS) for c in range(COLS)]


PAIRS_A = [(0, 1), (1, 0), (2, 3), (3, 2)]
PAIRS_B = [(0, 3), (3, 0), (1, 2), (2, 1)]


def index_of(row, col, layer):
    return (row * COLS + col) * LAYERS + layer


SWAP = [
    (index_of(r, c, l), index_of(c % 4, c // 4 * 4 + r, l))
    for r in range(ROWS)
    for c in range(COLS)
    for l in range(LAYERS)
]


def sum_all(values):
    for axes in ("col", ("row", "layer")):
        copies = jnp.broadcast_to(values[None], (16, *values.shape))
        values = jnp.sum(lax.all_to_all(copies, axes, 0, 0, tiled=True), axis=0)
    return values


def layer_swap(send0, send1, perms):
    return lax.ppermute(send0, "layer", perms[0]), lax.ppermute(send1, "layer", perms[1])


FIRST = (PAIRS_A, PAIRS_B)
SECOND = (PAIRS_B, PAIRS_A)


def after(*values):
    return lax.optimization_barrier(values)


def on_device(blocks, block_aux, block_row, block_col, extents, occ_green, virt_green):
    layer_blocks = occ_green.shape[0] // BS
    row_place = lax.axis_index("row").astype(jnp.int32)
    col_place = lax.axis_index("col").astype(jnp.int32)
    layer_place = lax.axis_index("layer").astype(jnp.int32)
    bit_a = ((layer_place == 1) | (layer_place == 2)).astype(jnp.int32)
    bit_b = layer_place // 2
    place = jnp.stack([row_place, bit_a, bit_b])
    plan = Plan(4)

    send = build_send(blocks, block_aux, block_row, block_col, extents, row_place[None], layer_blocks)
    own = lax.all_to_all(send, ("col", "layer"), 0, 0, tiled=True)
    virt_blocks = virt_green.reshape(layer_blocks, BS, WIDE)
    occ_blocks = occ_green.reshape(layer_blocks, BS, WIDE).transpose(0, 2, 1)

    half = OWNERS // 2
    own_a = own[:half, : CAP * QUARTER]
    later, occ_blocks = after(own, occ_blocks)
    own_b = later[half:, : CAP * QUARTER]
    meta = later[:, CAP * QUARTER, : 2 * CAP].astype(jnp.int32)
    up, down = rotate(ROWS, 1), rotate(ROWS, -1)
    prev_a = lax.ppermute(own_a, "row", up)
    next_a = lax.ppermute(own_a, "row", down)
    prev_a, next_a, own_b, occ_blocks, meta = after(prev_a, next_a, own_b, occ_blocks, meta)
    far_a = lax.ppermute(prev_a, "row", up)
    next_b = lax.ppermute(own_b, "row", down)
    far_a, next_b, own_b = after(far_a, next_b, own_b)
    prev_b = lax.ppermute(own_b, "row", up)
    far_b = lax.ppermute(next_b, "row", down)
    part_a, part_b = (own_a, prev_a, next_a, far_a), (own_b, prev_b, next_b, far_b)

    v_acc = contract_virt_first(meta, part_a, virt_blocks)
    v_keep, v0, v1 = contract_virt_last(meta, place, part_b, virt_blocks, v_acc, plan)
    v_got = layer_swap(v0, v1, FIRST)
    occ_blocks, v_keep = after(occ_blocks, v_keep)
    small, large = parts = Plan(4, 0, 4), Plan(4, 4, 8)
    a_keep, a0, a1, b_keep, b0, b1 = contract_occ(meta, place, (part_a, part_b), occ_blocks, parts)
    a_got = layer_swap(a0, a1, FIRST)
    v_keep, a_keep, b_keep = after(v_keep, a_keep, b_keep)
    v_left, v0, v1 = halve(place, v_keep, *v_got, plan, "halve_virt")
    v0, v1, *a_got = after(v0, v1, *a_got)
    v_got = layer_swap(v0, v1, SECOND)
    a_keep, v_left = after(a_keep, v_left)
    a_left, a0, a1 = halve(place, a_keep, *a_got, small, "halve_occ_a")
    a_left, *v_got = after(a_left, *v_got)
    a0, a1, b0, b1, *v_got = after(a0, a1, b0, b1, *v_got)
    b_got = layer_swap(b0, b1, FIRST)
    a_got = layer_swap(a0, a1, SECOND)
    virt = finish_virt(v_left, *v_got, plan)
    virt, b_keep = after(virt, b_keep)
    virt = lax.ppermute(virt, ALL, SWAP)
    b_left, b0, b1 = halve(place, b_keep, *b_got, large, "halve_occ_b")
    b_got = layer_swap(b0, b1, SECOND)
    here = jnp.stack([col_place // 4, col_place % 4])
    occ, *others = finish_occ(here, (a_left, *a_got, b_left, *b_got), parts, plan)
    far = lax.ppermute(others[1], "col", rotate_high(2))
    others = [lax.ppermute(others[0], "col", rotate_high(1)), far, lax.ppermute(others[2], "col", rotate_high(3))]
    partial = pair(here, occ, others, decode_virt(here, virt, plan), plan)
    return sum_all(jnp.sum(partial, axis=-1))


def solution(mesh):
    in_specs = (
        P(("col", "layer"), None, None),
        P(("col", "layer")),
        P(("col", "layer")),
        P(("col", "layer")),
        P(("col", "layer")),
        P("layer", "row"),
        P("layer", "row"),
    )
    return jax.shard_map(on_device, mesh=mesh, in_specs=in_specs, out_specs=P(), check_vma=False)
```
